32 devices in a mesh: dp: 8 (over z, x), seq: 4 (over y, core).
Axes of the slice: x: 2, y: 2, z: 4, core: 2. Of those that a mesh axis runs over, the one named last changes fastest.
Arguments:
- hidden_in: bfloat16 [24, 1024, 768], P('dp', 'seq'), may hold values from -8 to 8
- lengths: int32 [24], P('dp'), may hold values from 256 to 1024, as said below
- w_qkv: bfloat16 [768, 2304], P(('dp', 'seq')), may hold values from -0.3125 to 0.3125
- b_query: bfloat16 [768], P(('dp', 'seq')), may hold values from -1 to 1
- b_value: bfloat16 [768], P(('dp', 'seq')), may hold values from -1 to 1
- w_out: bfloat16 [768, 768], P(('dp', 'seq')), may hold values from -0.875 to 0.875
- b_out: bfloat16 [768], P(('dp', 'seq')), may hold values from -1 to 1
- gain_one: bfloat16 [768], P(('dp', 'seq')), may hold values from 0.5 to 1.5
- bias_one: bfloat16 [768], P(('dp', 'seq')), may hold values from -1 to 1
- w_in: bfloat16 [768, 3072], P(('dp', 'seq')), may hold values from -0.21875 to 0.21875
- b_in: bfloat16 [3072], P(('dp', 'seq')), may hold values from -1 to 1
- w_down: bfloat16 [3072, 768], P(('dp', 'seq')), may hold values from -0.21875 to 0.21875
- b_down: bfloat16 [768], P(('dp', 'seq')), may hold values from -1 to 1
- gain_two: bfloat16 [768], P(('dp', 'seq')), may hold values from 0.5 to 1.5
- bias_two: bfloat16 [768], P(('dp', 'seq')), may hold values from -1 to 1
- cotangent: bfloat16 [24, 1024, 768], P('dp', 'seq'), may hold values from -6 to 6
Outputs:
- layer_out: bfloat16 [24, 1024, 768], P('dp', 'seq')
- grad_input: float32 [24, 1024, 768], P('dp', 'seq')
- grad_wqkv: float32 [768, 2304], P(('dp', 'seq'))
- grad_bquery: float32 [768], P(('dp', 'seq'))
- grad_bvalue: float32 [768], P(('dp', 'seq'))
- grad_wout: float32 [768, 768], P(('dp', 'seq'))
- grad_bout: float32 [768], P(('dp', 'seq'))
- grad_gain1: float32 [768], P(('dp', 'seq'))
- grad_bias1: float32 [768], P(('dp', 'seq'))
- grad_win: float32 [768, 3072], P(('dp', 'seq'))
- grad_bin: float32 [3072], P(('dp', 'seq'))
- grad_wdown: float32 [3072, 768], P(('dp', 'seq'))
- grad_bdown: float32 [768], P(('dp', 'seq'))
- grad_gain2: float32 [768], P(('dp', 'seq'))
- grad_bias2: float32 [768], P(('dp', 'seq'))
- stat_rms: float32 [4], replicated
The draws below stay inside these ranges and needn't reach their ends.
Inputs may be any that keep to these rules, and one draw needn't show every extreme that they name: `lengths`: valid tokens of each sequence, which lie at its first slots; in every draw some sequence holds exactly 1024 and some exactly 256.
All inputs are finite; a program needn't handle non-finite values.
Results may differ from the reference program's by a relative error of at most 0.014.
The reference program's roundings to bfloat16 on the way count: a program that leaves them out, or rounds other values in their place, can miss the bound.
Values may be sent and summed in bfloat16 or wider, within the bound.
No kernel may reach another device: no remote copies, remote signals or barrier semaphores. Data moves between devices by JAX's collectives and lax.ppermute only.
A program may use at most 128 MiB of HBM per device.

```python
import jax
import jax.numpy as jnp
from jax import lax

D = 768
HEADS = 12
HD = 64
FF = 3072
LEN = 1024
MINLEN = 256
BATCH = 24


def draw_lengths(key, part):
    key_base, key_long, key_short = jax.random.split(key, 3)
    values = jax.random.randint(key_base, (BATCH,), MINLEN, LEN + 1)
    longest = jax.random.randint(key_long, (), 0, BATCH)
    offset = jax.random.randint(key_short, (), 1, BATCH)
    shortest = (longest + offset) % BATCH
    values = values.at[longest].set(LEN)
    values = values.at[shortest].set(MINLEN)
    return values.astype(jnp.int32)


def draw_hidden_in(key, part):
    key_base, key_scale = jax.random.split(key)
    rising = lax.iota(jnp.float32, BATCH) / max(BATCH - 1, 1)
    seq_scale = jnp.exp(jnp.log(0.6) + jnp.log(3.0) * rising)
    token_scale = jnp.exp(jax.random.uniform(key_scale, (BATCH, LEN, 1), jnp.float32, jnp.log(0.7), jnp.log(1.4)))
    raw_draw = jax.random.normal(key_base, (BATCH, LEN, D), jnp.float32)
    values = raw_draw * token_scale * seq_scale[:, None, None]
    return jnp.clip(values, -8.0, 8.0).astype(jnp.bfloat16)


def levels(rng, dims, cuts, smallest, top_value):
    gain, own = 1.0, jax.random.fold_in(rng, 6)
    for position, shards_of in cuts:
        heights = jnp.exp(jax.random.uniform(jax.random.fold_in(own, position), (shards_of,), jnp.float32, smallest / len(cuts), top_value / len(cuts)))
        gain = gain * jnp.repeat(heights, dims[position] // shards_of).reshape([-1 if axis == position else 1 for axis in range(len(dims))])
    return gain


def centred(key, extent, scale, reach, cuts=(), kind=jnp.bfloat16):
    gain = levels(key, extent, cuts, -0.22, 0.18) if cuts else 1.0
    drawn = jax.random.normal(key, extent, jnp.float32) * scale * gain
    return jnp.minimum(jnp.maximum(drawn, -reach), reach).astype(kind)


def setup_inputs(seed: int = 0) -> dict:
    key_list = jax.random.split(jax.random.key(seed), 17)
    return {
        "hidden_in": draw_hidden_in(jax.random.fold_in(key_list[16], 71), 0),
        "lengths": draw_lengths(jax.random.fold_in(key_list[16], 71), 0),
        "w_qkv": centred(key_list[2], (D, 3 * D), (D // 2) ** -0.5, 0.3125, ((0, 32),)),
        "b_query": centred(key_list[3], (D,), 0.2, 1.0, ((0, 32),)),
        "b_value": centred(key_list[4], (D,), 0.2, 1.0, ((0, 32),)),
        "w_out": centred(key_list[5], (D, D), (D // 16) ** -0.5, 0.875, ((0, 32),)),
        "b_out": centred(key_list[6], (D,), 0.2, 1.0, ((0, 32),)),
        "gain_one": jnp.clip(1.0 + 0.1 * jax.random.normal(key_list[7], (D,), jnp.float32), 0.5, 1.5).astype(jnp.bfloat16),
        "bias_one": centred(key_list[8], (D,), 0.2, 1.0, ((0, 32),)),
        "w_in": centred(key_list[9], (D, FF), D ** -0.5, 0.21875, ((0, 32),)),
        "b_in": centred(key_list[10], (FF,), 0.2, 1.0, ((0, 32),)),
        "w_down": centred(key_list[11], (FF, D), (FF // 4) ** -0.5, 0.21875, ((0, 32),)),
        "b_down": centred(key_list[12], (D,), 0.2, 1.0, ((0, 32),)),
        "gain_two": jnp.clip(1.0 + 0.1 * jax.random.normal(key_list[13], (D,), jnp.float32), 0.5, 1.5).astype(jnp.bfloat16),
        "bias_two": centred(key_list[14], (D,), 0.2, 1.0, ((0, 32),)),
        "cotangent": centred(key_list[15], (BATCH, LEN, D), 1.0, 6.0, ((0, 8), (1, 4))),
    }


@jax.custom_vjp
def low(v):
    return lax.optimization_barrier(v.astype(jnp.bfloat16)).astype(jnp.float32)

@jax.custom_vjp
def low_back(v):
    return v

def low_keep(v):
    return (low(v), None)

def low_pass(kept, grad):
    return (grad,)

def back_keep(v):
    return (v, None)

def back_low(kept, grad):
    return (low(grad),)
low.defvjp(low_keep, low_pass)
low_back.defvjp(back_keep, back_low)
NORM_EPS = 1e-12

def matmul(left, right):
    return jnp.matmul(left, right, precision=lax.Precision.HIGHEST)

def layer_norm(values, gain_vec, shift_vec):
    center = values - lax.optimization_barrier(jnp.mean(values, axis=-1, keepdims=True))
    spread = lax.optimization_barrier(jnp.mean(center * center, axis=-1, keepdims=True))
    return center * lax.rsqrt(spread + NORM_EPS) * gain_vec + shift_vec

def attend_one(packed_seq, valid_seq):
    query_rows = packed_seq[:, 0]
    key_rows = packed_seq[:, 1]
    value_rows = packed_seq[:, 2]
    scale_factor = HD ** (-0.5)
    scores = low_back(jnp.einsum('qhd,khd->hqk', query_rows, key_rows, precision=lax.Precision.HIGHEST) * scale_factor)
    masked = jnp.where(valid_seq[None, None, :], scores, -jnp.inf)
    row_max = lax.optimization_barrier(jnp.max(masked, axis=-1, keepdims=True))
    weights = jnp.exp(masked - row_max)
    attn_probs = weights / lax.optimization_barrier(jnp.sum(weights, axis=-1, keepdims=True))
    context = jnp.einsum('hqk,khd->qhd', low(attn_probs), value_rows, precision=lax.Precision.HIGHEST)
    return low_back(low(context))

def attend_pair(pair_in):
    return attend_one(pair_in[0], pair_in[1])

def forward(params, inputs, valid_g):
    w_qkv, b_query, b_value, w_out, b_out, gain_one, bias_one, w_in, b_in, w_down, b_down, gain_two, bias_two = params
    group_size = inputs.shape[0]
    rows_in = inputs.reshape(-1, D)
    bias_three = jnp.concatenate([b_query, jnp.zeros_like(b_query), b_value])
    packed = low_back(low(matmul(rows_in, w_qkv) + bias_three))
    packed = packed.reshape(group_size, LEN, 3, HEADS, HD)
    context = lax.map(jax.checkpoint(attend_pair), (packed, valid_g))
    context = context.reshape(-1, D)
    branch = low_back(matmul(context, w_out) + b_out)
    normed = layer_norm(rows_in + branch, gain_one, bias_one)
    inner = low_back(matmul(low(normed), w_in) + b_in)
    activated = low(jax.nn.gelu(inner, approximate=False))
    second = low_back(matmul(activated, w_down) + b_down)
    output = layer_norm(normed + second, gain_two, bias_two)
    shape_out = (group_size, LEN, D)
    return (output.reshape(shape_out), (branch.reshape(shape_out), second.reshape(shape_out)))

def regroup(array, step_count, group_size):
    return array.reshape((step_count, group_size) + array.shape[1:])

def reference(hidden_in, lengths, w_qkv, b_query, b_value, w_out, b_out, gain_one, bias_one, w_in, b_in, w_down, b_down, gain_two, bias_two, cotangent):
    params = tuple((member.astype(jnp.float32) for member in (w_qkv, b_query, b_value, w_out, b_out, gain_one, bias_one, w_in, b_in, w_down, b_down, gain_two, bias_two)))
    batch_size = hidden_in.shape[0]
    group_size = 4 if batch_size % 4 == 0 else 1
    step_count = batch_size // group_size
    valid_mask = lax.iota(jnp.int32, LEN)[None, :] < lengths[:, None]
    valid_float = valid_mask.astype(jnp.float32)[..., None]
    inputs = hidden_in.astype(jnp.float32)
    upstream = cotangent.astype(jnp.float32) * valid_float

    def scan_step(carry, pieces):
        grad_sums, stat_sums = carry
        inputs_g, valid_g, upstream_g = pieces

        def run(param_in, inputs_in):
            return forward(param_in, inputs_in, valid_g)
        output, pullback, extras = jax.vjp(run, params, inputs_g, has_aux=True)
        grad_params, grad_inputs = pullback(upstream_g)
        branch, second = extras
        weight_rows = valid_g.astype(jnp.float32)[..., None]
        stats = jnp.stack([jnp.sum(inputs_g * inputs_g * weight_rows), jnp.sum(branch * branch * weight_rows), jnp.sum(second * second * weight_rows), jnp.sum(output * output * weight_rows)])
        grad_sums = jax.tree.map(jnp.add, grad_sums, grad_params)
        layer_out = (output * weight_rows).astype(jnp.bfloat16)
        return ((grad_sums, stat_sums + stats), (layer_out, grad_inputs))
    start = (jax.tree.map(jnp.zeros_like, params), jnp.zeros((4,), jnp.float32))
    (grad_sums, stat_sums), (layer_out, grad_input) = lax.scan(scan_step, start, (regroup(inputs, step_count, group_size), regroup(valid_mask, step_count, group_size), regroup(upstream, step_count, group_size)))
    layer_out = layer_out.reshape(hidden_in.shape)
    grad_input = grad_input.reshape(hidden_in.shape)
    token_count = jnp.sum(lengths).astype(jnp.float32)
    stat_rms = jnp.sqrt(stat_sums / (token_count * D))
    return (layer_out, grad_input, grad_sums[0], grad_sums[1], grad_sums[2], grad_sums[3], grad_sums[4], grad_sums[5], grad_sums[6], grad_sums[7], grad_sums[8], grad_sums[9], grad_sums[10], grad_sums[11], grad_sums[12], stat_rms)
```

```python
import functools

import jax
import jax.numpy as jnp
from jax import lax
from jax.experimental import pallas as pl
from jax.experimental.pallas import tpu as pltpu
from jax.sharding import PartitionSpec as P

HD = 64
NORM_EPS = 1e-12
BOTH = ("dp", "seq")
F32 = jnp.float32
BF16 = jnp.bfloat16
VMEM_LIMIT = 56 * 1024 * 1024


def swap(array, axis, offset):
    size = lax.axis_size(axis)
    return lax.ppermute(array, axis, [(i, i ^ offset) for i in range(size)])


def gather_offsets(array, axis):
    size = lax.axis_size(axis)
    pieces = {0: array}
    bit = size // 2
    while bit:
        for key in list(pieces):
            pieces[key | bit] = swap(pieces[key], axis, bit)
        bit //= 2
    return [pieces[k] for k in range(size)]


def pick(array, index):
    return lax.dynamic_index_in_dim(array, index, 0, keepdims=False)


def xor_order(array, index):
    size = array.shape[0]
    return jnp.stack([pick(array, lax.bitwise_xor(index, i)) for i in range(size)])


def total_over(array, axes):
    for axis in axes:
        bit = 1
        while bit < lax.axis_size(axis):
            array = array + swap(array, axis, bit)
            bit *= 2
    return array


def dot(left, right, dims=((1,), (0,))):
    return lax.dot_general(left, right, (dims, ((), ())), preferred_element_type=F32)


NT = ((1,), (1,))
TN = ((0,), (0,))


def head_lanes(width, head):
    lane = lax.broadcasted_iota(jnp.int32, (1, width), 1)
    return (lane >= head * HD) & (lane < (head + 1) * HD)


def attend_kernel(pieces, seg, meta, *refs):
    hidden = refs[:pieces]
    wq, wk, wv, bias, q_out, k_out, v_out, ctx_out, lse_out = refs[pieces:]
    length, place = meta[0], meta[1]
    width = q_out.shape[-1]
    heads = width // HD
    filled = (length + seg - 1) // seg
    for j in range(pieces):
        at = lax.bitwise_xor(place, j)

        @pl.when(at < filled)
        def _():
            rows = hidden[j][0]
            q = (dot(rows, wq[...]) + bias[0:1]).astype(BF16)
            q_out[at] = q * jnp.asarray(HD**-0.5, BF16)
            k_out[at] = dot(rows, wk[...]).astype(BF16)
            v_out[at] = (dot(rows, wv[...]) + bias[1:2]).astype(BF16)

        @pl.when(at >= filled)
        def _():
            q_out[at] = jnp.zeros((seg, width), BF16)
            k_out[at] = jnp.zeros((seg, width), BF16)
            v_out[at] = jnp.zeros((seg, width), BF16)
            ctx_out[j] = jnp.zeros((seg, width), BF16)
            lse_out[at] = jnp.zeros((seg, lse_out.shape[-1]), F32)

    for count in range(1, pieces + 1):

        @pl.when(filled == count)
        def _(count=count):
            keys = k_out[0:count].reshape(count * seg, width)
            values = v_out[0:count].reshape(count * seg, width)
            column = lax.broadcasted_iota(jnp.int32, (1, seg), 1) + (count - 1) * seg
            tail_ok = column < length

            def block(at, carry):
                q = q_out[at]
                ctx = jnp.zeros((seg, width), F32)
                lse = jnp.zeros((seg, lse_out.shape[-1]), F32)
                for head in range(heads):
                    here = head_lanes(width, head)
                    scores = dot(jnp.where(here, q, jnp.zeros_like(q)), keys, NT)
                    tail = jnp.where(tail_ok, scores[:, (count - 1) * seg :], -jnp.inf)
                    if count > 1:
                        scores = jnp.concatenate([scores[:, : (count - 1) * seg], tail], axis=1)
                    else:
                        scores = tail
                    top = jnp.max(scores, axis=-1, keepdims=True)
                    weights = jnp.exp(scores - top)
                    total = jnp.sum(weights, axis=-1, keepdims=True)
                    probs = (weights * (1.0 / total)).astype(BF16)
                    ctx = jnp.where(here, dot(probs, values), ctx)
                    lane = lax.broadcasted_iota(jnp.int32, lse.shape, 1)
                    lse = jnp.where(lane == head, top + jnp.log(total), lse)
                ctx_out[lax.bitwise_xor(place, at)] = ctx.astype(BF16)
                lse_out[at] = lse
                return carry

            lax.fori_loop(0, count, block, 0)


def attend(seq_id, meta, hidden, weights, bias):
    pieces = len(hidden)
    _, seg, model = hidden[0].shape
    width = weights[0].shape[-1]
    whole = lambda shape: pl.BlockSpec(shape, lambda i, m: (0,) * len(shape))
    per_head = jax.ShapeDtypeStruct((pieces, seg, width), BF16)
    shape4 = (pieces, seg, width)
    return pl.pallas_call(
        functools.partial(attend_kernel, pieces, seg),
        out_shape=(per_head,) * 4 + (jax.ShapeDtypeStruct((pieces, seg, 128), F32),),
        grid_spec=pltpu.PrefetchScalarGridSpec(
            num_scalar_prefetch=1,
            grid=(1,),
            in_specs=[pl.BlockSpec((1, seg, model), lambda i, m: (seq_id, 0, 0))] * pieces
            + [whole((model, width))] * 3
            + [whole((2, width))],
            out_specs=[whole(shape4)] * 4 + [whole((pieces, seg, 128))],
        ),
        compiler_params=pltpu.CompilerParams(vmem_limit_bytes=VMEM_LIMIT),
        name="attend",
    )(meta, *hidden, *weights, bias)


def attend_back_kernel(pieces, seg, meta, *refs):
    hidden = refs[:pieces]
    grads = refs[pieces : 2 * pieces]
    (wq, wk, wv, q_in, k_in, v_in, ctx_in, lse_in, sum_q, sum_k, sum_v, sum_b) = refs[
        2 * pieces : 2 * pieces + 12
    ]
    gin_out, out_q, out_k, out_v, out_b, g_all, dq_t, d_q, d_k, d_v = refs[2 * pieces + 12 :]
    length, place = meta[0], meta[1]
    width = q_in.shape[-1]
    heads = width // HD
    model = wq.shape[0]
    filled = (length + seg - 1) // seg
    for j in range(pieces):
        g_all[lax.bitwise_xor(place, j)] = grads[j][...]

        @pl.when(lax.bitwise_xor(place, j) >= filled)
        def _():
            gin_out[j] = jnp.zeros((seg, model), gin_out.dtype)

    for count in range(1, pieces + 1):

        @pl.when(filled == count)
        def _(count=count):
            rows = count * seg
            queries = q_in[0:count].reshape(rows, width)
            upstream = g_all[0:count].reshape(rows, width)
            queries_t = queries.T
            upstream_t = upstream.T
            delta_rows = []
            lse_rows = []
            for at in range(count):
                lse_rows.append(lse_in[at].T[0:8])
                ctx = ctx_in[lax.bitwise_xor(place, at)].astype(F32)
                product = ctx * g_all[at].astype(F32)
                delta_rows.append(product.T)
            lse_t = jnp.concatenate(lse_rows, axis=1)
            product_t = jnp.concatenate(delta_rows, axis=1)
            delta_t = [
                jnp.sum(product_t[h * HD : (h + 1) * HD], axis=0, keepdims=True)
                for h in range(heads)
            ]
            dq_t[:, 0:rows] = jnp.zeros((width, rows), F32)

            def block(at, carry):
                keys = k_in[at]
                values = v_in[at]
                keys_t = keys.T
                row = lax.broadcasted_iota(jnp.int32, (seg, 1), 0) + at * seg
                row_ok = row < length
                dk = jnp.zeros((seg, width), F32)
                dv = jnp.zeros((seg, width), F32)
                for head in range(heads):
                    here = head_lanes(width, head)
                    scores = dot(jnp.where(here, keys, jnp.zeros_like(keys)), queries_t)
                    probs = jnp.exp(scores - lse_t[head : head + 1])
                    probs = jnp.where(row_ok, probs, 0.0)
                    g_probs = dot(jnp.where(here, values, jnp.zeros_like(values)), upstream_t)
                    g_scores = (probs * (g_probs - delta_t[head])).astype(BF16)
                    dv = jnp.where(here, dot(probs.astype(BF16), upstream), dv)
                    dk = jnp.where(here, dot(g_scores, queries), dk)
                    part = slice(head * HD, (head + 1) * HD)
                    dq_t[part, 0:rows] += dot(keys_t[part], g_scores)
                d_k[at] = dk.astype(BF16)
                d_v[at] = dv.astype(BF16)
                return carry

            lax.fori_loop(0, count, block, 0)
            for at in range(count):
                piece = dq_t[:, at * seg : (at + 1) * seg]
                d_q[at] = (piece.T * HD**-0.5).astype(BF16)

    out_q[...] = sum_q[...]
    out_k[...] = sum_k[...]
    out_v[...] = sum_v[...]
    out_b[...] = sum_b[...]
    for j in range(pieces):
        at = lax.bitwise_xor(place, j)

        @pl.when(at < filled)
        def _():
            gq, gk, gv = d_q[at], d_k[at], d_v[at]
            gin = dot(gq, wq[...], NT) + dot(gk, wk[...], NT) + dot(gv, wv[...], NT)
            gin_out[j] = gin.astype(gin_out.dtype)
            rows = hidden[j][0]
            out_q[...] += dot(rows, gq, TN)
            out_k[...] += dot(rows, gk, TN)
            out_v[...] += dot(rows, gv, TN)
            out_b[0:1] += jnp.sum(gq.astype(F32), axis=0, keepdims=True)
            out_b[1:2] += jnp.sum(gv.astype(F32), axis=0, keepdims=True)


def attend_back(seq_id, meta, hidden, grads, weights, saved, sums):
    pieces = len(hidden)
    _, seg, model = hidden[0].shape
    width = weights[0].shape[-1]
    whole = lambda shape: pl.BlockSpec(shape, lambda i, m: (0,) * len(shape))
    shape4 = (pieces, seg, width)
    sum_shapes = [(model, width)] * 3 + [(8, width)]
    return pl.pallas_call(
        functools.partial(attend_back_kernel, pieces, seg),
        out_shape=(jax.ShapeDtypeStruct((pieces, seg, model), F32),)
        + tuple(jax.ShapeDtypeStruct(s, F32) for s in sum_shapes),
        grid_spec=pltpu.PrefetchScalarGridSpec(
            num_scalar_prefetch=1,
            grid=(1,),
            in_specs=[pl.BlockSpec((1, seg, model), lambda i, m: (seq_id, 0, 0))] * pieces
            + [whole((seg, width))] * pieces
            + [whole((model, width))] * 3
            + [whole(shape4)] * 4
            + [whole((pieces, seg, 128))]
            + [whole(s) for s in sum_shapes],
            out_specs=[whole((pieces, seg, model))] + [whole(s) for s in sum_shapes],
            scratch_shapes=[pltpu.VMEM(shape4, BF16), pltpu.VMEM((width, pieces * seg), F32)]
            + [pltpu.VMEM(shape4, BF16)] * 3,
        ),
        compiler_params=pltpu.CompilerParams(vmem_limit_bytes=VMEM_LIMIT),
        name="attend_back",
    )(meta, *hidden, *grads, *weights, *saved, *sums)


def normal_parts(v):
    size = jnp.abs(v) * (0.5**0.5)
    t = 1.0 / (1.0 + 0.3275911 * size)
    poly = t * (
        0.254829592
        + t * (-0.284496736 + t * (1.421413741 + t * (-1.453152027 + t * 1.061405429)))
    )
    bell = jnp.exp(-0.5 * v * v)
    upper = 0.5 * poly * bell
    cdf = jnp.where(v < 0, upper, 1.0 - upper)
    return cdf, bell * (0.5 / jnp.pi) ** 0.5


def normalise(values):
    center = values - jnp.mean(values, axis=-1, keepdims=True)
    root = lax.rsqrt(jnp.mean(center * center, axis=-1, keepdims=True) + NORM_EPS)
    return center * root, root


def normalise_back(grad, unit, root):
    mean_grad = jnp.mean(grad, axis=-1, keepdims=True)
    mean_prod = jnp.mean(grad * unit, axis=-1, keepdims=True)
    return root * (grad - mean_grad - unit * mean_prod)


def body(
    hidden_in,
    lengths,
    w_qkv,
    b_query,
    b_value,
    w_out,
    b_out,
    gain_one,
    bias_one,
    w_in,
    b_in,
    w_down,
    b_down,
    gain_two,
    bias_two,
    cotangent,
):
    seqs, seg, model = hidden_in.shape
    groups = lax.axis_size("seq")
    ranks = lax.axis_size("dp")
    devices = groups * ranks
    place = lax.axis_index("seq")
    rank = lax.axis_index("dp")
    share = model // devices
    ff = w_in.shape[1]
    ff_share = ff // devices
    ratio = ff // model
    width = model // groups

    hidden = gather_offsets(hidden_in, "seq")

    cut = w_qkv.reshape(share, 3, groups, width).transpose(2, 1, 0, 3)
    first = (rank * groups + place) * share
    owner = first // width
    within = first - owner * width
    blank = jnp.zeros((2, width), BF16)
    shifts = lax.dynamic_update_slice(blank, jnp.stack([b_query, b_value]), (0, within))
    mine = lax.iota(jnp.int32, groups)[:, None, None] == owner
    rowed = jnp.where(mine, shifts[None], jnp.zeros_like(shifts)[None])
    rowed = jnp.stack([rowed[:, 0], jnp.zeros_like(rowed[:, 0]), rowed[:, 1]], axis=1)
    tall = -(-(share + 1) // 8) * 8
    packed = jnp.concatenate([cut, rowed[:, :, None, :]], axis=2)
    packed = jnp.pad(packed, ((0, 0), (0, 0), (0, tall - share - 1), (0, 0)))
    packed = packed.reshape(groups, 3 * tall, width)
    packed = lax.all_to_all(packed, "seq", split_axis=0, concat_axis=0, tiled=True)
    if ranks <= 8:
        blocks = [packed if k == 0 else swap(packed, "dp", k) for k in range(ranks)]
        blocks = xor_order(jnp.stack(blocks), rank)
    else:
        blocks = lax.all_gather(packed, "dp", axis=0, tiled=False)
    blocks = blocks.reshape(ranks, groups, 3, tall, width)
    weights = [blocks[:, :, i, :share].reshape(model, width) for i in range(3)]
    bias = jnp.stack(
        [jnp.sum(blocks[:, :, i, share].astype(F32), axis=(0, 1)) for i in (0, 2)]
    )

    small = jnp.concatenate([b_out, gain_one, bias_one, b_down, gain_two, bias_two, b_in])
    small = jnp.pad(small, (0, 8 * model - small.shape[0])).reshape(8, model)
    bundle = jnp.concatenate(
        [
            w_in.reshape(share, ratio, model).transpose(1, 0, 2).reshape(-1, model),
            w_down,
            w_out,
            small,
        ]
    )
    bundle = lax.all_gather(bundle, BOTH, axis=0, tiled=False)

    metas = [jnp.stack([lengths[b], place]).astype(jnp.int32) for b in range(seqs)]
    saved = []
    contexts = []
    for b in range(seqs):
        q, k, v, ctx, lse = attend(b, metas[b], hidden, weights, bias)
        saved.append((q, k, v, ctx, lse))
        contexts.append([ctx[0]] + [swap(ctx[j], "seq", j) for j in range(1, groups)])
    at = ratio * share
    win_full = bundle[:, :at].reshape(devices, ratio, share, model).transpose(1, 0, 2, 3)
    win_full = win_full.reshape(ratio, model, model)
    wdown_full = bundle[:, at : at + ff_share].reshape(ratio, model, model)
    at += ff_share
    wout_full = bundle[:, at : at + share].reshape(groups, width, model)
    at += share
    small = bundle[:, at].astype(F32)
    parts = [small[:, i * share : (i + 1) * share].reshape(1, model) for i in range(6)]
    bout, gain1, bias1, bdown, gain2, bias2 = parts
    bin_full = small[:, 6 * share : 6 * share + ff_share].reshape(ratio, 1, model)
    wout_rel = xor_order(wout_full, place).reshape(model, model)

    rows = seqs * seg
    context = jnp.concatenate(
        [jnp.concatenate([contexts[b][j] for b in range(seqs)], axis=0) for j in range(groups)],
        axis=1,
    )
    x = hidden_in.reshape(rows, model).astype(F32)
    positions = place * seg + lax.iota(jnp.int32, seg)
    mask = (positions[None, :] < lengths[:, None]).reshape(rows, 1).astype(F32)
    branch = dot(context, wout_rel) + bout
    n1, r1 = normalise(x + branch)
    normed = n1 * gain1 + bias1
    normed_low = normed.astype(BF16)
    acts = []
    slopes = []
    second = bdown
    for c in range(ratio):
        inner = dot(normed_low, win_full[c]) + bin_full[c]
        cdf, pdf = normal_parts(inner)
        act = (inner * cdf).astype(BF16)
        acts.append(act)
        slopes.append(cdf + inner * pdf)
        second = second + dot(act, wdown_full[c])
    n2, r2 = normalise(normed + second)
    output = n2 * gain2 + bias2
    layer_out = (output * mask).astype(BF16).reshape(seqs, seg, model)
    stats = jnp.stack(
        [jnp.sum(v * v * mask) for v in (x, branch, second, output)] + [jnp.sum(mask)]
    )
    stats = jnp.pad(stats, (0, 3)).reshape(1, 8)
    stats = total_over(stats, ("seq", "dp"))
    stat_rms = jnp.sqrt(stats[0, :4] / (stats[0, 4] * model))

    g_out = cotangent.reshape(rows, model).astype(F32) * mask
    g_gain2 = jnp.sum(g_out * n2, axis=0)
    g_bias2 = jnp.sum(g_out, axis=0)
    g_resid2 = normalise_back(g_out * gain2, n2, r2)
    g_second = g_resid2.astype(BF16)
    g_normed = g_resid2
    g_inners = []
    for c in range(ratio):
        g_act = dot(g_second, wdown_full[c], NT)
        g_inner = (g_act * slopes[c]).astype(BF16)
        g_inners.append(g_inner)
        g_normed = g_normed + dot(g_inner, win_full[c], NT)
    g_gain1 = jnp.sum(g_normed * n1, axis=0)
    g_bias1 = jnp.sum(g_normed, axis=0)
    g_resid1 = normalise_back(g_normed * gain1, n1, r1)
    g_branch = g_resid1.astype(BF16)
    g_context = dot(g_branch, wout_rel, NT).astype(BF16).reshape(seqs, seg, groups, width)
    g_pieces = [
        [g_context[b, :, 0]] + [swap(g_context[b, :, j], "seq", j) for j in range(1, groups)]
        for b in range(seqs)
    ]

    g_wdown = jnp.concatenate([dot(a, g_second, TN) for a in acts]).reshape(devices, ff_share, model)
    g_win = jnp.stack([dot(normed_low, g, TN) for g in g_inners])
    g_win = g_win.reshape(ratio, devices, share, model).transpose(1, 0, 2, 3)
    g_win = g_win.reshape(devices, ratio * share, model)
    g_wout = dot(context, g_branch, TN).reshape(groups, width, model)
    g_wout = xor_order(g_wout, place).reshape(devices, share, model)
    g_bdown = jnp.sum(g_second.astype(F32), axis=0)
    g_bout = jnp.sum(g_branch.astype(F32), axis=0)
    g_bin = jnp.concatenate([jnp.sum(g.astype(F32), axis=0) for g in g_inners])
    smalls = [g_bout, g_gain1, g_bias1, g_bdown, g_gain2, g_bias2, g_bin]
    smalls = jnp.concatenate([g.reshape(devices, -1) for g in smalls], axis=1)
    smalls = jnp.pad(smalls, ((0, 0), (0, 8 * model - smalls.shape[1])))
    smalls = smalls.reshape(devices, 8, model)
    grads = jnp.concatenate([g_win, g_wdown, g_wout, smalls], axis=1).astype(BF16)
    owned = lax.psum_scatter(grads, BOTH, scatter_dimension=0, tiled=False).astype(F32)

    sums = [jnp.zeros((model, width), F32)] * 3 + [jnp.zeros((8, width), F32)]
    inputs = []
    g_resid1 = g_resid1.reshape(seqs, seg, model)
    for b in range(seqs):
        gin, *sums = attend_back(b, metas[b], hidden, g_pieces[b], weights, saved[b], sums)
        live = [gin[j] for j in range(groups)]
        bit = 1
        while bit < groups:
            kept = {}
            for j in range(0, len(live), 2):
                kept[j // 2] = live[j] + swap(live[j + 1].astype(BF16), "seq", bit).astype(F32)
            live = [kept[j] for j in range(len(kept))]
            bit *= 2
        inputs.append(g_resid1[b] + live[0])
    grad_input = jnp.stack(inputs)

    bias_rows = jnp.stack([sums[3][0], jnp.zeros_like(sums[3][0]), sums[3][1]])
    heads_grad = jnp.stack([g.reshape(devices, share, width) for g in sums[:3]], axis=1)
    heads_grad = heads_grad.astype(BF16).reshape(ranks, groups, 3, share, width)
    if ranks <= 8:
        total = pick(heads_grad, rank).astype(F32)
        for k in range(1, ranks):
            part = pick(heads_grad, lax.bitwise_xor(rank, k))
            total = total + swap(part, "dp", k).astype(F32)
    else:
        total = lax.psum_scatter(heads_grad, "dp", scatter_dimension=0, tiled=False).astype(F32)
    own = lax.all_to_all(total.astype(BF16), "seq", split_axis=0, concat_axis=0, tiled=True)
    own_wqkv = own.astype(F32).transpose(2, 1, 0, 3).reshape(share, 3 * model)
    bias_rows = total_over(bias_rows, ("dp",))
    bias_all = lax.all_gather(bias_rows, "seq", axis=1, tiled=True)
    own_bq = lax.dynamic_slice(bias_all[0], (first,), (share,))
    own_bv = lax.dynamic_slice(bias_all[2], (first,), (share,))

    at = ratio * share
    own_win = owned[:at].reshape(ratio, share, model).transpose(1, 0, 2).reshape(share, ff)
    own_wdown = owned[at : at + ff_share]
    at += ff_share
    own_wout = owned[at : at + share]
    at += share
    flat = owned[at]
    own_bout, own_gain1, own_bias1, own_bdown, own_gain2, own_bias2 = [
        flat[i * share : (i + 1) * share] for i in range(6)
    ]
    own_bin = flat[6 * share : 6 * share + ff_share]
    return (
        layer_out,
        grad_input,
        own_wqkv,
        own_bq,
        own_bv,
        own_wout,
        own_bout,
        own_gain1,
        own_bias1,
        own_win,
        own_bin,
        own_wdown,
        own_bdown,
        own_gain2,
        own_bias2,
        stat_rms,
    )


def solution(mesh):
    token = P("dp", "seq", None)
    matrix = P(BOTH, None)
    vector = P(BOTH)
    placed = (
        (token, P("dp"), matrix, vector, vector, matrix, vector, vector, vector)
        + (matrix, vector, matrix, vector, vector, vector, token)
    )
    results = (
        (token, token, matrix, vector, vector, matrix, vector, vector, vector)
        + (matrix, vector, matrix, vector, vector, vector, P())
    )
    return jax.shard_map(
        body, mesh=mesh, in_specs=placed, out_specs=results, check_vma=False
    )
```

```python
import functools

import jax
import jax.numpy as jnp
from jax import lax
from jax.experimental import pallas as pl
from jax.experimental.pallas import tpu as pltpu
from jax.sharding import Mesh
from jax.sharding import PartitionSpec as P

HD = 64
NORM_EPS = 1e-12
BATCH_AXES = ("z", "x")
ROW_AXES = ("y", "c")
ALL_AXES = BATCH_AXES + ROW_AXES
F32 = jnp.float32
BF16 = jnp.bfloat16
VMEM_LIMIT = 56 * 1024 * 1024


def dot(left, right, dims=((1,), (0,))):
    return lax.dot_general(left, right, (dims, ((), ())), preferred_element_type=F32)


NT = ((1,), (1,))
TN = ((0,), (0,))


def params():
    return pltpu.CompilerParams(vmem_limit_bytes=VMEM_LIMIT)


def cost(micros):
    return pl.CostEstimate(flops=int(micros * 1e9), transcendentals=0, bytes_accessed=0)


def after(value, *others):
    return lax.optimization_barrier((value,) + others)[0]


def fixed(shape):
    return pl.BlockSpec(shape, lambda i, m: (0,) * len(shape))


def at_block(shape, *index):
    return pl.BlockSpec(shape, lambda i, m: index)


def swap(array, axis, offset=1):
    size = lax.axis_size(axis)
    return lax.ppermute(array, axis, [(i, i ^ offset) for i in range(size)])


def exchange(array, axes):
    return lax.all_to_all(array, axes, split_axis=0, concat_axis=0, tiled=True)


def gather_rows(array):
    far = swap(array, "y")
    near = swap(array, "c")
    return [array, near, far, swap(far, "c")]


def head_lanes(width, head):
    lane = lax.broadcasted_iota(jnp.int32, (1, width), 1)
    return (lane >= head * HD) & (lane < (head + 1) * HD)


def attend_kernel(first, pieces, meta, *refs):
    hidden = refs[:pieces]
    w_ref, b_ref, q_out, k_out, v_out, ctx_out, lse_out, w_all, b_all = refs[pieces:]
    width, seg = ctx_out.shape[1:]
    model = hidden[0].shape[-1]
    heads = width // HD
    length, place = meta[first + pl.program_id(0)], meta[meta.shape[0] - 1]
    filled = (length + seg - 1) // seg

    @pl.when(pl.program_id(0) == 0)
    def _():
        w_all[...] = w_ref[...].reshape(model, 3 * width)
        b_all[...] = jnp.sum(b_ref[...].astype(F32), axis=0)

    for j in range(pieces):
        at = lax.bitwise_xor(place, j)

        @pl.when(at < filled)
        def _():
            qkv = dot(hidden[j][0], w_all[...]) + b_all[0:1]
            q_out[0, at] = qkv[:, :width].astype(BF16) * jnp.asarray(HD**-0.5, BF16)
            k_out[0, at] = qkv[:, width : 2 * width].astype(BF16)
            v_out[0, at] = qkv[:, 2 * width :].astype(BF16)

        @pl.when(at >= filled)
        def _():
            q_out[0, at] = jnp.zeros((seg, width), BF16)
            k_out[0, at] = jnp.zeros((seg, width), BF16)
            v_out[0, at] = jnp.zeros((seg, width), BF16)
            ctx_out[at] = jnp.zeros((width, seg), BF16)
            lse_out[0, at] = jnp.zeros((seg, lse_out.shape[-1]), F32)

    for count in range(1, pieces + 1):

        @pl.when(filled == count)
        def _(count=count):
            keys = k_out[0, 0:count].reshape(count * seg, width)
            values = v_out[0, 0:count].reshape(count * seg, width)
            column = lax.broadcasted_iota(jnp.int32, (1, seg), 1) + (count - 1) * seg
            tail_ok = column < length

            def block(at, carry):
                q = q_out[0, at]
                ctx = jnp.zeros((seg, width), F32)
                lse = jnp.zeros((seg, lse_out.shape[-1]), F32)
                for head in range(heads):
                    here = head_lanes(width, head)
                    scores = dot(jnp.where(here, q, jnp.zeros_like(q)), keys, NT)
                    tail = jnp.where(tail_ok, scores[:, (count - 1) * seg :], -jnp.inf)
                    if count > 1:
                        scores = jnp.concatenate([scores[:, : (count - 1) * seg], tail], axis=1)
                    else:
                        scores = tail
                    top = jnp.max(scores, axis=-1, keepdims=True)
                    weights = jnp.exp(scores - top)
                    total = jnp.sum(weights, axis=-1, keepdims=True)
                    probs = (weights * (1.0 / total)).astype(BF16)
                    ctx = jnp.where(here, dot(probs, values), ctx)
                    lane = lax.broadcasted_iota(jnp.int32, lse.shape, 1)
                    lse = jnp.where(lane == head, top + jnp.log(total), lse)
                ctx_out[at] = ctx.T.astype(BF16)
                lse_out[0, at] = lse
                return carry

            lax.fori_loop(0, count, block, 0)


def attend(first, seqs, meta, hidden, qkv_specs, qkv_args):
    pieces = len(hidden)
    _, seg, model = hidden[0].shape
    width = model // pieces
    saved = jax.ShapeDtypeStruct((seqs, pieces, seg, width), BF16)
    saved_spec = pl.BlockSpec((1, pieces, seg, width), lambda i, m: (i, 0, 0, 0))
    return pl.pallas_call(
        functools.partial(attend_kernel, first, pieces),
        out_shape=(saved,) * 3
        + (
            jax.ShapeDtypeStruct((pieces, width, seqs * seg), BF16),
            jax.ShapeDtypeStruct((seqs, pieces, seg, 128), F32),
        ),
        grid_spec=pltpu.PrefetchScalarGridSpec(
            num_scalar_prefetch=1,
            grid=(seqs,),
            in_specs=[pl.BlockSpec((1, seg, model), lambda i, m: (first + i, 0, 0))] * pieces
            + qkv_specs,
            out_specs=[saved_spec] * 3
            + [
                pl.BlockSpec((pieces, width, seg), lambda i, m: (0, 0, i)),
                pl.BlockSpec((1, pieces, seg, 128), lambda i, m: (i, 0, 0, 0)),
            ],
            scratch_shapes=[pltpu.VMEM((model, 3 * width), BF16), pltpu.VMEM((8, 3 * width), F32)],
        ),
        compiler_params=params(),
        cost_estimate=cost(9 * seqs),
        name="attend",
    )(meta, *hidden, *qkv_args)


def attend_back_kernel(first, pieces, meta, *refs):
    hidden = refs[:pieces]
    (w_ref, grad_in, q_in, k_in, v_in, ctx_in, lse_in, sum_w, sum_b) = refs[pieces : pieces + 9]
    gin_keep, gin_send, out_w, out_b, w_all, dq_t, d_all = refs[pieces + 9 :]
    width, seg = grad_in.shape[1:]
    heads = width // HD
    model = hidden[0].shape[-1]
    length, place = meta[first + pl.program_id(0)], meta[meta.shape[0] - 1]
    filled = (length + seg - 1) // seg

    @pl.when(pl.program_id(0) == 0)
    def _():
        w_all[...] = w_ref[...].reshape(model, 3 * width)
        out_w[...] = sum_w[...]
        out_b[...] = sum_b[...]

    for count in range(1, pieces + 1):

        @pl.when(filled == count)
        def _(count=count):
            rows = count * seg
            queries = q_in[0, 0:count].reshape(rows, width)
            queries_t = queries.T
            upstream_t = jnp.concatenate([grad_in[at] for at in range(count)], axis=1)
            upstream = upstream_t.T
            ctx_t = jnp.concatenate([ctx_in[at] for at in range(count)], axis=1)
            lse_t = jnp.concatenate([lse_in[0, at].T[0:8] for at in range(count)], axis=1)
            product_t = ctx_t.astype(F32) * upstream_t.astype(F32)
            delta_t = [
                jnp.sum(product_t[h * HD : (h + 1) * HD], axis=0, keepdims=True)
                for h in range(heads)
            ]
            dq_t[:, 0:rows] = jnp.zeros((width, rows), F32)

            def block(at, carry):
                keys = k_in[0, at]
                values = v_in[0, at]
                keys_t = keys.T
                row = lax.broadcasted_iota(jnp.int32, (seg, 1), 0) + at * seg
                row_ok = row < length
                dk = jnp.zeros((seg, width), F32)
                dv = jnp.zeros((seg, width), F32)
                for head in range(heads):
                    here = head_lanes(width, head)
                    scores = dot(jnp.where(here, keys, jnp.zeros_like(keys)), queries_t)
                    probs = jnp.exp(scores - lse_t[head : head + 1])
                    probs = jnp.where(row_ok, probs, 0.0)
                    g_probs = dot(jnp.where(here, values, jnp.zeros_like(values)), upstream_t)
                    g_scores = (probs * (g_probs - delta_t[head])).astype(BF16)
                    dv = jnp.where(here, dot(probs.astype(BF16), upstream), dv)
                    dk = jnp.where(here, dot(g_scores, queries), dk)
                    part = slice(head * HD, (head + 1) * HD)
                    dq_t[part, 0:rows] += dot(keys_t[part], g_scores)
                d_all[at, :, width : 2 * width] = dk.astype(BF16)
                d_all[at, :, 2 * width :] = dv.astype(BF16)
                return carry

            lax.fori_loop(0, count, block, 0)
            for at in range(count):
                piece = dq_t[:, at * seg : (at + 1) * seg]
                d_all[at, :, 0:width] = (piece.T * HD**-0.5).astype(BF16)

    for j in range(pieces):
        at = lax.bitwise_xor(place, j)
        gin_out = (gin_send if j % 2 else gin_keep).at[j // 2]

        @pl.when(at < filled)
        def _():
            grads = d_all[at]
            gin_out[...] = dot(grads, w_all[...], NT).astype(BF16)
            out_w[...] += dot(hidden[j][0], grads, TN)
            out_b[0:1] += jnp.sum(grads.astype(F32), axis=0, keepdims=True)

        @pl.when(at >= filled)
        def _():
            gin_out[...] = jnp.zeros((seg, model), BF16)


def attend_back(first, seqs, meta, hidden, w_spec, w_arg, grad_ctx, saved, sums):
    pieces = len(hidden)
    _, seg, model = hidden[0].shape
    width = model // pieces
    saved_spec = pl.BlockSpec((1, pieces, seg, width), lambda i, m: (i, 0, 0, 0))
    sum_shapes = [(model, 3 * width), (8, 3 * width)]
    return pl.pallas_call(
        functools.partial(attend_back_kernel, first, pieces),
        out_shape=(jax.ShapeDtypeStruct((pieces // 2, seqs * seg, model), BF16),) * 2
        + tuple(jax.ShapeDtypeStruct(s, F32) for s in sum_shapes),
        grid_spec=pltpu.PrefetchScalarGridSpec(
            num_scalar_prefetch=1,
            grid=(seqs,),
            in_specs=[pl.BlockSpec((1, seg, model), lambda i, m: (first + i, 0, 0))] * pieces
            + [w_spec, pl.BlockSpec((pieces, width, seg), lambda i, m: (0, 0, first + i))]
            + [saved_spec] * 3
            + [
                pl.BlockSpec((pieces, width, seg), lambda i, m: (0, 0, i)),
                pl.BlockSpec((1, pieces, seg, 128), lambda i, m: (i, 0, 0, 0)),
            ]
            + [fixed(s) for s in sum_shapes],
            out_specs=[pl.BlockSpec((pieces // 2, seg, model), lambda i, m: (0, i, 0))] * 2
            + [fixed(s) for s in sum_shapes],
            scratch_shapes=[
                pltpu.VMEM((model, 3 * width), BF16),
                pltpu.VMEM((width, pieces * seg), F32),
                pltpu.VMEM((pieces, seg, 3 * width), BF16),
            ],
        ),
        compiler_params=params(),
        cost_estimate=cost(13 * seqs),
        name="attend_back",
    )(meta, *hidden, w_arg, grad_ctx, *saved, *sums)


def normal_parts(v):
    size = jnp.abs(v) * (0.5**0.5)
    t = 1.0 / (1.0 + 0.3275911 * size)
    poly = t * (
        0.254829592
        + t * (-0.284496736 + t * (1.421413741 + t * (-1.453152027 + t * 1.061405429)))
    )
    bell = jnp.exp(-0.5 * v * v)
    upper = 0.5 * poly * bell
    cdf = jnp.where(v < 0, upper, 1.0 - upper)
    return cdf, bell * (0.5 / jnp.pi) ** 0.5


def normalise(values):
    center = values - jnp.mean(values, axis=-1, keepdims=True)
    root = lax.rsqrt(jnp.mean(center * center, axis=-1, keepdims=True) + NORM_EPS)
    return center * root, root


def normalise_back(grad, unit, root):
    mean_grad = jnp.mean(grad, axis=-1, keepdims=True)
    mean_prod = jnp.mean(grad * unit, axis=-1, keepdims=True)
    return root * (grad - mean_grad - unit * mean_prod)


ROWS = 32


def row_loop(start, stop, fn):
    def step(i, carry):
        fn(pl.ds(pl.multiple_of(start + i * ROWS, ROWS), ROWS), start + i * ROWS)
        return carry

    lax.fori_loop(0, (stop - start) // ROWS, step, 0, unroll=2)


def fold(values):
    return jnp.sum(values.reshape(-1, 8, values.shape[-1]), axis=0)


def dense_kernel(ratio, groups, meta, *refs):
    ctxs = refs[:groups]
    (x_ref, cot_ref, wout_ref, win_ref, wdown_ref, small_a, small_b) = refs[groups : groups + 7]
    (
        out_ref,
        gres_ref,
        gctx_ref,
        act_ref,
        ginner_ref,
        gsecond_ref,
        low_ref,
        gbranch_ref,
        sums_ref,
        stats_ref,
        vecs,
        normed,
        unit,
        root,
        acc,
        inner,
        slopes,
        acc_sums,
    ) = refs[groups + 7 :]
    step = pl.program_id(0)
    seqs, seg, model = x_ref.shape
    rows = seqs * seg
    place = meta[meta.shape[0] - 1]
    parts, width = ctxs[0].shape[:2]

    def mask_of(base):
        seq = base // seg
        position = lax.broadcasted_iota(jnp.int32, (ROWS, 1), 0) + (base - seq * seg)
        return (position + place * seg < meta[seq]).astype(F32)

    def tokens(ref, base):
        seq = base // seg
        return ref[seq, pl.ds(pl.multiple_of(base - seq * seg, ROWS), ROWS)].astype(F32)

    @pl.when(step == 0)
    def _():
        vecs[0:8] = jnp.sum(small_a[...].astype(F32), axis=0)
        vecs[8:16] = jnp.sum(small_b[...].astype(F32), axis=0)
        acc_sums[...] = jnp.zeros(acc_sums.shape, F32)
        wout = wout_ref[...].reshape(model, model)
        done = 0
        for ref in ctxs:
            many = ref.shape[2]
            context = ref[...].reshape(parts * width, many)
            branch = dot(context, wout, TN) + vecs[0:1]
            acc[done : done + many] = branch
            done += many

        def first_norm(at, base):
            mask = mask_of(base)
            x = tokens(x_ref, base)
            branch = acc[at]
            n1, r1 = normalise(x + branch)
            value = n1 * vecs[1:2] + vecs[2:3]
            unit[at] = n1
            root[at] = jnp.broadcast_to(r1, (ROWS, root.shape[-1]))
            normed[at] = value
            low_ref[at] = value.astype(BF16)
            acc_sums[0] += fold(x * x * mask)
            acc_sums[1] += fold(branch * branch * mask)

        row_loop(0, rows, first_norm)
        acc[...] = jnp.broadcast_to(vecs[3:4], acc.shape)

    @pl.when(step < ratio)
    def _():
        chunk = step
        win = win_ref[...].reshape(model, model)
        wdown = wdown_ref[...].reshape(model, model)
        bin_row = vecs[pl.ds(6 + chunk, 1)]
        for b in range(seqs):
            lo, hi = b * seg, (b + 1) * seg
            inner[lo:hi] = dot(low_ref[lo:hi], win)

            def activate(at, base):
                value = inner[at] + bin_row
                cdf, pdf = normal_parts(value)
                act_ref[0, at] = (value * cdf).astype(BF16)
                slopes[chunk, at] = cdf + value * pdf

            row_loop(lo, hi, activate)
            acc[lo:hi] += dot(act_ref[0, lo:hi], wdown)

    @pl.when(step == ratio)
    def _():
        def second_norm(at, base):
            mask = mask_of(base)
            second = acc[at]
            n2, r2 = normalise(normed[at] + second)
            output = n2 * vecs[5:6] + vecs[15:16]
            out_ref[at] = (output * mask).astype(BF16)
            g_out = tokens(cot_ref, base) * mask
            g_resid = normalise_back(g_out * vecs[5:6], n2, r2)
            low = g_resid.astype(BF16)
            gsecond_ref[at] = low
            acc[at] = g_resid
            acc_sums[2] += fold(second * second * mask)
            acc_sums[3] += fold(output * output * mask)
            acc_sums[4] += fold(low.astype(F32))
            acc_sums[5] += fold(g_out * n2)
            acc_sums[6] += fold(g_out)

        row_loop(0, rows, second_norm)

    @pl.when(step >= ratio)
    def _():
        chunk = 2 * ratio - 1 - step
        win = win_ref[...].reshape(model, model)
        wdown = wdown_ref[...].reshape(model, model)
        acc_sums[7] = jnp.zeros(acc_sums.shape[1:], F32)
        for b in range(seqs):
            lo, hi = b * seg, (b + 1) * seg
            inner[lo:hi] = dot(gsecond_ref[lo:hi], wdown, NT)

            def through(at, base):
                low = (inner[at] * slopes[chunk, at]).astype(BF16)
                ginner_ref[0, at] = low
                acc_sums[7] += fold(low.astype(F32))

            row_loop(lo, hi, through)
            acc[lo:hi] += dot(ginner_ref[0, lo:hi], win, NT)
        sums_ref[pl.ds(6 + chunk, 1)] = jnp.sum(acc_sums[7], axis=0, keepdims=True)

    @pl.when(step == 2 * ratio - 1)
    def _():
        for k in range(8, 11):
            acc_sums[k] = jnp.zeros(acc_sums.shape[1:], F32)

        def first_back(at, base):
            grad = acc[at]
            n1 = unit[at]
            g_resid = normalise_back(grad * vecs[1:2], n1, root[at][:, 0:1])
            low = g_resid.astype(BF16)
            gres_ref[at] = g_resid
            gbranch_ref[at] = low
            acc_sums[8] += fold(low.astype(F32))
            acc_sums[9] += fold(grad * n1)
            acc_sums[10] += fold(grad)

        row_loop(0, rows, first_back)
        wout = wout_ref[...].reshape(model, model)
        for t in range(parts):
            piece = dot(wout[t * width : (t + 1) * width], gbranch_ref[...], NT)
            gctx_ref[t] = piece.astype(BF16)

        def total(k):
            return jnp.sum(acc_sums[k], axis=0, keepdims=True)

        for row, k in enumerate((8, 9, 10, 4, 5, 6)):
            sums_ref[row : row + 1] = total(k)
        for row in range(4):
            stats_ref[row : row + 1] = total(row)
        stats_ref[4:8] = jnp.zeros((4, model), F32)
        sums_ref[6 + ratio :] = jnp.zeros((16 - 6 - ratio, model), F32)


def dense(meta, ctxs, x, cot, weight_specs, weight_args, ratio):
    seqs, seg, model = x.shape
    rows = seqs * seg
    parts, width, _ = ctxs[0].shape
    low = jax.ShapeDtypeStruct((rows, model), BF16)
    chunked = jax.ShapeDtypeStruct((ratio, rows, model), BF16)
    flat = (rows, model)
    last = 2 * ratio - 1
    return pl.pallas_call(
        functools.partial(dense_kernel, ratio, len(ctxs)),
        out_shape=(
            low,
            jax.ShapeDtypeStruct(flat, F32),
            jax.ShapeDtypeStruct((parts, width, rows), BF16),
            chunked,
            chunked,
            low,
            low,
            low,
            jax.ShapeDtypeStruct((16, model), F32),
            jax.ShapeDtypeStruct((8, model), F32),
        ),
        grid_spec=pltpu.PrefetchScalarGridSpec(
            num_scalar_prefetch=1,
            grid=(2 * ratio,),
            in_specs=[fixed(c.shape) for c in ctxs]
            + [fixed(x.shape), fixed(cot.shape)]
            + weight_specs,
            out_specs=[
                fixed(flat),
                fixed(flat),
                fixed((parts, width, rows)),
                pl.BlockSpec((1, rows, model), lambda i, m: (jnp.minimum(i, ratio - 1), 0, 0)),
                pl.BlockSpec(
                    (1, rows, model), lambda i, m: (jnp.minimum(last - i, ratio - 1), 0, 0)
                ),
                fixed(flat),
                fixed(flat),
                fixed(flat),
                fixed((16, model)),
                fixed((8, model)),
            ],
            scratch_shapes=[
                pltpu.VMEM((16, model), F32),
                pltpu.VMEM(flat, F32),
                pltpu.VMEM(flat, F32),
                pltpu.VMEM((rows, 128), F32),
                pltpu.VMEM(flat, F32),
                pltpu.VMEM(flat, F32),
                pltpu.VMEM((ratio, rows, model), F32),
                pltpu.VMEM((11, 8, model), F32),
            ],
        ),
        compiler_params=params(),
        cost_estimate=cost(50),
        name="dense",
    )(meta, *ctxs, x, cot, *weight_args)


def down_kernel(act_ref, g_ref, out_ref):
    grad = dot(act_ref[0], g_ref[...], TN).astype(BF16)
    out_ref[...] = grad.reshape(out_ref.shape)


def down_grads(acts, g_second, each):
    ratio, rows, model = acts.shape
    return pl.pallas_call(
        down_kernel,
        out_shape=jax.ShapeDtypeStruct((ratio * model // each, each, model), BF16),
        grid=(ratio,),
        in_specs=[
            pl.BlockSpec((1, rows, model), lambda i: (i, 0, 0)),
            pl.BlockSpec((rows, model), lambda i: (0, 0)),
        ],
        out_specs=pl.BlockSpec((model // each, each, model), lambda i: (i, 0, 0)),
        compiler_params=params(),
        cost_estimate=cost(8),
        name="down_grads",
    )(acts, g_second)


def rest_kernel(ratio, groups, cut, meta, low_ref, ginner_ref, *refs):
    ctxs = refs[:groups]
    gbranch_ref, sums_ref = refs[groups : groups + 2]
    outs = refs[groups + 2 : groups + 6]
    grad = refs[groups + 6]
    me = meta[meta.shape[0] - 2]
    step = pl.program_id(0)
    devices, each, model = grad.shape
    near, far = outs[0].shape[:2]

    @pl.when(step < ratio)
    def _():
        grad[...] = dot(low_ref[...], ginner_ref[0], TN).astype(BF16).reshape(grad.shape)

    @pl.when(step == ratio)
    def _():
        total = 0.0
        done = 0
        for ref in ctxs:
            parts, width, many = ref.shape
            context = ref[...].reshape(parts * width, many)
            total = total + dot(context, gbranch_ref[done : done + many])
            done += many
        grad[...] = total.astype(BF16).reshape(grad.shape)

    @pl.when(step == ratio + 1)
    def _():
        block = jnp.concatenate([sums_ref[...], jnp.zeros((each - 16, model), F32)], axis=0)
        grad[...] = jnp.broadcast_to(block.astype(BF16)[None], grad.shape)

    for keep, send, here in ((outs[0], outs[1], step < cut), (outs[2], outs[3], step >= cut)):

        @pl.when(here)
        def _():
            for k in range(near):
                for z in range(far):
                    slot = (z * near + k) * 2
                    keep[k, z] = grad[lax.bitwise_xor(me, slot)]
                    send[k, z] = grad[lax.bitwise_xor(me, slot + 1)]


def rest_grads(meta, low, g_inner, ctxs, g_branch, sums, near, far, each):
    ratio, rows, model = g_inner.shape
    cut = (ratio + 2) // 2
    shapes = [jax.ShapeDtypeStruct((near, far, n * each, model), BF16) for n in (cut, ratio + 2 - cut)]
    specs = [
        pl.BlockSpec((near, far, each, model), lambda i, m: (0, 0, jnp.minimum(i, cut - 1), 0)),
        pl.BlockSpec((near, far, each, model), lambda i, m: (0, 0, jnp.maximum(i - cut, 0), 0)),
    ]
    return pl.pallas_call(
        functools.partial(rest_kernel, ratio, len(ctxs), cut),
        out_shape=(shapes[0], shapes[0], shapes[1], shapes[1]),
        grid_spec=pltpu.PrefetchScalarGridSpec(
            num_scalar_prefetch=1,
            grid=(ratio + 2,),
            in_specs=[
                fixed(low.shape),
                pl.BlockSpec((1, rows, model), lambda i, m: (jnp.minimum(i, ratio - 1), 0, 0)),
            ]
            + [fixed(c.shape) for c in ctxs]
            + [fixed(g_branch.shape), fixed(sums.shape)],
            out_specs=[specs[0], specs[0], specs[1], specs[1]],
            scratch_shapes=[pltpu.VMEM((2 * near * far, each, model), BF16)],
        ),
        compiler_params=params(),
        cost_estimate=cost(10),
        name="rest_grads",
    )(meta, low, g_inner, *ctxs, g_branch, sums)


def natural_grads(acts, g_second, low, g_inner, ctxs, g_branch, sums, devices, share):
    ratio, rows, model = acts.shape
    down = jnp.concatenate([dot(a, g_second, TN) for a in acts]).reshape(devices, -1, model)
    context = jnp.concatenate(ctxs, axis=2).reshape(model, rows)
    rest = [dot(low, g, TN) for g in g_inner] + [dot(context, g_branch)]
    rest = [r.reshape(devices, share, model) for r in rest]
    rest.append(jnp.broadcast_to(sums[None], (devices,) + sums.shape))
    return down.astype(BF16), jnp.concatenate(rest, axis=1).astype(BF16)


def pair(kept, sent):
    return (kept.astype(F32) + sent.astype(F32)).astype(BF16)


def add_up(pieces):
    return jnp.sum(pieces.astype(F32), axis=0)


def body(
    hidden_in,
    lengths,
    w_qkv,
    b_query,
    b_value,
    w_out,
    b_out,
    gain_one,
    bias_one,
    w_in,
    b_in,
    w_down,
    b_down,
    gain_two,
    bias_two,
    cotangent,
):
    seqs, seg, model = hidden_in.shape
    sizes = tuple(lax.axis_size(a) for a in ALL_AXES)
    far, wide, near_y, cores = sizes
    groups = near_y * cores
    devices = far * wide * groups
    place = lax.axis_index(ROW_AXES)
    me = lax.axis_index(ALL_AXES)
    share = model // devices
    ff = w_in.shape[1]
    ff_share = ff // devices
    ratio = ff // model
    width = model // groups
    aligned = share % 8 == 0 and devices == 8 * ratio and far == ratio
    meta = jnp.concatenate([lengths, me[None], place[None]]).astype(jnp.int32)

    first = me * share
    owner = first // width
    within = first - owner * width
    cut = w_qkv.reshape(share, 3, groups, width).transpose(2, 0, 1, 3)
    cut = cut.reshape(groups, share, 3 * width)
    extra = jnp.zeros((1, 8, 3 * width), BF16)
    extra = lax.dynamic_update_slice(extra, b_query[None, None], (0, 0, within))
    extra = lax.dynamic_update_slice(extra, b_value[None, None], (0, 0, 2 * width + within))
    mine = lax.broadcasted_iota(jnp.int32, (groups, 1, 1), 0) == owner
    extra = jnp.where(mine, extra, jnp.zeros_like(extra))
    packed = jnp.concatenate([cut, extra], axis=1)
    tall = share + 8
    packed = jnp.broadcast_to(packed[None], (far * wide,) + packed.shape)
    qkv = exchange(packed.reshape(devices, tall, 3 * width), ALL_AXES)
    if aligned:
        qkv_specs = [
            at_block((devices, share, 3 * width), 0, 0, 0),
            at_block((devices, 8, 3 * width), 0, share // 8, 0),
        ]
        qkv_args = [qkv, qkv]
    else:
        qkv_args = [qkv[:, :share].reshape(model, 3 * width), qkv[:, share:]]
        qkv_specs = [fixed(a.shape) for a in qkv_args]

    hidden = gather_rows(hidden_in)

    small = jnp.zeros((16, model), BF16)
    vectors = jnp.stack([b_out, gain_one, bias_one, b_down, b_down, gain_two])
    small = lax.dynamic_update_slice(small, vectors, (0, first))
    small = lax.dynamic_update_slice(small, bias_two[None], (15, first))
    ff_first = me * ff_share
    ff_row = ff_first // model
    small = lax.dynamic_update_slice(small, b_in[None], (6 + ff_row, ff_first - ff_row * model))
    bundle = jnp.concatenate(
        [
            w_in.reshape(share, ratio, model).transpose(1, 0, 2).reshape(-1, model),
            w_down,
            w_out,
            small,
        ]
    )
    bundle = lax.all_gather(bundle, ALL_AXES, axis=0, tiled=False)
    at = ratio * share
    last = 2 * ratio - 1
    chunk = lambda i: jnp.minimum(i, last - i)
    if aligned:
        weight_specs = [
            at_block((devices, share, model), 0, (at + ff_share) // share, 0),
            pl.BlockSpec((devices, share, model), lambda i, m: (0, chunk(i), 0)),
            pl.BlockSpec((devices // ratio, ff_share, model), lambda i, m: (chunk(i), 1, 0)),
            at_block((devices, 8, model), 0, (at + ff_share + share) // 8, 0),
            at_block((devices, 8, model), 0, (at + ff_share + share) // 8 + 1, 0),
        ]
        weight_args = [bundle] * 5
    else:
        win = bundle[:, :at].reshape(devices, ratio, share, model).transpose(1, 0, 2, 3)
        small = bundle[:, at + ff_share + share :]
        weight_args = [
            bundle[:, at + ff_share : at + ff_share + share].reshape(model, model),
            win.reshape(ratio, model, model),
            bundle[:, at : at + ff_share].reshape(ratio, model, model),
            small[:, :8],
            small[:, 8:],
        ]
        by_chunk = pl.BlockSpec((1, model, model), lambda i, m: (chunk(i), 0, 0))
        weight_specs = [fixed(a.shape) for a in weight_args]
        weight_specs[1] = weight_specs[2] = by_chunk

    spans = [(0, seqs - 1), (seqs - 1, 1)]
    saved = []
    ctxs = []
    for start, count in spans:
        q, k, v, ctx, lse = attend(start, count, meta, hidden, qkv_specs, qkv_args)
        saved.append((q, k, v, ctx, lse))
        ctxs.append(exchange(ctx, ROW_AXES))

    (out, g_resid, g_ctx, acts, g_inner, g_second, low, g_branch, sums, stats) = dense(
        meta, ctxs, hidden_in, cotangent, weight_specs, weight_args, ratio
    )
    layer_out = out.reshape(seqs, seg, model)
    g_ctx = exchange(g_ctx, ROW_AXES)

    if aligned:
        down = down_grads(acts, g_second, ff_share)
        down = lax.psum_scatter(down, ALL_AXES, scatter_dimension=0, tiled=False)
        keep_a, send_a, keep_b, send_b = rest_grads(
            meta, low, g_inner, ctxs, g_branch, sums, wide * near_y, far, share
        )
        shape = (wide, near_y) + keep_a.shape[1:]
        got_a, got_b = swap(send_a, "c").reshape(shape), swap(send_b, "c").reshape(shape)
        keep_a, keep_b = keep_a.reshape(shape), keep_b.reshape(shape)
        go_a, go_b = pair(keep_a[1], got_a[1]), pair(keep_b[:, 1], got_b[:, 1])
        stay_a, stay_b = pair(keep_a[0], got_a[0]), pair(keep_b[:, 0], got_b[:, 0])
        gate = (go_a, go_b)
    else:
        down, rest = natural_grads(
            acts, g_second, low, g_inner, ctxs, g_branch, sums, devices, share
        )
        down = lax.psum_scatter(down, ALL_AXES, scatter_dimension=0, tiled=False)
        rest = lax.psum_scatter(rest, ALL_AXES, scatter_dimension=0, tiled=False)
        gate = ()

    w_sums = [jnp.zeros((model, 3 * width), F32), jnp.zeros((8, 3 * width), F32)]
    inputs = []
    for (start, count), kept in zip(spans, saved):
        g_ctx = after(g_ctx, *gate)
        gin_keep, gin_send, *w_sums = attend_back(
            start, count, meta, hidden, qkv_specs[0], qkv_args[0], g_ctx, kept, w_sums
        )
        if start == 0 and aligned:
            got_a, got_b = swap(go_a, "x"), swap(go_b, "y")
            go_a, go_b = pair(stay_a[1], got_a[1]), pair(stay_b[1], got_b[1])
            stay_a, stay_b = pair(stay_a[0], got_a[0]), pair(stay_b[0], got_b[0])
            gate = (go_a, go_b)
        near = swap(gin_send, "c")
        here = gin_keep[0].astype(F32) + near[0].astype(F32)
        beyond = swap(pair(gin_keep[1], near[1]), "y")
        lo = start * seg
        own = g_resid[lo : lo + count * seg] + here + beyond.astype(F32)
        inputs.append(own.reshape(count, seg, model))
    grad_input = jnp.concatenate(inputs)
    if aligned:
        kept_a, kept_b = pair(stay_a, swap(go_a, "y")), pair(stay_b, swap(go_b, "x"))
        bit = 1
        while bit < far:
            kept_a = kept_a.reshape((-1, 2) + kept_a.shape[-2:])
            kept_b = kept_b.reshape((-1, 2) + kept_b.shape[-2:])
            kept_a = pair(kept_a[:, 0], swap(kept_a[:, 1], "z", bit))
            kept_b = pair(kept_b[:, 0], swap(kept_b[:, 1], "z", bit))
            bit *= 2
        rest = jnp.concatenate([kept_a[0], kept_b[0]])
    rest = rest.astype(F32)
    down = down.astype(F32)

    squares = jnp.sum(stats[:4], axis=1)
    valid = jnp.sum(jnp.clip(lengths - place * seg, 0, seg)).astype(F32)
    exact = jnp.concatenate([squares, valid[None]])
    pieces = []
    for _ in range(3):
        pieces.append(lax.reduce_precision(exact, 8, 7))
        exact = exact - pieces[-1]
    stat_row = jnp.pad(jnp.concatenate(pieces), (0, 3 * width - 15))
    rows = jnp.stack([w_sums[1][0], stat_row]).astype(BF16)
    rows = jnp.pad(rows, ((0, 6), (0, 0)))
    block = jnp.concatenate(
        [
            w_sums[0].astype(BF16).reshape(devices, share, 3 * width),
            jnp.broadcast_to(rows[None], (devices,) + rows.shape),
        ],
        axis=1,
    )
    block = exchange(block, ALL_AXES).astype(F32)
    totals = jnp.sum(block.reshape(far * wide, groups, tall, 3 * width), axis=0)
    own_wqkv = totals[:, :share].reshape(groups, share, 3, width).transpose(1, 2, 0, 3)
    own_wqkv = own_wqkv.reshape(share, 3 * model)
    own_bq = lax.dynamic_slice(totals[:, share, :width].reshape(-1), (first,), (share,))
    own_bv = lax.dynamic_slice(totals[:, share, 2 * width :].reshape(-1), (first,), (share,))
    stats = jnp.sum(block[:, share + 1, :15], axis=0)
    stats = stats[:5] + stats[5:10] + stats[10:]
    stat_rms = jnp.sqrt(stats[:4] / (stats[4] * model))

    rest = rest.reshape(-1, model)
    own_win = rest[: ratio * share].reshape(ratio, share, model).transpose(1, 0, 2)
    own_win = own_win.reshape(share, ff)
    at = ratio * share
    own_wout = rest[at : at + share]
    at += share
    vectors = lax.dynamic_slice(rest, (at, first), (6, share))
    own_bin = lax.dynamic_slice(rest, (at + 6 + ff_row, ff_first - ff_row * model), (1, ff_share))
    return (
        layer_out,
        grad_input,
        own_wqkv,
        own_bq,
        own_bv,
        own_wout,
        vectors[0],
        vectors[1],
        vectors[2],
        own_win,
        own_bin[0],
        down.reshape(ff_share, model),
        vectors[3],
        vectors[4],
        vectors[5],
        stat_rms,
    )


def solution(mesh):
    dp, seq = mesh.shape["dp"], mesh.shape["seq"]
    finer = Mesh(mesh.devices.reshape(dp // 2, 2, seq // 2, 2), ALL_AXES)
    token = P(BATCH_AXES, ROW_AXES, None)
    matrix = P(ALL_AXES, None)
    vector = P(ALL_AXES)
    placed = (
        (token, P(BATCH_AXES), matrix, vector, vector, matrix, vector, vector, vector)
        + (matrix, vector, matrix, vector, vector, vector, token)
    )
    results = (
        (token, token, matrix, vector, vector, matrix, vector, vector, vector)
        + (matrix, vector, matrix, vector, vector, vector, P())
    )
    return jax.shard_map(
        body, mesh=finer, in_specs=placed, out_specs=results, check_vma=False
    )
```

```python
import functools

import jax
import jax.numpy as jnp
from jax import lax
from jax.experimental import pallas as pl
from jax.experimental.pallas import tpu as pltpu
from jax.sharding import Mesh
from jax.sharding import PartitionSpec as P

HD = 64
NORM_EPS = 1e-12
BATCH_AXES = ("z", "x")
ROW_AXES = ("y", "c")
ALL_AXES = BATCH_AXES + ROW_AXES
F32 = jnp.float32
BF16 = jnp.bfloat16
VMEM_LIMIT = 56 * 1024 * 1024


def dot(left, right, dims=((1,), (0,))):
    return lax.dot_general(left, right, (dims, ((), ())), preferred_element_type=F32)


NT = ((1,), (1,))
TN = ((0,), (0,))


def params():
    return pltpu.CompilerParams(vmem_limit_bytes=VMEM_LIMIT)


def cost(micros):
    return pl.CostEstimate(flops=int(micros * 1e9), transcendentals=0, bytes_accessed=0)


def after(value, *others):
    return lax.optimization_barrier((value,) + others)[0]


def fixed(shape):
    return pl.BlockSpec(shape, lambda i, m: (0,) * len(shape))


def at_block(shape, *index):
    return pl.BlockSpec(shape, lambda i, m: index)


def swap(array, axis, offset=1):
    size = lax.axis_size(axis)
    return lax.ppermute(array, axis, [(i, i ^ offset) for i in range(size)])


def exchange(array, axes):
    return lax.all_to_all(array, axes, split_axis=0, concat_axis=0, tiled=True)


def gather_rows(array):
    far = swap(array, "y")
    near = swap(array, "c")
    return [array, near, far, swap(far, "c")]


def head_lanes(width, head):
    lane = lax.broadcasted_iota(jnp.int32, (1, width), 1)
    return (lane >= head * HD) & (lane < (head + 1) * HD)


def attend_kernel(first, pieces, meta, *refs):
    hidden = refs[:pieces]
    w_ref, b_ref, q_out, k_out, v_out, ctx_out, lse_out, w_all, b_all = refs[pieces:]
    width, seg = ctx_out.shape[1:]
    model = hidden[0].shape[-1]
    heads = width // HD
    length, place = meta[first + pl.program_id(0)], meta[meta.shape[0] - 1]
    filled = (length + seg - 1) // seg

    @pl.when(pl.program_id(0) == 0)
    def _():
        w_all[...] = w_ref[...].reshape(model, 3 * width)
        b_all[...] = jnp.sum(b_ref[...].astype(F32), axis=0)

    for j in range(pieces):
        at = lax.bitwise_xor(place, j)

        @pl.when(at < filled)
        def _():
            qkv = dot(hidden[j][0], w_all[...]) + b_all[0:1]
            q_out[0, at] = qkv[:, :width].astype(BF16) * jnp.asarray(HD**-0.5, BF16)
            k_out[0, at] = qkv[:, width : 2 * width].astype(BF16)
            v_out[0, at] = qkv[:, 2 * width :].astype(BF16)

        @pl.when(at >= filled)
        def _():
            q_out[0, at] = jnp.zeros((seg, width), BF16)
            k_out[0, at] = jnp.zeros((seg, width), BF16)
            v_out[0, at] = jnp.zeros((seg, width), BF16)
            ctx_out[at] = jnp.zeros((width, seg), BF16)
            lse_out[0, at] = jnp.zeros((seg, lse_out.shape[-1]), F32)

    for count in range(1, pieces + 1):

        @pl.when(filled == count)
        def _(count=count):
            keys = k_out[0, 0:count].reshape(count * seg, width)
            values = v_out[0, 0:count].reshape(count * seg, width)
            column = lax.broadcasted_iota(jnp.int32, (1, seg), 1) + (count - 1) * seg
            tail_ok = column < length

            def block(at, carry):
                q = q_out[0, at]
                ctx = jnp.zeros((seg, width), F32)
                lse = jnp.zeros((seg, lse_out.shape[-1]), F32)
                for head in range(heads):
                    here = head_lanes(width, head)
                    scores = dot(jnp.where(here, q, jnp.zeros_like(q)), keys, NT)
                    tail = jnp.where(tail_ok, scores[:, (count - 1) * seg :], -jnp.inf)
                    if count > 1:
                        scores = jnp.concatenate([scores[:, : (count - 1) * seg], tail], axis=1)
                    else:
                        scores = tail
                    top = jnp.max(scores, axis=-1, keepdims=True)
                    weights = jnp.exp(scores - top)
                    total = jnp.sum(weights, axis=-1, keepdims=True)
                    probs = (weights * (1.0 / total)).astype(BF16)
                    ctx = jnp.where(here, dot(probs, values), ctx)
                    lane = lax.broadcasted_iota(jnp.int32, lse.shape, 1)
                    lse = jnp.where(lane == head, top + jnp.log(total), lse)
                ctx_out[at] = ctx.T.astype(BF16)
                lse_out[0, at] = lse
                return carry

            lax.fori_loop(0, count, block, 0)


def attend(first, seqs, meta, hidden, qkv_specs, qkv_args):
    pieces = len(hidden)
    _, seg, model = hidden[0].shape
    width = model // pieces
    saved = jax.ShapeDtypeStruct((seqs, pieces, seg, width), BF16)
    saved_spec = pl.BlockSpec((1, pieces, seg, width), lambda i, m: (i, 0, 0, 0))
    return pl.pallas_call(
        functools.partial(attend_kernel, first, pieces),
        out_shape=(saved,) * 3
        + (
            jax.ShapeDtypeStruct((pieces, width, seqs * seg), BF16),
            jax.ShapeDtypeStruct((seqs, pieces, seg, 128), F32),
        ),
        grid_spec=pltpu.PrefetchScalarGridSpec(
            num_scalar_prefetch=1,
            grid=(seqs,),
            in_specs=[pl.BlockSpec((1, seg, model), lambda i, m: (first + i, 0, 0))] * pieces
            + qkv_specs,
            out_specs=[saved_spec] * 3
            + [
                pl.BlockSpec((pieces, width, seg), lambda i, m: (0, 0, i)),
                pl.BlockSpec((1, pieces, seg, 128), lambda i, m: (i, 0, 0, 0)),
            ],
            scratch_shapes=[pltpu.VMEM((model, 3 * width), BF16), pltpu.VMEM((8, 3 * width), F32)],
        ),
        compiler_params=params(),
        cost_estimate=cost(9 * seqs),
        name="attend",
    )(meta, *hidden, *qkv_args)


def attend_back_kernel(seq, pieces, earlier, meta, *refs):
    hidden = refs[:pieces]
    (w_ref, grad_in, q_in, k_in, v_in, ctx_in, lse_in) = refs[pieces : pieces + 7]
    before = refs[pieces + 7 : pieces + 7 + earlier]
    if earlier:
        gin_keep, gin_send, block_out, w_all, dq_t, d_all, out_w, out_b = refs[pieces + 7 + earlier :]
    else:
        gin_keep, gin_send, out_w, out_b, w_all, dq_t, d_all = refs[pieces + 7 :]
    width, seg = grad_in.shape[1:]
    heads = width // HD
    model = hidden[0].shape[-1]
    length, place = meta[seq], meta[meta.shape[0] - 1]
    filled = (length + seg - 1) // seg
    w_all[...] = w_ref[...].reshape(model, 3 * width)
    out_w[...] = jnp.zeros(out_w.shape, F32)
    out_b[...] = jnp.zeros(out_b.shape, F32)

    for count in range(1, pieces + 1):

        @pl.when(filled == count)
        def _(count=count):
            rows = count * seg
            queries = q_in[0, 0:count].reshape(rows, width)
            queries_t = queries.T
            upstream_t = jnp.concatenate([grad_in[at] for at in range(count)], axis=1)
            upstream = upstream_t.T
            ctx_t = jnp.concatenate([ctx_in[at] for at in range(count)], axis=1)
            lse_t = jnp.concatenate([lse_in[0, at].T[0:8] for at in range(count)], axis=1)
            product_t = ctx_t.astype(F32) * upstream_t.astype(F32)
            delta_t = [
                jnp.sum(product_t[h * HD : (h + 1) * HD], axis=0, keepdims=True)
                for h in range(heads)
            ]
            dq_t[:, 0:rows] = jnp.zeros((width, rows), F32)

            def block(at, carry):
                keys = k_in[0, at]
                values = v_in[0, at]
                keys_t = keys.T
                row = lax.broadcasted_iota(jnp.int32, (seg, 1), 0) + at * seg
                row_ok = row < length
                dk = jnp.zeros((seg, width), F32)
                dv = jnp.zeros((seg, width), F32)
                for head in range(heads):
                    here = head_lanes(width, head)
                    scores = dot(jnp.where(here, keys, jnp.zeros_like(keys)), queries_t)
                    probs = jnp.exp(scores - lse_t[head : head + 1])
                    probs = jnp.where(row_ok, probs, 0.0)
                    g_probs = dot(jnp.where(here, values, jnp.zeros_like(values)), upstream_t)
                    g_scores = (probs * (g_probs - delta_t[head])).astype(BF16)
                    dv = jnp.where(here, dot(probs.astype(BF16), upstream), dv)
                    dk = jnp.where(here, dot(g_scores, queries), dk)
                    part = slice(head * HD, (head + 1) * HD)
                    dq_t[part, 0:rows] += dot(keys_t[part], g_scores)
                d_all[at, :, width : 2 * width] = dk.astype(BF16)
                d_all[at, :, 2 * width :] = dv.astype(BF16)
                return carry

            lax.fori_loop(0, count, block, 0)
            for at in range(count):
                piece = dq_t[:, at * seg : (at + 1) * seg]
                d_all[at, :, 0:width] = (piece.T * HD**-0.5).astype(BF16)

    for j in range(pieces):
        at = lax.bitwise_xor(place, j)
        gin_out = (gin_send if j % 2 else gin_keep).at[j // 2]

        @pl.when(at < filled)
        def _():
            grads = d_all[at]
            gin_out[...] = dot(grads, w_all[...], NT).astype(BF16)
            out_w[...] += dot(hidden[j][0], grads, TN)
            out_b[0:1] += jnp.sum(grads.astype(F32), axis=0, keepdims=True)

        @pl.when(at >= filled)
        def _():
            gin_out[...] = jnp.zeros((seg, model), BF16)

    if earlier:
        devices, tall, _ = block_out.shape
        total = out_w[...]
        extra = out_b[...] + before[-1][...]
        for w_sum, b_sum in zip(before[:-1:2], before[1:-1:2]):
            total = total + w_sum[...]
            extra = extra + b_sum[...]
        block_out[:, : tall - 8] = total.astype(BF16).reshape(devices, tall - 8, 3 * width)
        block_out[:, tall - 8 :] = jnp.broadcast_to(
            extra.astype(BF16)[None], (devices, 8, 3 * width)
        )


def finish_kernel(block, own_ref, extra_ref, stats_ref):
    share, full = own_ref.shape
    devices, tall, width = block.shape
    part = width // 3
    groups = full // width
    stats = 0.0
    for g in range(groups):
        total = 0.0
        for r in range(devices // groups):
            total = total + block[r * groups + g].astype(F32)
        for p in range(3):
            at = p * groups * part + g * part
            own_ref[:, at : at + part] = total[:share, p * part : (p + 1) * part]
            extra_ref[:, at : at + part] = total[share:, p * part : (p + 1) * part]
        stats = stats + total[share:]
    stats_ref[...] = stats


def finish(block, share, full):
    devices, tall, width = block.shape
    return pl.pallas_call(
        finish_kernel,
        out_shape=[
            jax.ShapeDtypeStruct(s, F32) for s in ((share, full), (8, full), (8, width))
        ],
        compiler_params=params(),
        name="finish",
    )(block)


def attend_back(seq, index, meta, hidden, w_spec, w_arg, grad_ctx, saved, before=(), tall=0):
    pieces = len(hidden)
    _, seg, model = hidden[0].shape
    width = model // pieces
    saved_spec = at_block((1, pieces, seg, width), index, 0, 0, 0)
    gin = (pieces // 2, seg, model)
    sums = [((model, 3 * width), F32), ((8, 3 * width), F32)]
    blocks = [((model // max(tall - 8, 1), tall, 3 * width), BF16)]
    outs = [(gin, BF16)] * 2 + (blocks if before else sums)
    return pl.pallas_call(
        functools.partial(attend_back_kernel, seq, pieces, len(before)),
        out_shape=[jax.ShapeDtypeStruct(*o) for o in outs],
        grid_spec=pltpu.PrefetchScalarGridSpec(
            num_scalar_prefetch=1,
            grid=(1,),
            in_specs=[at_block((1, seg, model), seq, 0, 0)] * pieces
            + [w_spec, at_block((pieces, width, seg), 0, 0, seq)]
            + [saved_spec] * 3
            + [
                at_block((pieces, width, seg), 0, 0, index),
                at_block((1, pieces, seg, 128), index, 0, 0, 0),
            ]
            + [fixed(a.shape) for a in before],
            out_specs=[fixed(o[0]) for o in outs],
            scratch_shapes=[
                pltpu.VMEM((model, 3 * width), BF16),
                pltpu.VMEM((width, pieces * seg), F32),
                pltpu.VMEM((pieces, seg, 3 * width), BF16),
            ]
            + [pltpu.VMEM(*o) for o in (sums if before else [])],
        ),
        compiler_params=params(),
        cost_estimate=cost(13),
        name="attend_back",
    )(meta, *hidden, w_arg, grad_ctx, *saved, *before)


def normal_parts(v):
    size = jnp.abs(v) * (0.5**0.5)
    t = 1.0 / (1.0 + 0.3275911 * size)
    poly = t * (
        0.254829592
        + t * (-0.284496736 + t * (1.421413741 + t * (-1.453152027 + t * 1.061405429)))
    )
    bell = jnp.exp(-0.5 * v * v)
    upper = 0.5 * poly * bell
    cdf = jnp.where(v < 0, upper, 1.0 - upper)
    return cdf, bell * (0.5 / jnp.pi) ** 0.5


def normalise(values):
    center = values - jnp.mean(values, axis=-1, keepdims=True)
    root = lax.rsqrt(jnp.mean(center * center, axis=-1, keepdims=True) + NORM_EPS)
    return center * root, root


def normalise_back(grad, unit, root):
    mean_grad = jnp.mean(grad, axis=-1, keepdims=True)
    mean_prod = jnp.mean(grad * unit, axis=-1, keepdims=True)
    return root * (grad - mean_grad - unit * mean_prod)


ROWS = 32


def row_loop(start, stop, fn):
    def step(i, carry):
        fn(pl.ds(pl.multiple_of(start + i * ROWS, ROWS), ROWS), start + i * ROWS)
        return carry

    lax.fori_loop(0, (stop - start) // ROWS, step, 0, unroll=2)


def fold(values):
    return jnp.sum(values.reshape(-1, 8, values.shape[-1]), axis=0)


def mask_rows(meta, base, seg):
    seq = base // seg
    position = lax.broadcasted_iota(jnp.int32, (ROWS, 1), 0) + (base - seq * seg)
    return (position + meta[meta.shape[0] - 1] * seg < meta[seq]).astype(F32)


def tokens(ref, base):
    seg = ref.shape[1]
    seq = base // seg
    return ref[seq, pl.ds(pl.multiple_of(base - seq * seg, ROWS), ROWS)].astype(F32)


def over_rows(ref, k):
    return jnp.sum(ref[k], axis=0, keepdims=True)


def onward_kernel(groups, meta, *refs):
    ctxs = refs[:groups]
    (x_ref, cot_ref, wout_ref, win_ref, wdown_ref, small_a, small_b) = refs[groups : groups + 7]
    (
        out_ref,
        act_ref,
        slope_ref,
        gsecond_ref,
        low_ref,
        gres_ref,
        unit,
        root,
        vecs,
        stats_ref,
        sums_ref,
        normed,
        acc,
        inner,
        acc_sums,
    ) = refs[groups + 7 :]
    step = pl.program_id(0)
    seqs, seg, model = x_ref.shape
    rows = seqs * seg

    @pl.when(step == 0)
    def _():
        vecs[0:8] = jnp.sum(small_a[...].astype(F32), axis=0)
        vecs[8:16] = jnp.sum(small_b[...].astype(F32), axis=0)
        acc_sums[...] = jnp.zeros(acc_sums.shape, F32)
        wout = wout_ref[...].reshape(model, model)
        done = 0
        for ref in ctxs:
            parts, width, many = ref.shape
            context = ref[...].reshape(parts * width, many)
            acc[done : done + many] = dot(context, wout, TN) + vecs[0:1]
            done += many

        def first_norm(at, base):
            mask = mask_rows(meta, base, seg)
            x = tokens(x_ref, base)
            branch = acc[at]
            n1, r1 = normalise(x + branch)
            value = n1 * vecs[1:2] + vecs[2:3]
            unit[at] = n1
            root[at] = jnp.broadcast_to(r1, (ROWS, root.shape[-1]))
            normed[at] = value
            low_ref[at] = value.astype(BF16)
            acc_sums[0] += fold(x * x * mask)
            acc_sums[1] += fold(branch * branch * mask)

        row_loop(0, rows, first_norm)
        acc[...] = jnp.broadcast_to(vecs[3:4], acc.shape)

    win = win_ref[...].reshape(model, model)
    wdown = wdown_ref[...].reshape(model, model)
    bin_row = vecs[pl.ds(6 + step, 1)]
    for b in range(seqs):
        lo, hi = b * seg, (b + 1) * seg
        inner[lo:hi] = dot(low_ref[lo:hi], win)

        def activate(at, base):
            value = inner[at] + bin_row
            cdf, pdf = normal_parts(value)
            act_ref[0, at] = (value * cdf).astype(BF16)
            slope_ref[0, at] = cdf + value * pdf

        row_loop(lo, hi, activate)
        acc[lo:hi] += dot(act_ref[0, lo:hi], wdown)

    @pl.when(step == pl.num_programs(0) - 1)
    def _():
        def second_norm(at, base):
            mask = mask_rows(meta, base, seg)
            second = acc[at]
            n2, r2 = normalise(normed[at] + second)
            output = n2 * vecs[5:6] + vecs[15:16]
            out_ref[at] = (output * mask).astype(BF16)
            g_out = tokens(cot_ref, base) * mask
            g_resid = normalise_back(g_out * vecs[5:6], n2, r2)
            low = g_resid.astype(BF16)
            gsecond_ref[at] = low
            gres_ref[at] = g_resid
            acc_sums[2] += fold(second * second * mask)
            acc_sums[3] += fold(output * output * mask)
            acc_sums[4] += fold(low.astype(F32))
            acc_sums[5] += fold(g_out * n2)
            acc_sums[6] += fold(g_out)

        row_loop(0, rows, second_norm)
        for row in range(8):
            stats_ref[row : row + 1] = over_rows(acc_sums, row)
        sums_ref[...] = jnp.zeros(sums_ref.shape, F32)
        for row in range(3):
            sums_ref[row : row + 1] = over_rows(acc_sums, 4 + row)


def onward(meta, ctxs, x, cot, specs, args, ratio):
    seqs, seg, model = x.shape
    rows = seqs * seg
    flat = (rows, model)
    chunked = (ratio, rows, model)
    outs = [(flat, BF16), (chunked, BF16), (chunked, F32), (flat, BF16), (flat, BF16)]
    outs += [(flat, F32), (flat, F32), ((rows, 128), F32), ((16, model), F32)]
    outs += [((8, model), F32)] * 2
    by_chunk = pl.BlockSpec((1, rows, model), lambda i, m: (i, 0, 0))
    return pl.pallas_call(
        functools.partial(onward_kernel, len(ctxs)),
        out_shape=[jax.ShapeDtypeStruct(*o) for o in outs],
        grid_spec=pltpu.PrefetchScalarGridSpec(
            num_scalar_prefetch=1,
            grid=(ratio,),
            in_specs=[fixed(c.shape) for c in ctxs] + [fixed(x.shape), fixed(cot.shape)] + specs,
            out_specs=[by_chunk if o[0] == chunked else fixed(o[0]) for o in outs],
            scratch_shapes=[
                pltpu.VMEM(flat, F32),
                pltpu.VMEM(flat, F32),
                pltpu.VMEM(flat, F32),
                pltpu.VMEM((8, 8, model), F32),
            ],
        ),
        compiler_params=params(),
        cost_estimate=cost(28),
        name="onward",
    )(meta, *ctxs, x, cot, *args)


def back_kernel(
    slope_ref,
    gsecond_ref,
    start_ref,
    unit,
    root,
    vecs,
    wout_ref,
    win_ref,
    wdown_ref,
    gres_ref,
    gctx_ref,
    ginner_ref,
    gbranch_ref,
    sums_ref,
    acc,
    inner,
    acc_sums,
):
    step = pl.program_id(0)
    rows, model = acc.shape
    many = rows // 3 if rows % 3 == 0 else rows

    @pl.when(step == 0)
    def _():
        acc[...] = start_ref[...]
        sums_ref[...] = jnp.zeros(sums_ref.shape, F32)

    win = win_ref[...].reshape(model, model)
    wdown = wdown_ref[...].reshape(model, model)
    acc_sums[...] = jnp.zeros(acc_sums.shape, F32)
    for lo in range(0, rows, many):
        hi = lo + many
        inner[lo:hi] = dot(gsecond_ref[lo:hi], wdown, NT)

        def through(at, base):
            low = (inner[at] * slope_ref[0, at]).astype(BF16)
            ginner_ref[0, at] = low
            acc_sums[0] += fold(low.astype(F32))

        row_loop(lo, hi, through)
        acc[lo:hi] += dot(ginner_ref[0, lo:hi], win, NT)
    sums_ref[pl.ds(6 + step, 1)] = over_rows(acc_sums, 0)

    @pl.when(step == pl.num_programs(0) - 1)
    def _():
        acc_sums[0] = jnp.zeros(acc_sums.shape[1:], F32)

        def first_back(at, base):
            grad = acc[at]
            n1 = unit[at]
            g_resid = normalise_back(grad * vecs[1:2], n1, root[at][:, 0:1])
            low = g_resid.astype(BF16)
            gres_ref[at] = g_resid
            gbranch_ref[at] = low
            acc_sums[0] += fold(low.astype(F32))
            acc_sums[1] += fold(grad * n1)
            acc_sums[2] += fold(grad)

        row_loop(0, rows, first_back)
        wout = wout_ref[...].reshape(model, model)
        piece = dot(wout, gbranch_ref[...], NT).astype(BF16)
        gctx_ref[...] = piece.reshape(gctx_ref.shape)
        for row in range(3):
            sums_ref[row : row + 1] = over_rows(acc_sums, row)


def back(slopes, g_second, start, unit, root, vecs, specs, args, parts):
    ratio, rows, model = slopes.shape
    flat = (rows, model)
    chunked = (ratio, rows, model)
    outs = [(flat, F32), ((parts, model // parts, rows), BF16), (chunked, BF16)]
    outs += [(flat, BF16), ((16, model), F32)]
    by_chunk = pl.BlockSpec((1, rows, model), lambda i: (i, 0, 0))
    whole = lambda shape: pl.BlockSpec(shape, lambda i: (0,) * len(shape))
    specs = [pl.BlockSpec(x.block_shape, functools.partial(drop_last, x.index_map)) for x in specs]
    return pl.pallas_call(
        back_kernel,
        out_shape=[jax.ShapeDtypeStruct(*o) for o in outs],
        grid=(ratio,),
        in_specs=[by_chunk]
        + [whole(a.shape) for a in (g_second, start, unit, root, vecs)]
        + specs[:3],
        out_specs=[by_chunk if o[0] == chunked else whole(o[0]) for o in outs],
        scratch_shapes=[
            pltpu.VMEM(flat, F32),
            pltpu.VMEM(flat, F32),
            pltpu.VMEM((3, 8, model), F32),
        ],
        compiler_params=params(),
        cost_estimate=cost(22),
        name="back",
    )(slopes, g_second, start, unit, root, vecs, *args[:3])


def drop_last(index_map, i):
    return index_map(i, None)


def spread(grad, keep, send, me, order):
    many = keep.shape[0]
    for n in range(many):
        slot = 0
        for i, bit in enumerate(order):
            slot |= ((n >> (len(order) - 1 - i)) & 1) << bit
        keep[n] = grad[lax.bitwise_xor(me, slot)]
        send[n] = grad[lax.bitwise_xor(me, slot + 1)]


Y_BIT, X_BIT, NEAR_Z_BIT, FAR_Z_BIT = 1, 2, 3, 4


def down_kernel(act_ref, g_ref, out_ref):
    grad = dot(act_ref[0], g_ref[...], TN).astype(BF16)
    out_ref[...] = grad.reshape(out_ref.shape)


def down_grads(acts, g_second, each):
    ratio, rows, model = acts.shape
    return pl.pallas_call(
        down_kernel,
        out_shape=jax.ShapeDtypeStruct((ratio * model // each, each, model), BF16),
        grid=(ratio,),
        in_specs=[
            pl.BlockSpec((1, rows, model), lambda i: (i, 0, 0)),
            pl.BlockSpec((rows, model), lambda i: (0, 0)),
        ],
        out_specs=pl.BlockSpec((model // each, each, model), lambda i: (i, 0, 0)),
        compiler_params=params(),
        cost_estimate=cost(8),
        name="down_grads",
    )(acts, g_second)


def rest_kernel(ratio, groups, cut, meta, low_ref, ginner_ref, *refs):
    ctxs = refs[:groups]
    gbranch_ref, sums_one, sums_two = refs[groups : groups + 3]
    outs = refs[groups + 3 : groups + 7]
    grad = refs[groups + 7]
    me = meta[meta.shape[0] - 2]
    step = pl.program_id(0)
    devices, each, model = grad.shape

    @pl.when(step < ratio)
    def _():
        grad[...] = dot(low_ref[...], ginner_ref[0], TN).astype(BF16).reshape(grad.shape)

    @pl.when(step == ratio)
    def _():
        total = 0.0
        done = 0
        for ref in ctxs:
            parts, width, many = ref.shape
            context = ref[...].reshape(parts * width, many)
            total = total + dot(context, gbranch_ref[done : done + many])
            done += many
        grad[...] = total.astype(BF16).reshape(grad.shape)

    @pl.when(step == ratio + 1)
    def _():
        block = jnp.concatenate(
            [sums_one[...], sums_two[...], jnp.zeros((each - 24, model), F32)]
            if each > 24
            else [sums_one[...], sums_two[...]],
            axis=0,
        )
        grad[...] = jnp.broadcast_to(block.astype(BF16)[None], grad.shape)

    x_first = (X_BIT, Y_BIT, NEAR_Z_BIT, FAR_Z_BIT)
    y_first = (Y_BIT, X_BIT, NEAR_Z_BIT, FAR_Z_BIT)

    @pl.when(step < cut)
    def _():
        spread(grad, outs[0], outs[1], me, x_first)

    @pl.when(step >= cut)
    def _():
        spread(grad, outs[2], outs[3], me, y_first)


def rest_grads(meta, low, g_inner, ctxs, g_branch, sums_one, sums_two, devices, each):
    ratio, rows, model = g_inner.shape
    cut = (ratio + 2) // 2
    half = devices // 2
    shapes = [jax.ShapeDtypeStruct((half, n * each, model), BF16) for n in (cut, ratio + 2 - cut)]
    specs = [
        pl.BlockSpec((half, each, model), lambda i, m: (0, jnp.minimum(i, cut - 1), 0)),
        pl.BlockSpec((half, each, model), lambda i, m: (0, jnp.maximum(i - cut, 0), 0)),
    ]
    return pl.pallas_call(
        functools.partial(rest_kernel, ratio, len(ctxs), cut),
        out_shape=(shapes[0], shapes[0], shapes[1], shapes[1]),
        grid_spec=pltpu.PrefetchScalarGridSpec(
            num_scalar_prefetch=1,
            grid=(ratio + 2,),
            in_specs=[
                fixed(low.shape),
                pl.BlockSpec((1, rows, model), lambda i, m: (jnp.minimum(i, ratio - 1), 0, 0)),
            ]
            + [fixed(c.shape) for c in ctxs]
            + [fixed(g_branch.shape), fixed(sums_one.shape), fixed(sums_two.shape)],
            out_specs=[specs[0], specs[0], specs[1], specs[1]],
            scratch_shapes=[pltpu.VMEM((devices, each, model), BF16)],
        ),
        compiler_params=params(),
        cost_estimate=cost(10),
        name="rest_grads",
    )(meta, low, g_inner, *ctxs, g_branch, sums_one, sums_two)


def natural_grads(acts, g_second, low, g_inner, ctxs, g_branch, sums, devices, share):
    ratio, rows, model = acts.shape
    down = jnp.concatenate([dot(a, g_second, TN) for a in acts]).reshape(devices, -1, model)
    context = jnp.concatenate(ctxs, axis=2).reshape(model, rows)
    rest = [dot(low, g, TN) for g in g_inner] + [dot(context, g_branch)]
    rest = [r.reshape(devices, share, model) for r in rest]
    rest.append(jnp.broadcast_to(sums[None], (devices,) + sums.shape))
    return down.astype(BF16), jnp.concatenate(rest, axis=1).astype(BF16)


def pair(kept, sent):
    return (kept.astype(F32) + sent.astype(F32)).astype(BF16)


def halves(kept, got):
    half = kept.shape[0] // 2
    return pair(kept[half:], got[half:]), pair(kept[:half], got[:half])


def body(
    hidden_in,
    lengths,
    w_qkv,
    b_query,
    b_value,
    w_out,
    b_out,
    gain_one,
    bias_one,
    w_in,
    b_in,
    w_down,
    b_down,
    gain_two,
    bias_two,
    cotangent,
):
    seqs, seg, model = hidden_in.shape
    sizes = tuple(lax.axis_size(a) for a in ALL_AXES)
    far, wide, near_y, cores = sizes
    groups = near_y * cores
    devices = far * wide * groups
    place = lax.axis_index(ROW_AXES)
    me = lax.axis_index(ALL_AXES)
    share = model // devices
    ff = w_in.shape[1]
    ff_share = ff // devices
    ratio = ff // model
    width = model // groups
    aligned = share % 8 == 0 and devices == 8 * ratio and far == ratio
    meta = jnp.concatenate([lengths, me[None], place[None]]).astype(jnp.int32)

    first = me * share
    owner = first // width
    within = first - owner * width
    cut = w_qkv.reshape(share, 3, groups, width).transpose(2, 0, 1, 3)
    cut = cut.reshape(groups, share, 3 * width)
    extra = jnp.zeros((1, 8, 3 * width), BF16)
    extra = lax.dynamic_update_slice(extra, b_query[None, None], (0, 0, within))
    extra = lax.dynamic_update_slice(extra, b_value[None, None], (0, 0, 2 * width + within))
    mine = lax.broadcasted_iota(jnp.int32, (groups, 1, 1), 0) == owner
    extra = jnp.where(mine, extra, jnp.zeros_like(extra))
    packed = jnp.concatenate([cut, extra], axis=1)
    tall = share + 8
    packed = jnp.broadcast_to(packed[None], (far * wide,) + packed.shape)
    qkv = exchange(packed.reshape(devices, tall, 3 * width), ALL_AXES)
    if aligned:
        qkv_specs = [
            at_block((devices, share, 3 * width), 0, 0, 0),
            at_block((devices, 8, 3 * width), 0, share // 8, 0),
        ]
        qkv_args = [qkv, qkv]
    else:
        qkv_args = [qkv[:, :share].reshape(model, 3 * width), qkv[:, share:]]
        qkv_specs = [fixed(a.shape) for a in qkv_args]

    hidden = gather_rows(hidden_in)

    small = jnp.zeros((16, model), BF16)
    vectors = jnp.stack([b_out, gain_one, bias_one, b_down, b_down, gain_two])
    small = lax.dynamic_update_slice(small, vectors, (0, first))
    small = lax.dynamic_update_slice(small, bias_two[None], (15, first))
    ff_first = me * ff_share
    ff_row = ff_first // model
    small = lax.dynamic_update_slice(small, b_in[None], (6 + ff_row, ff_first - ff_row * model))
    bundle = jnp.concatenate(
        [
            w_in.reshape(share, ratio, model).transpose(1, 0, 2).reshape(-1, model),
            w_down,
            w_out,
            small,
        ]
    )
    bundle = lax.all_gather(bundle, ALL_AXES, axis=0, tiled=False)
    at = ratio * share
    if aligned:
        weight_specs = [
            at_block((devices, share, model), 0, (at + ff_share) // share, 0),
            pl.BlockSpec((devices, share, model), lambda i, m: (0, i, 0)),
            pl.BlockSpec((devices // ratio, ff_share, model), lambda i, m: (i, 1, 0)),
            at_block((devices, 8, model), 0, (at + ff_share + share) // 8, 0),
            at_block((devices, 8, model), 0, (at + ff_share + share) // 8 + 1, 0),
        ]
        weight_args = [bundle] * 5
    else:
        win = bundle[:, :at].reshape(devices, ratio, share, model).transpose(1, 0, 2, 3)
        small = bundle[:, at + ff_share + share :]
        weight_args = [
            bundle[:, at + ff_share : at + ff_share + share].reshape(model, model),
            win.reshape(ratio, model, model),
            bundle[:, at : at + ff_share].reshape(ratio, model, model),
            small[:, :8],
            small[:, 8:],
        ]
        by_chunk = pl.BlockSpec((1, model, model), lambda i, m: (i, 0, 0))
        weight_specs = [fixed(a.shape) for a in weight_args]
        weight_specs[1] = weight_specs[2] = by_chunk

    spans = [(0, seqs - 1), (seqs - 1, 1)]
    saved = []
    ctxs = []
    for start, count in spans:
        q, k, v, ctx, lse = attend(start, count, meta, hidden, qkv_specs, qkv_args)
        saved.append((q, k, v, ctx, lse))
        ctxs.append(exchange(ctx, ROW_AXES))

    (out, acts, slopes, g_second, low, start, unit, root, vecs, stats, sums_two) = onward(
        meta, ctxs, hidden_in, cotangent, weight_specs, weight_args, ratio
    )
    layer_out = out.reshape(seqs, seg, model)
    if aligned:
        down = down_grads(acts, g_second, ff_share)
        start = after(start, down)
        down = lax.psum_scatter(down, ALL_AXES, scatter_dimension=0, tiled=False)
    g_resid, g_ctx, g_inner, g_branch, sums_one = back(
        slopes, g_second, start, unit, root, vecs, weight_specs, weight_args, groups
    )
    g_ctx = exchange(g_ctx, ROW_AXES)
    if aligned:
        keep_a, send_a, keep_b, send_b = rest_grads(
            meta, low, g_inner, ctxs, g_branch, sums_one, sums_two, devices, share
        )
        got_a, got_b = swap(send_a, "c"), swap(send_b, "c")
    else:
        sums = jnp.concatenate([sums_one, sums_two])
        down, rest = natural_grads(
            acts, g_second, low, g_inner, ctxs, g_branch, sums, devices, share
        )
        down = lax.psum_scatter(down, ALL_AXES, scatter_dimension=0, tiled=False)
        rest = lax.psum_scatter(rest, ALL_AXES, scatter_dimension=0, tiled=False)

    squares = jnp.sum(stats[:4], axis=1)
    valid = jnp.sum(jnp.clip(lengths - place * seg, 0, seg)).astype(F32)
    exact = jnp.concatenate([squares, valid[None]])
    terms = []
    for _ in range(3):
        terms.append(lax.reduce_precision(exact, 8, 7))
        exact = exact - terms[-1]
    stat_rows = jnp.pad(jnp.concatenate(terms)[None], ((1, 6), (0, 3 * width - 15)))

    homes = [(span, i) for span, (_, count) in enumerate(spans) for i in range(count)]
    w_sums = []
    partials = []
    inputs = [None] * seqs
    over = [None] * seqs

    def settle(b):
        kept, near = partials[b]
        here = kept[0].astype(F32) + near[0].astype(F32)
        inputs[b] = g_resid[b * seg : (b + 1) * seg] + here
        over[b] = pair(kept[1], near[1])

    for b, (span, index) in enumerate(homes):
        if b == 1 and aligned:
            go_a, keep_a = halves(keep_a, after(got_a, gin_send))
            go_b, keep_b = halves(keep_b, after(got_b, gin_send))
            g_ctx = after(g_ctx, go_a, go_b)
            got_a, got_b = swap(go_a, "x"), swap(go_b, "y")
        if b == seqs - 1 and aligned:
            go_a, keep_a = halves(keep_a, after(got_a, gin_send))
            go_b, keep_b = halves(keep_b, after(got_b, gin_send))
            g_ctx = after(g_ctx, go_a, go_b)
            got_a, got_b = swap(go_a, "y"), swap(go_b, "x")
        before = ()
        if b == seqs - 1 and aligned:
            before = [w for w_sum in w_sums for w in w_sum] + [stat_rows]
        gin_keep, gin_send, *w_sum = attend_back(
            b, index, meta, hidden, qkv_specs[0], qkv_args[0], g_ctx, saved[span], before, tall
        )
        block = w_sum[0]
        w_sums.append(w_sum)
        partials.append((gin_keep, swap(gin_send, "c")))
        if b:
            partials[b - 1] = after(partials[b - 1], gin_send)
            settle(b - 1)
    settle(seqs - 1)
    inputs = [mine + swap(far_part, "y").astype(F32) for mine, far_part in zip(inputs, over)]
    grad_input = jnp.stack(inputs)
    if aligned:
        rest = jnp.concatenate([keep_a, keep_b], axis=1)
        got_a, got_b, block = lax.optimization_barrier((got_a, got_b, block))
        got = jnp.concatenate([got_a, got_b], axis=1)
        go, rest = halves(rest, got)
        got = swap(go, "z", 1)
        go, rest = halves(rest, got)
        rest = pair(rest, swap(after(go, over[-1], down), "z", 2))
    rest = rest.astype(F32)
    down = down.astype(F32)

    if aligned:
        own_wqkv, extra, stats = finish(exchange(block, ALL_AXES), share, 3 * model)
    else:
        block = jnp.concatenate(
            [
                sum(w for w, _ in w_sums).astype(BF16).reshape(devices, share, 3 * width),
                jnp.broadcast_to(
                    (sum(w for _, w in w_sums) + stat_rows).astype(BF16)[None],
                    (devices, 8, 3 * width),
                ),
            ],
            axis=1,
        )
        block = exchange(block, ALL_AXES).astype(F32)
        totals = jnp.sum(block.reshape(far * wide, groups, tall, 3, width), axis=0)
        totals = totals.transpose(1, 2, 0, 3).reshape(tall, 3 * model)
        own_wqkv, extra = totals[:share], totals[share:]
        stats = jnp.sum(block[:, share:], axis=0)
    own_bq = lax.dynamic_slice(extra, (0, first), (1, share))[0]
    own_bv = lax.dynamic_slice(extra, (0, 2 * model + first), (1, share))[0]
    stats = stats[1, :5] + stats[1, 5:10] + stats[1, 10:15]
    stat_rms = jnp.sqrt(stats[:4] / (stats[4] * model))

    rest = rest.reshape(-1, model)
    own_win = rest[: ratio * share].reshape(ratio, share, model).transpose(1, 0, 2)
    own_win = own_win.reshape(share, ff)
    at = ratio * share
    own_wout = rest[at : at + share]
    at += share
    vectors = lax.dynamic_slice(rest, (at, first), (3, share))
    vectors_two = lax.dynamic_slice(rest, (at + 16, first), (3, share))
    own_bin = lax.dynamic_slice(rest, (at + 6 + ff_row, ff_first - ff_row * model), (1, ff_share))
    return (
        layer_out,
        grad_input,
        own_wqkv,
        own_bq,
        own_bv,
        own_wout,
        vectors[0],
        vectors[1],
        vectors[2],
        own_win,
        own_bin[0],
        down.reshape(ff_share, model),
        vectors_two[0],
        vectors_two[1],
        vectors_two[2],
        stat_rms,
    )


def solution(mesh):
    dp, seq = mesh.shape["dp"], mesh.shape["seq"]
    finer = Mesh(mesh.devices.reshape(dp // 2, 2, seq // 2, 2), ALL_AXES)
    token = P(BATCH_AXES, ROW_AXES, None)
    matrix = P(ALL_AXES, None)
    vector = P(ALL_AXES)
    placed = (
        (token, P(BATCH_AXES), matrix, vector, vector, matrix, vector, vector, vector)
        + (matrix, vector, matrix, vector, vector, vector, token)
    )
    results = (
        (token, token, matrix, vector, vector, matrix, vector, vector, vector)
        + (matrix, vector, matrix, vector, vector, vector, P())
    )
    return jax.shard_map(
        body, mesh=finer, in_specs=placed, out_specs=results, check_vma=False
    )
```

```python
import functools
import math

import jax
import jax.numpy as jnp
from jax import lax
from jax.experimental import pallas as pl
from jax.experimental.pallas import tpu as pltpu
from jax.sharding import Mesh
from jax.sharding import PartitionSpec as P

HD = 64
NORM_EPS = 1e-12
BATCH_AXES = ("z", "x")
ROW_AXES = ("y", "c")
ALL_AXES = BATCH_AXES + ROW_AXES
F32 = jnp.float32
BF16 = jnp.bfloat16
VMEM_LIMIT = 56 * 1024 * 1024


def dot(left, right, dims=((1,), (0,))):
    return lax.dot_general(left, right, (dims, ((), ())), preferred_element_type=F32)


NT = ((1,), (1,))
TN = ((0,), (0,))


def params():
    return pltpu.CompilerParams(vmem_limit_bytes=VMEM_LIMIT)


def cost(micros):
    return pl.CostEstimate(flops=int(micros * 1e9), transcendentals=0, bytes_accessed=0)


def after(value, *others):
    return lax.optimization_barrier((value,) + others)[0]


def fixed(shape):
    return pl.BlockSpec(shape, lambda i, m: (0,) * len(shape))


def at_block(shape, *index):
    return pl.BlockSpec(shape, lambda i, m: index)


def swap(array, axis, offset=1):
    size = lax.axis_size(axis)
    return lax.ppermute(array, axis, [(i, i ^ offset) for i in range(size)])


def exchange(array, axes):
    return lax.all_to_all(array, axes, split_axis=0, concat_axis=0, tiled=True)


def gather_rows(array):
    far = swap(array, "y")
    near = swap(array, "c")
    return [array, near, far, swap(far, "c")]


def head_lanes(width, head):
    lane = lax.broadcasted_iota(jnp.int32, (1, width), 1)
    return (lane >= head * HD) & (lane < (head + 1) * HD)


def attend_kernel(first, pieces, meta, *refs):
    hidden = refs[:pieces]
    w_ref, b_ref, q_out, k_out, v_out, ctx_out, lse_out, w_all, b_all = refs[pieces:]
    width, seg = ctx_out.shape[1:]
    model = hidden[0].shape[-1]
    heads = width // HD
    length, place = meta[first + pl.program_id(0)], meta[meta.shape[0] - 1]
    filled = (length + seg - 1) // seg

    @pl.when(pl.program_id(0) == 0)
    def _():
        w_all[...] = w_ref[...].reshape(model, 3 * width)
        b_all[...] = jnp.sum(b_ref[...].astype(F32), axis=0)

    for j in range(pieces):
        at = lax.bitwise_xor(place, j)

        @pl.when(at < filled)
        def _():
            qkv = dot(hidden[j][0], w_all[...]) + b_all[0:1]
            q_out[0, at] = qkv[:, :width].astype(BF16) * jnp.asarray(HD**-0.5, BF16)
            k_out[0, at] = qkv[:, width : 2 * width].astype(BF16)
            v_out[0, at] = qkv[:, 2 * width :].astype(BF16)

        @pl.when(at >= filled)
        def _():
            q_out[0, at] = jnp.zeros((seg, width), BF16)
            k_out[0, at] = jnp.zeros((seg, width), BF16)
            v_out[0, at] = jnp.zeros((seg, width), BF16)
            ctx_out[at] = jnp.zeros((width, seg), BF16)
            lse_out[0, at] = jnp.zeros((seg, lse_out.shape[-1]), F32)

    for count in range(1, pieces + 1):

        @pl.when(filled == count)
        def _(count=count):
            keys = k_out[0, 0:count].reshape(count * seg, width)
            values = v_out[0, 0:count].reshape(count * seg, width)
            column = lax.broadcasted_iota(jnp.int32, (1, seg), 1) + (count - 1) * seg
            tail_ok = column < length

            def block(at, carry):
                q = q_out[0, at]
                ctx = jnp.zeros((seg, width), F32)
                lse = jnp.zeros((seg, lse_out.shape[-1]), F32)
                for head in range(heads):
                    here = head_lanes(width, head)
                    scores = dot(jnp.where(here, q, jnp.zeros_like(q)), keys, NT)
                    tail = jnp.where(tail_ok, scores[:, (count - 1) * seg :], -jnp.inf)
                    if count > 1:
                        scores = jnp.concatenate([scores[:, : (count - 1) * seg], tail], axis=1)
                    else:
                        scores = tail
                    top = jnp.max(scores, axis=-1, keepdims=True)
                    weights = jnp.exp(scores - top)
                    total = jnp.sum(weights, axis=-1, keepdims=True)
                    probs = (weights * (1.0 / total)).astype(BF16)
                    ctx = jnp.where(here, dot(probs, values), ctx)
                    lane = lax.broadcasted_iota(jnp.int32, lse.shape, 1)
                    lse = jnp.where(lane == head, top + jnp.log(total), lse)
                ctx_out[at] = ctx.T.astype(BF16)
                lse_out[0, at] = lse
                return carry

            lax.fori_loop(0, count, block, 0)


def attend(first, seqs, meta, hidden, qkv_specs, qkv_args):
    pieces = len(hidden)
    _, seg, model = hidden[0].shape
    width = model // pieces
    saved = jax.ShapeDtypeStruct((seqs, pieces, seg, width), BF16)
    saved_spec = pl.BlockSpec((1, pieces, seg, width), lambda i, m: (i, 0, 0, 0))
    return pl.pallas_call(
        functools.partial(attend_kernel, first, pieces),
        out_shape=(saved,) * 3
        + (
            jax.ShapeDtypeStruct((pieces, width, seqs * seg), BF16),
            jax.ShapeDtypeStruct((seqs, pieces, seg, 128), F32),
        ),
        grid_spec=pltpu.PrefetchScalarGridSpec(
            num_scalar_prefetch=1,
            grid=(seqs,),
            in_specs=[pl.BlockSpec((1, seg, model), lambda i, m: (first + i, 0, 0))] * pieces
            + qkv_specs,
            out_specs=[saved_spec] * 3
            + [
                pl.BlockSpec((pieces, width, seg), lambda i, m: (0, 0, i)),
                pl.BlockSpec((1, pieces, seg, 128), lambda i, m: (i, 0, 0, 0)),
            ],
            scratch_shapes=[pltpu.VMEM((model, 3 * width), BF16), pltpu.VMEM((8, 3 * width), F32)],
        ),
        compiler_params=params(),
        cost_estimate=cost(9 * seqs),
        name="attend",
    )(meta, *hidden, *qkv_args)


def attend_back_kernel(seq, pieces, earlier, meta, *refs):
    hidden = refs[:pieces]
    (w_ref, grad_in, q_in, k_in, v_in, ctx_in, lse_in) = refs[pieces : pieces + 7]
    before = refs[pieces + 7 : pieces + 7 + earlier]
    if earlier:
        gin_keep, gin_send, block_out, w_all, dq_t, d_all, out_w, out_b = refs[pieces + 7 + earlier :]
    else:
        gin_keep, gin_send, out_w, out_b, w_all, dq_t, d_all = refs[pieces + 7 :]
    width, seg = grad_in.shape[1:]
    heads = width // HD
    model = hidden[0].shape[-1]
    length, place = meta[seq], meta[meta.shape[0] - 1]
    filled = (length + seg - 1) // seg
    w_all[...] = w_ref[...].reshape(model, 3 * width)
    out_w[...] = jnp.zeros(out_w.shape, F32)
    out_b[...] = jnp.zeros(out_b.shape, F32)

    for count in range(1, pieces + 1):

        @pl.when(filled == count)
        def _(count=count):
            rows = count * seg
            queries = q_in[0, 0:count].reshape(rows, width)
            queries_t = queries.T
            upstream_t = jnp.concatenate([grad_in[at] for at in range(count)], axis=1)
            upstream = upstream_t.T
            ctx_t = jnp.concatenate([ctx_in[at] for at in range(count)], axis=1)
            lse_t = jnp.concatenate([lse_in[0, at].T[0:8] for at in range(count)], axis=1)
            product_t = ctx_t.astype(F32) * upstream_t.astype(F32)
            delta_t = [
                jnp.sum(product_t[h * HD : (h + 1) * HD], axis=0, keepdims=True)
                for h in range(heads)
            ]
            dq_t[:, 0:rows] = jnp.zeros((width, rows), F32)

            def block(at, carry):
                keys = k_in[0, at]
                values = v_in[0, at]
                keys_t = keys.T
                row = lax.broadcasted_iota(jnp.int32, (seg, 1), 0) + at * seg
                row_ok = row < length
                dk = jnp.zeros((seg, width), F32)
                dv = jnp.zeros((seg, width), F32)
                for head in range(heads):
                    here = head_lanes(width, head)
                    scores = dot(jnp.where(here, keys, jnp.zeros_like(keys)), queries_t)
                    probs = jnp.exp(scores - lse_t[head : head + 1])
                    probs = jnp.where(row_ok, probs, 0.0)
                    g_probs = dot(jnp.where(here, values, jnp.zeros_like(values)), upstream_t)
                    g_scores = (probs * (g_probs - delta_t[head])).astype(BF16)
                    dv = jnp.where(here, dot(probs.astype(BF16), upstream), dv)
                    dk = jnp.where(here, dot(g_scores, queries), dk)
                    part = slice(head * HD, (head + 1) * HD)
                    dq_t[part, 0:rows] += dot(keys_t[part], g_scores)
                d_all[at, :, width : 2 * width] = dk.astype(BF16)
                d_all[at, :, 2 * width :] = dv.astype(BF16)
                return carry

            lax.fori_loop(0, count, block, 0)
            for at in range(count):
                piece = dq_t[:, at * seg : (at + 1) * seg]
                d_all[at, :, 0:width] = (piece.T * HD**-0.5).astype(BF16)

    for j in range(pieces):
        at = lax.bitwise_xor(place, j)
        gin_out = (gin_send if j % 2 else gin_keep).at[j // 2]

        @pl.when(at < filled)
        def _():
            grads = d_all[at]
            gin_out[...] = dot(grads, w_all[...], NT).astype(BF16)
            out_w[...] += dot(hidden[j][0], grads, TN)
            out_b[...] += dot(grads, jnp.ones((seg, out_b.shape[-1]), BF16), TN)

        @pl.when(at >= filled)
        def _():
            gin_out[...] = jnp.zeros((seg, model), BF16)

    if earlier:
        devices, share, full = block_out.shape
        total = out_w[...]
        columns = out_b[...]
        for w_sum, b_sum in zip(before[:-1:2], before[1:-1:2]):
            total = total + w_sum[...]
            columns = columns + b_sum[...]
        block_out[:, :, : 3 * width] = total.astype(BF16).reshape(devices, share, 3 * width)
        spare = full - 3 * width
        side = before[-1][...]
        block_out[:, :, 3 * width :] = jnp.broadcast_to(
            side.astype(BF16)[None], (devices, share, spare)
        )
        lane = lax.broadcasted_iota(jnp.int32, (share, spare), 1)
        owners = width // share
        for k in range(owners):
            query = columns[k * share : (k + 1) * share, :spare]
            value = columns[2 * width + k * share : 2 * width + (k + 1) * share, :spare]
            mine = jnp.where(lane == 0, query, jnp.where(lane == 1, value, side))
            block_out[place * owners + k, :, 3 * width :] = mine.astype(BF16)


def finish_kernel(groups, block, own_ref, extra_ref):
    share, full = own_ref.shape
    devices = block.shape[0]
    part = full // (3 * groups)
    side = 0.0
    for g in range(groups):
        total = 0.0
        for r in range(devices // groups):
            total = total + block[r * groups + g].astype(F32)
        for p in range(3):
            at = p * groups * part + g * part
            own_ref[:, at : at + part] = total[:, p * part : (p + 1) * part]
        side = side + total[:, 3 * part :]
    spare = side.shape[1]
    side = jnp.concatenate([side, jnp.zeros((128 - share, spare), F32)], axis=0)
    side = jnp.concatenate([side, jnp.zeros((128, 128 - spare), F32)], axis=1)
    extra_ref[...] = side.T[: extra_ref.shape[0]]


def finish(block, share, full, groups):
    return pl.pallas_call(
        functools.partial(finish_kernel, groups),
        out_shape=[jax.ShapeDtypeStruct(s, F32) for s in ((share, full), (32, 128))],
        compiler_params=params(),
        name="finish",
    )(block)


def attend_back(seq, index, meta, hidden, w_spec, w_arg, grad_ctx, saved, before=(), share=1):
    pieces = len(hidden)
    _, seg, model = hidden[0].shape
    width = model // pieces
    saved_spec = at_block((1, pieces, seg, width), index, 0, 0, 0)
    gin = (pieces // 2, seg, model)
    sums = [((model, 3 * width), F32), ((3 * width, 128), F32)]
    blocks = [((model // share, share, -(-3 * width // 128) * 128), BF16)]
    outs = [(gin, BF16)] * 2 + (blocks if before else sums)
    return pl.pallas_call(
        functools.partial(attend_back_kernel, seq, pieces, len(before)),
        out_shape=[jax.ShapeDtypeStruct(*o) for o in outs],
        grid_spec=pltpu.PrefetchScalarGridSpec(
            num_scalar_prefetch=1,
            grid=(1,),
            in_specs=[at_block((1, seg, model), seq, 0, 0)] * pieces
            + [w_spec, at_block((pieces, width, seg), 0, 0, seq)]
            + [saved_spec] * 3
            + [
                at_block((pieces, width, seg), 0, 0, index),
                at_block((1, pieces, seg, 128), index, 0, 0, 0),
            ]
            + [fixed(a.shape) for a in before],
            out_specs=[fixed(o[0]) for o in outs],
            scratch_shapes=[
                pltpu.VMEM((model, 3 * width), BF16),
                pltpu.VMEM((width, pieces * seg), F32),
                pltpu.VMEM((pieces, seg, 3 * width), BF16),
            ]
            + [pltpu.VMEM(*o) for o in (sums if before else [])],
        ),
        compiler_params=params(),
        cost_estimate=cost(13),
        name="attend_back",
    )(meta, *hidden, w_arg, grad_ctx, *saved, *before)


def normal_parts(v):
    t = 1.0 / (1.0 + (0.3275911 * 0.5**0.5) * jnp.abs(v))
    poly = t * (
        0.127414796
        + t * (-0.142248368 + t * (0.7107068705 + t * (-0.7265760135 + t * 0.5307027145)))
    )
    bell = jnp.exp2(v * v * (-0.5 / math.log(2.0)))
    upper = poly * bell
    cdf = jnp.where(v < 0, upper, 1.0 - upper)
    return cdf, bell * (0.5 / math.pi) ** 0.5


def normalise(values):
    center = values - jnp.mean(values, axis=-1, keepdims=True)
    root = lax.rsqrt(jnp.mean(center * center, axis=-1, keepdims=True) + NORM_EPS)
    return center * root, root


def normalise_back(grad, unit, root):
    mean_grad = jnp.mean(grad, axis=-1, keepdims=True)
    mean_prod = jnp.mean(grad * unit, axis=-1, keepdims=True)
    return root * (grad - mean_grad - unit * mean_prod)


ROWS = 64


def row_loop(start, stop, fn):
    def step(i, carry):
        fn(pl.ds(pl.multiple_of(start + i * ROWS, ROWS), ROWS), start + i * ROWS)
        return carry

    lax.fori_loop(0, (stop - start) // ROWS, step, 0, unroll=2)


def fold(values):
    return jnp.sum(values.reshape(-1, 8, values.shape[-1]), axis=0)


def mask_rows(meta, base, seg):
    seq = base // seg
    position = lax.broadcasted_iota(jnp.int32, (ROWS, 1), 0) + (base - seq * seg)
    return (position + meta[meta.shape[0] - 1] * seg < meta[seq]).astype(F32)


def tokens(ref, base):
    seg = ref.shape[1]
    seq = base // seg
    return ref[seq, pl.ds(pl.multiple_of(base - seq * seg, ROWS), ROWS)].astype(F32)


def over_rows(ref, k):
    return jnp.sum(ref[k], axis=0, keepdims=True)


def onward_kernel(groups, meta, *refs):
    ctxs = refs[:groups]
    (x_ref, cot_ref, wout_ref, win_ref, wdown_ref, small_a, small_b) = refs[groups : groups + 7]
    (
        out_ref,
        act_ref,
        slope_ref,
        gsecond_ref,
        low_ref,
        gres_ref,
        unit,
        root,
        vecs,
        stats_ref,
        sums_ref,
        normed,
        acc,
        inner,
        acc_sums,
    ) = refs[groups + 7 :]
    step = pl.program_id(0)
    seqs, seg, model = x_ref.shape
    rows = seqs * seg

    @pl.when(step == 0)
    def _():
        vecs[0:8] = jnp.sum(small_a[...].astype(F32), axis=0)
        vecs[8:16] = jnp.sum(small_b[...].astype(F32), axis=0)
        acc_sums[...] = jnp.zeros(acc_sums.shape, F32)
        wout = wout_ref[...].reshape(model, model)
        done = 0
        for ref in ctxs:
            parts, width, many = ref.shape
            context = ref[...].reshape(parts * width, many)
            acc[done : done + many] = dot(context, wout, TN) + vecs[0:1]
            done += many

        def first_norm(at, base):
            mask = mask_rows(meta, base, seg)
            x = tokens(x_ref, base)
            branch = acc[at]
            n1, r1 = normalise(x + branch)
            value = n1 * vecs[1:2] + vecs[2:3]
            unit[at] = n1
            root[at] = jnp.broadcast_to(r1, (ROWS, root.shape[-1]))
            normed[at] = value
            low_ref[at] = value.astype(BF16)
            acc_sums[0] += fold(x * x * mask)
            acc_sums[1] += fold(branch * branch * mask)

        row_loop(0, rows, first_norm)
        acc[...] = jnp.broadcast_to(vecs[3:4], acc.shape)

    win = win_ref[...].reshape(model, model)
    wdown = wdown_ref[...].reshape(model, model)
    bin_row = vecs[pl.ds(6 + step, 1)]
    for b in range(seqs):
        lo, hi = b * seg, (b + 1) * seg
        inner[lo:hi] = dot(low_ref[lo:hi], win)

        def activate(at, base):
            value = inner[at] + bin_row
            cdf, pdf = normal_parts(value)
            act_ref[0, at] = (value * cdf).astype(BF16)
            slope_ref[0, at] = cdf + value * pdf

        row_loop(lo, hi, activate)
        acc[lo:hi] += dot(act_ref[0, lo:hi], wdown)

    @pl.when(step == pl.num_programs(0) - 1)
    def _():
        def second_norm(at, base):
            mask = mask_rows(meta, base, seg)
            second = acc[at]
            n2, r2 = normalise(normed[at] + second)
            output = n2 * vecs[5:6] + vecs[15:16]
            out_ref[at] = (output * mask).astype(BF16)
            g_out = tokens(cot_ref, base) * mask
            g_resid = normalise_back(g_out * vecs[5:6], n2, r2)
            low = g_resid.astype(BF16)
            gsecond_ref[at] = low
            gres_ref[at] = g_resid
            acc_sums[2] += fold(second * second * mask)
            acc_sums[3] += fold(output * output * mask)
            acc_sums[4] += fold(low.astype(F32))
            acc_sums[5] += fold(g_out * n2)
            acc_sums[6] += fold(g_out)

        row_loop(0, rows, second_norm)
        for row in range(8):
            stats_ref[row : row + 1] = over_rows(acc_sums, row)
        sums_ref[...] = jnp.zeros(sums_ref.shape, F32)
        for row in range(3):
            sums_ref[row : row + 1] = over_rows(acc_sums, 4 + row)


def onward(meta, ctxs, x, cot, specs, args, ratio):
    seqs, seg, model = x.shape
    rows = seqs * seg
    flat = (rows, model)
    chunked = (ratio, rows, model)
    outs = [(flat, BF16), (chunked, BF16), (chunked, F32), (flat, BF16), (flat, BF16)]
    outs += [(flat, F32), (flat, F32), ((rows, 128), F32), ((16, model), F32)]
    outs += [((8, model), F32)] * 2
    by_chunk = pl.BlockSpec((1, rows, model), lambda i, m: (i, 0, 0))
    return pl.pallas_call(
        functools.partial(onward_kernel, len(ctxs)),
        out_shape=[jax.ShapeDtypeStruct(*o) for o in outs],
        grid_spec=pltpu.PrefetchScalarGridSpec(
            num_scalar_prefetch=1,
            grid=(ratio,),
            in_specs=[fixed(c.shape) for c in ctxs] + [fixed(x.shape), fixed(cot.shape)] + specs,
            out_specs=[by_chunk if o[0] == chunked else fixed(o[0]) for o in outs],
            scratch_shapes=[
                pltpu.VMEM(flat, F32),
                pltpu.VMEM(flat, F32),
                pltpu.VMEM(flat, F32),
                pltpu.VMEM((8, 8, model), F32),
            ],
        ),
        compiler_params=params(),
        cost_estimate=cost(28),
        name="onward",
    )(meta, *ctxs, x, cot, *args)


def back_kernel(
    slope_ref,
    gsecond_ref,
    start_ref,
    unit,
    root,
    vecs,
    wout_ref,
    win_ref,
    wdown_ref,
    gres_ref,
    gctx_ref,
    ginner_ref,
    gbranch_ref,
    sums_ref,
    acc,
    inner,
    acc_sums,
):
    step = pl.program_id(0)
    rows, model = acc.shape
    many = rows // 3 if rows % 3 == 0 else rows

    @pl.when(step == 0)
    def _():
        acc[...] = start_ref[...]
        sums_ref[...] = jnp.zeros(sums_ref.shape, F32)

    win = win_ref[...].reshape(model, model)
    wdown = wdown_ref[...].reshape(model, model)
    acc_sums[...] = jnp.zeros(acc_sums.shape, F32)
    for lo in range(0, rows, many):
        hi = lo + many
        inner[lo:hi] = dot(gsecond_ref[lo:hi], wdown, NT)

        def through(at, base):
            low = (inner[at] * slope_ref[0, at]).astype(BF16)
            ginner_ref[0, at] = low
            acc_sums[0] += fold(low.astype(F32))

        row_loop(lo, hi, through)
        acc[lo:hi] += dot(ginner_ref[0, lo:hi], win, NT)
    sums_ref[pl.ds(6 + step, 1)] = over_rows(acc_sums, 0)

    @pl.when(step == pl.num_programs(0) - 1)
    def _():
        acc_sums[0] = jnp.zeros(acc_sums.shape[1:], F32)

        def first_back(at, base):
            grad = acc[at]
            n1 = unit[at]
            g_resid = normalise_back(grad * vecs[1:2], n1, root[at][:, 0:1])
            low = g_resid.astype(BF16)
            gres_ref[at] = g_resid
            gbranch_ref[at] = low
            acc_sums[0] += fold(low.astype(F32))
            acc_sums[1] += fold(grad * n1)
            acc_sums[2] += fold(grad)

        row_loop(0, rows, first_back)
        wout = wout_ref[...].reshape(model, model)
        piece = dot(wout, gbranch_ref[...], NT).astype(BF16)
        gctx_ref[...] = piece.reshape(gctx_ref.shape)
        for row in range(3):
            sums_ref[row : row + 1] = over_rows(acc_sums, row)


def back(slopes, g_second, start, unit, root, vecs, specs, args, parts):
    ratio, rows, model = slopes.shape
    flat = (rows, model)
    chunked = (ratio, rows, model)
    outs = [(flat, F32), ((parts, model // parts, rows), BF16), (chunked, BF16)]
    outs += [(flat, BF16), ((16, model), F32)]
    by_chunk = pl.BlockSpec((1, rows, model), lambda i: (i, 0, 0))
    whole = lambda shape: pl.BlockSpec(shape, lambda i: (0,) * len(shape))
    specs = [pl.BlockSpec(x.block_shape, functools.partial(drop_last, x.index_map)) for x in specs]
    return pl.pallas_call(
        back_kernel,
        out_shape=[jax.ShapeDtypeStruct(*o) for o in outs],
        grid=(ratio,),
        in_specs=[by_chunk]
        + [whole(a.shape) for a in (g_second, start, unit, root, vecs)]
        + specs[:3],
        out_specs=[by_chunk if o[0] == chunked else whole(o[0]) for o in outs],
        scratch_shapes=[
            pltpu.VMEM(flat, F32),
            pltpu.VMEM(flat, F32),
            pltpu.VMEM((3, 8, model), F32),
        ],
        compiler_params=params(),
        cost_estimate=cost(22),
        name="back",
    )(slopes, g_second, start, unit, root, vecs, *args[:3])


def drop_last(index_map, i):
    return index_map(i, None)


def spread(grad, keep, send, me, order):
    many = keep.shape[0]
    for n in range(many):
        slot = 0
        for i, bit in enumerate(order):
            slot |= ((n >> (len(order) - 1 - i)) & 1) << bit
        keep[n] = grad[lax.bitwise_xor(me, slot)]
        send[n] = grad[lax.bitwise_xor(me, slot + 1)]


Y_BIT, X_BIT, NEAR_Z_BIT, FAR_Z_BIT = 1, 2, 3, 4


def down_kernel(act_ref, g_ref, out_ref):
    grad = dot(act_ref[0], g_ref[...], TN).astype(BF16)
    out_ref[...] = grad.reshape(out_ref.shape)


def down_grads(acts, g_second, each):
    ratio, rows, model = acts.shape
    return pl.pallas_call(
        down_kernel,
        out_shape=jax.ShapeDtypeStruct((ratio * model // each, each, model), BF16),
        grid=(ratio,),
        in_specs=[
            pl.BlockSpec((1, rows, model), lambda i: (i, 0, 0)),
            pl.BlockSpec((rows, model), lambda i: (0, 0)),
        ],
        out_specs=pl.BlockSpec((model // each, each, model), lambda i: (i, 0, 0)),
        compiler_params=params(),
        cost_estimate=cost(8),
        name="down_grads",
    )(acts, g_second)


def rest_kernel(ratio, groups, cut, meta, low_ref, ginner_ref, *refs):
    ctxs = refs[:groups]
    gbranch_ref, sums_one, sums_two = refs[groups : groups + 3]
    outs = refs[groups + 3 : groups + 7]
    grad = refs[groups + 7]
    me = meta[meta.shape[0] - 2]
    step = pl.program_id(0)
    devices, each, model = grad.shape

    @pl.when(step < ratio)
    def _():
        grad[...] = dot(low_ref[...], ginner_ref[0], TN).astype(BF16).reshape(grad.shape)

    @pl.when(step == ratio)
    def _():
        total = 0.0
        done = 0
        for ref in ctxs:
            parts, width, many = ref.shape
            context = ref[...].reshape(parts * width, many)
            total = total + dot(context, gbranch_ref[done : done + many])
            done += many
        grad[...] = total.astype(BF16).reshape(grad.shape)

    @pl.when(step == ratio + 1)
    def _():
        block = jnp.concatenate(
            [sums_one[...], sums_two[...], jnp.zeros((each - 24, model), F32)]
            if each > 24
            else [sums_one[...], sums_two[...]],
            axis=0,
        )
        grad[...] = jnp.broadcast_to(block.astype(BF16)[None], grad.shape)

    x_first = (X_BIT, Y_BIT, NEAR_Z_BIT, FAR_Z_BIT)
    y_first = (Y_BIT, X_BIT, NEAR_Z_BIT, FAR_Z_BIT)

    @pl.when(step < cut)
    def _():
        spread(grad, outs[0], outs[1], me, x_first)

    @pl.when(step >= cut)
    def _():
        spread(grad, outs[2], outs[3], me, y_first)


def rest_grads(meta, low, g_inner, ctxs, g_branch, sums_one, sums_two, devices, each):
    ratio, rows, model = g_inner.shape
    cut = (ratio + 2) // 2
    half = devices // 2
    shapes = [jax.ShapeDtypeStruct((half, n * each, model), BF16) for n in (cut, ratio + 2 - cut)]
    specs = [
        pl.BlockSpec((half, each, model), lambda i, m: (0, jnp.minimum(i, cut - 1), 0)),
        pl.BlockSpec((half, each, model), lambda i, m: (0, jnp.maximum(i - cut, 0), 0)),
    ]
    return pl.pallas_call(
        functools.partial(rest_kernel, ratio, len(ctxs), cut),
        out_shape=(shapes[0], shapes[0], shapes[1], shapes[1]),
        grid_spec=pltpu.PrefetchScalarGridSpec(
            num_scalar_prefetch=1,
            grid=(ratio + 2,),
            in_specs=[
                fixed(low.shape),
                pl.BlockSpec((1, rows, model), lambda i, m: (jnp.minimum(i, ratio - 1), 0, 0)),
            ]
            + [fixed(c.shape) for c in ctxs]
            + [fixed(g_branch.shape), fixed(sums_one.shape), fixed(sums_two.shape)],
            out_specs=[specs[0], specs[0], specs[1], specs[1]],
            scratch_shapes=[pltpu.VMEM((devices, each, model), BF16)],
        ),
        compiler_params=params(),
        cost_estimate=cost(10),
        name="rest_grads",
    )(meta, low, g_inner, *ctxs, g_branch, sums_one, sums_two)


def natural_grads(acts, g_second, low, g_inner, ctxs, g_branch, sums, devices, share):
    ratio, rows, model = acts.shape
    down = jnp.concatenate([dot(a, g_second, TN) for a in acts]).reshape(devices, -1, model)
    context = jnp.concatenate(ctxs, axis=2).reshape(model, rows)
    rest = [dot(low, g, TN) for g in g_inner] + [dot(context, g_branch)]
    rest = [r.reshape(devices, share, model) for r in rest]
    rest.append(jnp.broadcast_to(sums[None], (devices,) + sums.shape))
    return down.astype(BF16), jnp.concatenate(rest, axis=1).astype(BF16)


def pair(kept, sent):
    return (kept.astype(F32) + sent.astype(F32)).astype(BF16)


def halves(kept, got):
    half = kept.shape[0] // 2
    return pair(kept[half:], got[half:]), pair(kept[:half], got[:half])


def body(
    hidden_in,
    lengths,
    w_qkv,
    b_query,
    b_value,
    w_out,
    b_out,
    gain_one,
    bias_one,
    w_in,
    b_in,
    w_down,
    b_down,
    gain_two,
    bias_two,
    cotangent,
):
    seqs, seg, model = hidden_in.shape
    sizes = tuple(lax.axis_size(a) for a in ALL_AXES)
    far, wide, near_y, cores = sizes
    groups = near_y * cores
    devices = far * wide * groups
    place = lax.axis_index(ROW_AXES)
    me = lax.axis_index(ALL_AXES)
    share = model // devices
    ff = w_in.shape[1]
    ff_share = ff // devices
    ratio = ff // model
    width = model // groups
    aligned = share % 8 == 0 and devices == 8 * ratio and far == ratio
    meta = jnp.concatenate([lengths, me[None], place[None]]).astype(jnp.int32)

    first = me * share
    owner = first // width
    within = first - owner * width
    cut = w_qkv.reshape(share, 3, groups, width).transpose(2, 0, 1, 3)
    cut = cut.reshape(groups, share, 3 * width)
    extra = jnp.zeros((1, 8, 3 * width), BF16)
    extra = lax.dynamic_update_slice(extra, b_query[None, None], (0, 0, within))
    extra = lax.dynamic_update_slice(extra, b_value[None, None], (0, 0, 2 * width + within))
    mine = lax.broadcasted_iota(jnp.int32, (groups, 1, 1), 0) == owner
    extra = jnp.where(mine, extra, jnp.zeros_like(extra))
    packed = jnp.concatenate([cut, extra], axis=1)
    tall = share + 8
    packed = jnp.broadcast_to(packed[None], (far * wide,) + packed.shape)
    qkv = exchange(packed.reshape(devices, tall, 3 * width), ALL_AXES)
    if aligned:
        qkv_specs = [
            at_block((devices, share, 3 * width), 0, 0, 0),
            at_block((devices, 8, 3 * width), 0, share // 8, 0),
        ]
        qkv_args = [qkv, qkv]
    else:
        qkv_args = [qkv[:, :share].reshape(model, 3 * width), qkv[:, share:]]
        qkv_specs = [fixed(a.shape) for a in qkv_args]

    hidden = gather_rows(hidden_in)

    small = jnp.zeros((16, model), BF16)
    vectors = jnp.stack([b_out, gain_one, bias_one, b_down, b_down, gain_two])
    small = lax.dynamic_update_slice(small, vectors, (0, first))
    small = lax.dynamic_update_slice(small, bias_two[None], (15, first))
    ff_first = me * ff_share
    ff_row = ff_first // model
    small = lax.dynamic_update_slice(small, b_in[None], (6 + ff_row, ff_first - ff_row * model))
    bundle = jnp.concatenate(
        [
            w_in.reshape(share, ratio, model).transpose(1, 0, 2).reshape(-1, model),
            w_down,
            w_out,
            small,
        ]
    )
    bundle = lax.all_gather(bundle, ALL_AXES, axis=0, tiled=False)
    at = ratio * share
    if aligned:
        weight_specs = [
            at_block((devices, share, model), 0, (at + ff_share) // share, 0),
            pl.BlockSpec((devices, share, model), lambda i, m: (0, i, 0)),
            pl.BlockSpec((devices // ratio, ff_share, model), lambda i, m: (i, 1, 0)),
            at_block((devices, 8, model), 0, (at + ff_share + share) // 8, 0),
            at_block((devices, 8, model), 0, (at + ff_share + share) // 8 + 1, 0),
        ]
        weight_args = [bundle] * 5
    else:
        win = bundle[:, :at].reshape(devices, ratio, share, model).transpose(1, 0, 2, 3)
        small = bundle[:, at + ff_share + share :]
        weight_args = [
            bundle[:, at + ff_share : at + ff_share + share].reshape(model, model),
            win.reshape(ratio, model, model),
            bundle[:, at : at + ff_share].reshape(ratio, model, model),
            small[:, :8],
            small[:, 8:],
        ]
        by_chunk = pl.BlockSpec((1, model, model), lambda i, m: (i, 0, 0))
        weight_specs = [fixed(a.shape) for a in weight_args]
        weight_specs[1] = weight_specs[2] = by_chunk

    spans = [(0, seqs - 1), (seqs - 1, 1)]
    saved = []
    ctxs = []
    for start, count in spans:
        q, k, v, ctx, lse = attend(start, count, meta, hidden, qkv_specs, qkv_args)
        saved.append((q, k, v, ctx, lse))
        ctxs.append(exchange(ctx, ROW_AXES))

    (out, acts, slopes, g_second, low, start, unit, root, vecs, stats, sums_two) = onward(
        meta, ctxs, hidden_in, cotangent, weight_specs, weight_args, ratio
    )
    layer_out = out.reshape(seqs, seg, model)
    if aligned:
        down = down_grads(acts, g_second, ff_share)
        start = after(start, down)
        down = lax.psum_scatter(down, ALL_AXES, scatter_dimension=0, tiled=False)
    g_resid, g_ctx, g_inner, g_branch, sums_one = back(
        slopes, g_second, start, unit, root, vecs, weight_specs, weight_args, groups
    )
    g_ctx = exchange(g_ctx, ROW_AXES)
    if aligned:
        keep_a, send_a, keep_b, send_b = rest_grads(
            meta, low, g_inner, ctxs, g_branch, sums_one, sums_two, devices, share
        )
        got_a, got_b = swap(send_a, "c"), swap(send_b, "c")
    else:
        sums = jnp.concatenate([sums_one, sums_two])
        down, rest = natural_grads(
            acts, g_second, low, g_inner, ctxs, g_branch, sums, devices, share
        )
        down = lax.psum_scatter(down, ALL_AXES, scatter_dimension=0, tiled=False)
        rest = lax.psum_scatter(rest, ALL_AXES, scatter_dimension=0, tiled=False)

    squares = jnp.sum(stats[:4], axis=1)
    valid = jnp.sum(jnp.clip(lengths - place * seg, 0, seg)).astype(F32)
    exact = jnp.concatenate([squares, valid[None]])
    terms = []
    for _ in range(3):
        terms.append(lax.reduce_precision(exact, 8, 7))
        exact = exact - terms[-1]
    spare = -3 * width % 128
    stat_rows = jnp.pad(jnp.concatenate(terms)[None], ((0, share - 1), (2, spare - 17)))

    homes = [(span, i) for span, (_, count) in enumerate(spans) for i in range(count)]
    w_sums = []
    partials = []
    inputs = [None] * seqs
    over = [None] * seqs

    def settle(b):
        kept, near = partials[b]
        here = kept[0].astype(F32) + near[0].astype(F32)
        inputs[b] = g_resid[b * seg : (b + 1) * seg] + here
        over[b] = pair(kept[1], near[1])

    for b, (span, index) in enumerate(homes):
        if b == 1 and aligned:
            go_a, keep_a = halves(keep_a, after(got_a, gin_send))
            go_b, keep_b = halves(keep_b, after(got_b, gin_send))
            g_ctx = after(g_ctx, go_a, go_b)
            got_a, got_b = swap(go_a, "x"), swap(go_b, "y")
        if b == seqs - 1 and aligned:
            go_a, keep_a = halves(keep_a, after(got_a, gin_send))
            go_b, keep_b = halves(keep_b, after(got_b, gin_send))
            g_ctx = after(g_ctx, go_a, go_b)
            got_a, got_b = swap(go_a, "y"), swap(go_b, "x")
        before = ()
        if b == seqs - 1 and aligned:
            before = [w for w_sum in w_sums for w in w_sum] + [stat_rows]
        gin_keep, gin_send, *w_sum = attend_back(
            b, index, meta, hidden, qkv_specs[0], qkv_args[0], g_ctx, saved[span], before, share
        )
        block = w_sum[0]
        w_sums.append(w_sum)
        partials.append((gin_keep, swap(gin_send, "c")))
        if b:
            partials[b - 1] = after(partials[b - 1], gin_send)
            settle(b - 1)
    settle(seqs - 1)
    inputs = [mine + swap(far_part, "y").astype(F32) for mine, far_part in zip(inputs, over)]
    grad_input = jnp.stack(inputs)
    if aligned:
        rest = jnp.concatenate([keep_a, keep_b], axis=1)
        got_a, got_b, block = lax.optimization_barrier((got_a, got_b, block))
        got = jnp.concatenate([got_a, got_b], axis=1)
        go, rest = halves(rest, got)
        got = swap(after(go, over[-1]), "z", 1)
        go, rest = halves(rest, got)
        rest = pair(rest, after(swap(after(go, over[-1], down), "z", 2), grad_input))
    rest = rest.astype(F32)
    down = down.astype(F32)

    if aligned:
        own_wqkv, extra = finish(exchange(block, ALL_AXES), share, 3 * model, groups)
        own_bq, own_bv, stats = extra[0, :share], extra[1, :share], extra[2:17, 0]
    else:
        w_sum = sum(w for w, _ in w_sums).astype(BF16).reshape(devices, share, 3 * width)
        b_sum = jnp.pad(sum(w for _, w in w_sums)[None, :, 0], ((0, 7), (0, 0)))
        b_sum = b_sum + jnp.pad(stat_rows[:1], ((1, 6), (0, 3 * width - spare)))
        b_sum = jnp.broadcast_to(b_sum.astype(BF16)[None], (devices, 8, 3 * width))
        block = exchange(jnp.concatenate([w_sum, b_sum], axis=1), ALL_AXES).astype(F32)
        totals = jnp.sum(block.reshape(far * wide, groups, tall, 3, width), axis=0)
        totals = totals.transpose(1, 2, 0, 3).reshape(tall, 3 * model)
        own_wqkv, extra = totals[:share], totals[share:]
        own_bq = lax.dynamic_slice(extra, (0, first), (1, share))[0]
        own_bv = lax.dynamic_slice(extra, (0, 2 * model + first), (1, share))[0]
        stats = jnp.sum(block[:, share + 1, 2:17], axis=0)
    stats = stats[:5] + stats[5:10] + stats[10:15]
    stat_rms = jnp.sqrt(stats[:4] / (stats[4] * model))

    rest = rest.reshape(-1, model)
    own_win = rest[: ratio * share].reshape(ratio, share, model).transpose(1, 0, 2)
    own_win = own_win.reshape(share, ff)
    at = ratio * share
    own_wout = rest[at : at + share]
    at += share
    vectors = lax.dynamic_slice(rest, (at, first), (3, share))
    vectors_two = lax.dynamic_slice(rest, (at + 16, first), (3, share))
    own_bin = lax.dynamic_slice(rest, (at + 6 + ff_row, ff_first - ff_row * model), (1, ff_share))
    return (
        layer_out,
        grad_input,
        own_wqkv,
        own_bq,
        own_bv,
        own_wout,
        vectors[0],
        vectors[1],
        vectors[2],
        own_win,
        own_bin[0],
        down.reshape(ff_share, model),
        vectors_two[0],
        vectors_two[1],
        vectors_two[2],
        stat_rms,
    )


def solution(mesh):
    dp, seq = mesh.shape["dp"], mesh.shape["seq"]
    finer = Mesh(mesh.devices.reshape(dp // 2, 2, seq // 2, 2), ALL_AXES)
    token = P(BATCH_AXES, ROW_AXES, None)
    matrix = P(ALL_AXES, None)
    vector = P(ALL_AXES)
    placed = (
        (token, P(BATCH_AXES), matrix, vector, vector, matrix, vector, vector, vector)
        + (matrix, vector, matrix, vector, vector, vector, token)
    )
    results = (
        (token, token, matrix, vector, vector, matrix, vector, vector, vector)
        + (matrix, vector, matrix, vector, vector, vector, P())
    )
    return jax.shard_map(
        body, mesh=finer, in_specs=placed, out_specs=results, check_vma=False
    )
```

```python
import functools
import math

import jax
import jax.numpy as jnp
from jax import lax
from jax.experimental import pallas as pl
from jax.experimental.pallas import tpu as pltpu
from jax.sharding import Mesh
from jax.sharding import PartitionSpec as P

HD = 64
NORM_EPS = 1e-12
BATCH_AXES = ("z", "x")
ROW_AXES = ("y", "c")
ALL_AXES = BATCH_AXES + ROW_AXES
F32 = jnp.float32
BF16 = jnp.bfloat16
VMEM_LIMIT = 56 * 1024 * 1024


def dot(left, right, dims=((1,), (0,))):
    return lax.dot_general(left, right, (dims, ((), ())), preferred_element_type=F32)


NT = ((1,), (1,))
TN = ((0,), (0,))


def params():
    return pltpu.CompilerParams(vmem_limit_bytes=VMEM_LIMIT)


def cost(micros):
    return pl.CostEstimate(flops=int(micros * 1e9), transcendentals=0, bytes_accessed=0)


def after(value, *others):
    return lax.optimization_barrier((value,) + others)[0]


def fixed(shape):
    return pl.BlockSpec(shape, lambda i, m: (0,) * len(shape))


def at_block(shape, *index):
    return pl.BlockSpec(shape, lambda i, m: index)


def swap(array, axis, offset=1):
    size = lax.axis_size(axis)
    return lax.ppermute(array, axis, [(i, i ^ offset) for i in range(size)])


def exchange(array, axes):
    return lax.all_to_all(array, axes, split_axis=0, concat_axis=0, tiled=True)


def gather_rows(array):
    far = swap(array, "y")
    near = swap(array, "c")
    return [array, near, far, swap(far, "c")]


def head_lanes(width, head):
    lane = lax.broadcasted_iota(jnp.int32, (1, width), 1)
    return (lane >= head * HD) & (lane < (head + 1) * HD)


def attend_kernel(first, pieces, meta, *refs):
    hidden = refs[:pieces]
    w_ref, q_out, k_out, v_out, ctx_out, lse_out, w_all, b_all = refs[pieces:]
    width, seg = ctx_out.shape[1:]
    model = hidden[0].shape[-1]
    heads = width // HD
    length, place = meta[first + pl.program_id(0)], meta[meta.shape[0] - 1]
    filled = (length + seg - 1) // seg

    @pl.when(pl.program_id(0) == 0)
    def _():
        w_all[...] = w_ref[:, :, : 3 * width].reshape(model, 3 * width)
        each = w_ref.shape[1]
        if each < model:
            owners = width // each
            side = w_ref[pl.ds(place * owners, owners), :, 3 * width :]
        else:
            side = w_ref[:, pl.ds(pl.multiple_of(place * width, width), width), 3 * width :]
        side = side.reshape(width, -1).astype(F32)
        tall, spare = -width % 128, -side.shape[1] % 128
        side = jnp.concatenate([side, jnp.zeros((width, spare), F32)], axis=1)
        side = jnp.concatenate([side, jnp.zeros((tall, side.shape[1]), F32)], axis=0).T
        b_all[...] = jnp.zeros(b_all.shape, F32)
        b_all[0:1, :width] = side[0:1, :width]
        b_all[0:1, 2 * width :] = side[1:2, :width]

    for j in range(pieces):
        at = lax.bitwise_xor(place, j)

        @pl.when(at < filled)
        def _():
            qkv = dot(hidden[j][0], w_all[...]) + b_all[0:1]
            q_out[0, at] = qkv[:, :width].astype(BF16) * jnp.asarray(HD**-0.5, BF16)
            k_out[0, at] = qkv[:, width : 2 * width].astype(BF16)
            v_out[0, at] = qkv[:, 2 * width :].astype(BF16)

        @pl.when(at >= filled)
        def _():
            q_out[0, at] = jnp.zeros((seg, width), BF16)
            k_out[0, at] = jnp.zeros((seg, width), BF16)
            v_out[0, at] = jnp.zeros((seg, width), BF16)
            ctx_out[at] = jnp.zeros((width, seg), BF16)
            lse_out[0, at] = jnp.zeros((seg, lse_out.shape[-1]), F32)

    for count in range(1, pieces + 1):

        @pl.when(filled == count)
        def _(count=count):
            keys = k_out[0, 0:count].reshape(count * seg, width)
            values = v_out[0, 0:count].reshape(count * seg, width)
            column = lax.broadcasted_iota(jnp.int32, (1, seg), 1) + (count - 1) * seg
            tail_ok = column < length

            def block(at, carry):
                q = q_out[0, at]
                ctx = jnp.zeros((seg, width), F32)
                lse = jnp.zeros((seg, lse_out.shape[-1]), F32)
                for head in range(heads):
                    here = head_lanes(width, head)
                    scores = dot(jnp.where(here, q, jnp.zeros_like(q)), keys, NT)
                    tail = jnp.where(tail_ok, scores[:, (count - 1) * seg :], -jnp.inf)
                    if count > 1:
                        scores = jnp.concatenate([scores[:, : (count - 1) * seg], tail], axis=1)
                    else:
                        scores = tail
                    top = jnp.max(scores, axis=-1, keepdims=True)
                    weights = jnp.exp(scores - top)
                    total = jnp.sum(weights, axis=-1, keepdims=True)
                    probs = (weights * (1.0 / total)).astype(BF16)
                    ctx = jnp.where(here, dot(probs, values), ctx)
                    lane = lax.broadcasted_iota(jnp.int32, lse.shape, 1)
                    lse = jnp.where(lane == head, top + jnp.log(total), lse)
                ctx_out[at] = ctx.T.astype(BF16)
                lse_out[0, at] = lse
                return carry

            lax.fori_loop(0, count, block, 0)


def attend(first, seqs, meta, hidden, qkv):
    pieces = len(hidden)
    _, seg, model = hidden[0].shape
    width = model // pieces
    saved = jax.ShapeDtypeStruct((seqs, pieces, seg, width), BF16)
    saved_spec = pl.BlockSpec((1, pieces, seg, width), lambda i, m: (i, 0, 0, 0))
    return pl.pallas_call(
        functools.partial(attend_kernel, first, pieces),
        out_shape=(saved,) * 3
        + (
            jax.ShapeDtypeStruct((pieces, width, seqs * seg), BF16),
            jax.ShapeDtypeStruct((seqs, pieces, seg, 128), F32),
        ),
        grid_spec=pltpu.PrefetchScalarGridSpec(
            num_scalar_prefetch=1,
            grid=(seqs,),
            in_specs=[pl.BlockSpec((1, seg, model), lambda i, m: (first + i, 0, 0))] * pieces
            + [fixed(qkv.shape)],
            out_specs=[saved_spec] * 3
            + [
                pl.BlockSpec((pieces, width, seg), lambda i, m: (0, 0, i)),
                pl.BlockSpec((1, pieces, seg, 128), lambda i, m: (i, 0, 0, 0)),
            ],
            scratch_shapes=[pltpu.VMEM((model, 3 * width), BF16), pltpu.VMEM((8, 3 * width), F32)],
        ),
        compiler_params=params(),
        cost_estimate=cost(9 * seqs),
        name="attend",
    )(meta, *hidden, qkv)


def attend_back_kernel(seq, pieces, earlier, meta, *refs):
    hidden = refs[:pieces]
    (w_ref, grad_in, q_in, k_in, v_in, ctx_in, lse_in) = refs[pieces : pieces + 7]
    before = refs[pieces + 7 : pieces + 7 + earlier]
    if earlier:
        gin_keep, gin_send, block_out, w_all, dq_t, d_all, out_w, out_b = refs[pieces + 7 + earlier :]
    else:
        gin_keep, gin_send, out_w, out_b, w_all, dq_t, d_all = refs[pieces + 7 :]
    width, seg = grad_in.shape[1:]
    heads = width // HD
    model = hidden[0].shape[-1]
    length, place = meta[seq], meta[meta.shape[0] - 1]
    filled = (length + seg - 1) // seg
    w_all[...] = w_ref[:, :, : 3 * width].reshape(model, 3 * width)
    out_w[...] = jnp.zeros(out_w.shape, F32)
    out_b[...] = jnp.zeros(out_b.shape, F32)

    for count in range(1, pieces + 1):

        @pl.when(filled == count)
        def _(count=count):
            rows = count * seg
            queries = q_in[0, 0:count].reshape(rows, width)
            queries_t = queries.T
            upstream_t = jnp.concatenate([grad_in[at] for at in range(count)], axis=1)
            upstream = upstream_t.T
            ctx_t = jnp.concatenate([ctx_in[at] for at in range(count)], axis=1)
            lse_t = jnp.concatenate([lse_in[0, at].T[0:8] for at in range(count)], axis=1)
            product_t = ctx_t.astype(F32) * upstream_t.astype(F32)
            delta_t = [
                jnp.sum(product_t[h * HD : (h + 1) * HD], axis=0, keepdims=True)
                for h in range(heads)
            ]
            dq_t[:, 0:rows] = jnp.zeros((width, rows), F32)

            def block(at, carry):
                keys = k_in[0, at]
                values = v_in[0, at]
                keys_t = keys.T
                row = lax.broadcasted_iota(jnp.int32, (seg, 1), 0) + at * seg
                row_ok = row < length
                dk = jnp.zeros((seg, width), F32)
                dv = jnp.zeros((seg, width), F32)
                for head in range(heads):
                    here = head_lanes(width, head)
                    scores = dot(jnp.where(here, keys, jnp.zeros_like(keys)), queries_t)
                    probs = jnp.exp(scores - lse_t[head : head + 1])
                    probs = jnp.where(row_ok, probs, 0.0)
                    g_probs = dot(jnp.where(here, values, jnp.zeros_like(values)), upstream_t)
                    g_scores = (probs * (g_probs - delta_t[head])).astype(BF16)
                    dv = jnp.where(here, dot(probs.astype(BF16), upstream), dv)
                    dk = jnp.where(here, dot(g_scores, queries), dk)
                    part = slice(head * HD, (head + 1) * HD)
                    dq_t[part, 0:rows] += dot(keys_t[part], g_scores)
                d_all[at, :, width : 2 * width] = dk.astype(BF16)
                d_all[at, :, 2 * width :] = dv.astype(BF16)
                return carry

            lax.fori_loop(0, count, block, 0)
            for at in range(count):
                piece = dq_t[:, at * seg : (at + 1) * seg]
                d_all[at, :, 0:width] = (piece.T * HD**-0.5).astype(BF16)

    for j in range(pieces):
        at = lax.bitwise_xor(place, j)
        gin_out = (gin_send if j % 2 else gin_keep).at[j // 2]

        @pl.when(at < filled)
        def _():
            grads = d_all[at]
            gin_out[...] = dot(grads, w_all[...], NT).astype(BF16)
            out_w[...] += dot(hidden[j][0], grads, TN)
            out_b[...] += dot(grads, jnp.ones((seg, out_b.shape[-1]), BF16), TN)

        @pl.when(at >= filled)
        def _():
            gin_out[...] = jnp.zeros((seg, model), BF16)

    if earlier:
        devices, share, full = block_out.shape
        total = out_w[...]
        columns = out_b[...]
        for w_sum, b_sum in zip(before[:-1:2], before[1:-1:2]):
            total = total + w_sum[...]
            columns = columns + b_sum[...]
        block_out[:, :, : 3 * width] = total.astype(BF16).reshape(devices, share, 3 * width)
        spare = full - 3 * width
        side = before[-1][...]
        block_out[:, :, 3 * width :] = jnp.broadcast_to(
            side.astype(BF16)[None], (devices, share, spare)
        )
        lane = lax.broadcasted_iota(jnp.int32, (share, spare), 1)
        owners = width // share
        for k in range(owners):
            query = columns[k * share : (k + 1) * share, :spare]
            value = columns[2 * width + k * share : 2 * width + (k + 1) * share, :spare]
            mine = jnp.where(lane == 0, query, jnp.where(lane == 1, value, side))
            block_out[place * owners + k, :, 3 * width :] = mine.astype(BF16)


def finish_kernel(groups, block, own_ref, extra_ref):
    share, full = own_ref.shape
    devices = block.shape[0]
    part = full // (3 * groups)
    side = 0.0
    for g in range(groups):
        total = 0.0
        for r in range(devices // groups):
            total = total + block[r * groups + g].astype(F32)
        for p in range(3):
            at = p * groups * part + g * part
            own_ref[:, at : at + part] = total[:, p * part : (p + 1) * part]
        side = side + total[:, 3 * part :]
    spare = side.shape[1]
    side = jnp.concatenate([side, jnp.zeros((128 - share, spare), F32)], axis=0)
    side = jnp.concatenate([side, jnp.zeros((128, 128 - spare), F32)], axis=1)
    extra_ref[...] = side.T[: extra_ref.shape[0]]


def finish(block, share, full, groups):
    return pl.pallas_call(
        functools.partial(finish_kernel, groups),
        out_shape=[jax.ShapeDtypeStruct(s, F32) for s in ((share, full), (32, 128))],
        compiler_params=params(),
        name="finish",
    )(block)


def attend_back(seq, index, meta, hidden, qkv, grad_ctx, saved, before=(), share=1):
    pieces = len(hidden)
    _, seg, model = hidden[0].shape
    width = model // pieces
    saved_spec = at_block((1, pieces, seg, width), index, 0, 0, 0)
    gin = (pieces // 2, seg, model)
    sums = [((model, 3 * width), F32), ((3 * width, 128), F32)]
    blocks = [((model // share, share, -(-3 * width // 128) * 128), BF16)]
    outs = [(gin, BF16)] * 2 + (blocks if before else sums)
    return pl.pallas_call(
        functools.partial(attend_back_kernel, seq, pieces, len(before)),
        out_shape=[jax.ShapeDtypeStruct(*o) for o in outs],
        grid_spec=pltpu.PrefetchScalarGridSpec(
            num_scalar_prefetch=1,
            grid=(1,),
            in_specs=[at_block((1, seg, model), seq, 0, 0)] * pieces
            + [fixed(qkv.shape), at_block((pieces, width, seg), 0, 0, seq)]
            + [saved_spec] * 3
            + [
                at_block((pieces, width, seg), 0, 0, index),
                at_block((1, pieces, seg, 128), index, 0, 0, 0),
            ]
            + [fixed(a.shape) for a in before],
            out_specs=[fixed(o[0]) for o in outs],
            scratch_shapes=[
                pltpu.VMEM((model, 3 * width), BF16),
                pltpu.VMEM((width, pieces * seg), F32),
                pltpu.VMEM((pieces, seg, 3 * width), BF16),
            ]
            + [pltpu.VMEM(*o) for o in (sums if before else [])],
        ),
        compiler_params=params(),
        cost_estimate=cost(13),
        name="attend_back",
    )(meta, *hidden, qkv, grad_ctx, *saved, *before)


def normal_parts(v):
    t = 1.0 / (1.0 + (0.3275911 * 0.5**0.5) * jnp.abs(v))
    poly = t * (
        0.127414796
        + t * (-0.142248368 + t * (0.7107068705 + t * (-0.7265760135 + t * 0.5307027145)))
    )
    bell = jnp.exp2(v * v * (-0.5 / math.log(2.0)))
    upper = poly * bell
    cdf = jnp.where(v < 0, upper, 1.0 - upper)
    return cdf, bell * (0.5 / math.pi) ** 0.5


def normalise(values):
    center = values - jnp.mean(values, axis=-1, keepdims=True)
    root = lax.rsqrt(jnp.mean(center * center, axis=-1, keepdims=True) + NORM_EPS)
    return center * root, root


def normalise_back(grad, unit, root):
    mean_grad = jnp.mean(grad, axis=-1, keepdims=True)
    mean_prod = jnp.mean(grad * unit, axis=-1, keepdims=True)
    return root * (grad - mean_grad - unit * mean_prod)


ROWS = 64


def row_loop(start, stop, fn):
    def step(i, carry):
        fn(pl.ds(pl.multiple_of(start + i * ROWS, ROWS), ROWS), start + i * ROWS)
        return carry

    lax.fori_loop(0, (stop - start) // ROWS, step, 0, unroll=2)


def fold(values):
    return jnp.sum(values.reshape(-1, 8, values.shape[-1]), axis=0)


def mask_rows(meta, base, seg):
    seq = base // seg
    position = lax.broadcasted_iota(jnp.int32, (ROWS, 1), 0) + (base - seq * seg)
    return (position + meta[meta.shape[0] - 1] * seg < meta[seq]).astype(F32)


def tokens(ref, base):
    seg = ref.shape[1]
    seq = base // seg
    return ref[seq, pl.ds(pl.multiple_of(base - seq * seg, ROWS), ROWS)].astype(F32)


def over_rows(ref, k):
    return jnp.sum(ref[k], axis=0, keepdims=True)


def onward_kernel(groups, meta, *refs):
    ctxs = refs[:groups]
    (x_ref, cot_ref, wout_ref, win_ref, wdown_ref, small_a, small_b) = refs[groups : groups + 7]
    (
        out_ref,
        act_ref,
        slope_ref,
        gsecond_ref,
        low_ref,
        gres_ref,
        unit,
        root,
        vecs,
        stats_ref,
        sums_ref,
        normed,
        acc,
        inner,
        acc_sums,
    ) = refs[groups + 7 :]
    step = pl.program_id(0)
    seqs, seg, model = x_ref.shape
    rows = seqs * seg

    @pl.when(step == 0)
    def _():
        vecs[0:8] = jnp.sum(small_a[...].astype(F32), axis=0)
        vecs[8:16] = jnp.sum(small_b[...].astype(F32), axis=0)
        acc_sums[...] = jnp.zeros(acc_sums.shape, F32)
        wout = wout_ref[...].reshape(model, model)
        done = 0
        for ref in ctxs:
            parts, width, many = ref.shape
            context = ref[...].reshape(parts * width, many)
            acc[done : done + many] = dot(context, wout, TN) + vecs[0:1]
            done += many

        def first_norm(at, base):
            mask = mask_rows(meta, base, seg)
            x = tokens(x_ref, base)
            branch = acc[at]
            n1, r1 = normalise(x + branch)
            value = n1 * vecs[1:2] + vecs[2:3]
            unit[at] = n1
            root[at] = jnp.broadcast_to(r1, (ROWS, root.shape[-1]))
            normed[at] = value
            low_ref[at] = value.astype(BF16)
            acc_sums[0] += fold(x * x * mask)
            acc_sums[1] += fold(branch * branch * mask)

        row_loop(0, rows, first_norm)
        acc[...] = jnp.broadcast_to(vecs[3:4], acc.shape)

    win = win_ref[...].reshape(model, model)
    wdown = wdown_ref[...].reshape(model, model)
    bin_row = vecs[pl.ds(6 + step, 1)]
    for b in range(seqs):
        lo, hi = b * seg, (b + 1) * seg
        inner[lo:hi] = dot(low_ref[lo:hi], win)

        def activate(at, base):
            value = inner[at] + bin_row
            cdf, pdf = normal_parts(value)
            act_ref[0, at] = (value * cdf).astype(BF16)
            slope_ref[0, at] = cdf + value * pdf

        row_loop(lo, hi, activate)
        acc[lo:hi] += dot(act_ref[0, lo:hi], wdown)

    @pl.when(step == pl.num_programs(0) - 1)
    def _():
        def second_norm(at, base):
            mask = mask_rows(meta, base, seg)
            second = acc[at]
            n2, r2 = normalise(normed[at] + second)
            output = n2 * vecs[5:6] + vecs[15:16]
            out_ref[at] = (output * mask).astype(BF16)
            g_out = tokens(cot_ref, base) * mask
            g_resid = normalise_back(g_out * vecs[5:6], n2, r2)
            low = g_resid.astype(BF16)
            gsecond_ref[at] = low
            gres_ref[at] = g_resid
            acc_sums[2] += fold(second * second * mask)
            acc_sums[3] += fold(output * output * mask)
            acc_sums[4] += fold(low.astype(F32))
            acc_sums[5] += fold(g_out * n2)
            acc_sums[6] += fold(g_out)

        row_loop(0, rows, second_norm)
        for row in range(8):
            stats_ref[row : row + 1] = over_rows(acc_sums, row)
        sums_ref[...] = jnp.zeros(sums_ref.shape, F32)
        for row in range(3):
            sums_ref[row : row + 1] = over_rows(acc_sums, 4 + row)


def onward(meta, ctxs, x, cot, specs, args, ratio):
    seqs, seg, model = x.shape
    rows = seqs * seg
    flat = (rows, model)
    chunked = (ratio, rows, model)
    outs = [(flat, BF16), (chunked, BF16), (chunked, F32), (flat, BF16), (flat, BF16)]
    outs += [(flat, F32), (flat, F32), ((rows, 128), F32), ((16, model), F32)]
    outs += [((8, model), F32)] * 2
    by_chunk = pl.BlockSpec((1, rows, model), lambda i, m: (i, 0, 0))
    return pl.pallas_call(
        functools.partial(onward_kernel, len(ctxs)),
        out_shape=[jax.ShapeDtypeStruct(*o) for o in outs],
        grid_spec=pltpu.PrefetchScalarGridSpec(
            num_scalar_prefetch=1,
            grid=(ratio,),
            in_specs=[fixed(c.shape) for c in ctxs] + [fixed(x.shape), fixed(cot.shape)] + specs,
            out_specs=[by_chunk if o[0] == chunked else fixed(o[0]) for o in outs],
            scratch_shapes=[
                pltpu.VMEM(flat, F32),
                pltpu.VMEM(flat, F32),
                pltpu.VMEM(flat, F32),
                pltpu.VMEM((8, 8, model), F32),
            ],
        ),
        compiler_params=params(),
        cost_estimate=cost(28),
        name="onward",
    )(meta, *ctxs, x, cot, *args)


def back_kernel(
    slope_ref,
    gsecond_ref,
    start_ref,
    unit,
    root,
    vecs,
    wout_ref,
    win_ref,
    wdown_ref,
    gres_ref,
    gctx_ref,
    ginner_ref,
    gbranch_ref,
    sums_ref,
    acc,
    inner,
    acc_sums,
):
    step = pl.program_id(0)
    rows, model = acc.shape
    many = rows // 3 if rows % 3 == 0 else rows

    @pl.when(step == 0)
    def _():
        acc[...] = start_ref[...]
        sums_ref[...] = jnp.zeros(sums_ref.shape, F32)

    win = win_ref[...].reshape(model, model)
    wdown = wdown_ref[...].reshape(model, model)
    acc_sums[...] = jnp.zeros(acc_sums.shape, F32)
    for lo in range(0, rows, many):
        hi = lo + many
        inner[lo:hi] = dot(gsecond_ref[lo:hi], wdown, NT)

        def through(at, base):
            low = (inner[at] * slope_ref[0, at]).astype(BF16)
            ginner_ref[0, at] = low
            acc_sums[0] += fold(low.astype(F32))

        row_loop(lo, hi, through)
        acc[lo:hi] += dot(ginner_ref[0, lo:hi], win, NT)
    sums_ref[pl.ds(6 + step, 1)] = over_rows(acc_sums, 0)

    @pl.when(step == pl.num_programs(0) - 1)
    def _():
        acc_sums[0] = jnp.zeros(acc_sums.shape[1:], F32)

        def first_back(at, base):
            grad = acc[at]
            n1 = unit[at]
            g_resid = normalise_back(grad * vecs[1:2], n1, root[at][:, 0:1])
            low = g_resid.astype(BF16)
            gres_ref[at] = g_resid
            gbranch_ref[at] = low
            acc_sums[0] += fold(low.astype(F32))
            acc_sums[1] += fold(grad * n1)
            acc_sums[2] += fold(grad)

        row_loop(0, rows, first_back)
        wout = wout_ref[...].reshape(model, model)
        piece = dot(wout, gbranch_ref[...], NT).astype(BF16)
        gctx_ref[...] = piece.reshape(gctx_ref.shape)
        for row in range(3):
            sums_ref[row : row + 1] = over_rows(acc_sums, row)


def back(slopes, g_second, start, unit, root, vecs, specs, args, parts):
    ratio, rows, model = slopes.shape
    flat = (rows, model)
    chunked = (ratio, rows, model)
    outs = [(flat, F32), ((parts, model // parts, rows), BF16), (chunked, BF16)]
    outs += [(flat, BF16), ((16, model), F32)]
    by_chunk = pl.BlockSpec((1, rows, model), lambda i: (i, 0, 0))
    whole = lambda shape: pl.BlockSpec(shape, lambda i: (0,) * len(shape))
    specs = [pl.BlockSpec(x.block_shape, functools.partial(drop_last, x.index_map)) for x in specs]
    return pl.pallas_call(
        back_kernel,
        out_shape=[jax.ShapeDtypeStruct(*o) for o in outs],
        grid=(ratio,),
        in_specs=[by_chunk]
        + [whole(a.shape) for a in (g_second, start, unit, root, vecs)]
        + specs[:3],
        out_specs=[by_chunk if o[0] == chunked else whole(o[0]) for o in outs],
        scratch_shapes=[
            pltpu.VMEM(flat, F32),
            pltpu.VMEM(flat, F32),
            pltpu.VMEM((3, 8, model), F32),
        ],
        compiler_params=params(),
        cost_estimate=cost(22),
        name="back",
    )(slopes, g_second, start, unit, root, vecs, *args[:3])


def drop_last(index_map, i):
    return index_map(i, None)


def spread(grad, keep, send, me, order):
    many = keep.shape[0]
    for n in range(many):
        slot = 0
        for i, bit in enumerate(order):
            slot |= ((n >> (len(order) - 1 - i)) & 1) << bit
        keep[n] = grad[lax.bitwise_xor(me, slot)]
        send[n] = grad[lax.bitwise_xor(me, slot + 1)]


Y_BIT, X_BIT, NEAR_Z_BIT, FAR_Z_BIT = 1, 2, 3, 4


def down_kernel(act_ref, g_ref, out_ref):
    grad = dot(act_ref[0], g_ref[...], TN).astype(BF16)
    out_ref[...] = grad.reshape(out_ref.shape)


def down_grads(acts, g_second, each):
    ratio, rows, model = acts.shape
    return pl.pallas_call(
        down_kernel,
        out_shape=jax.ShapeDtypeStruct((ratio * model // each, each, model), BF16),
        grid=(ratio,),
        in_specs=[
            pl.BlockSpec((1, rows, model), lambda i: (i, 0, 0)),
            pl.BlockSpec((rows, model), lambda i: (0, 0)),
        ],
        out_specs=pl.BlockSpec((model // each, each, model), lambda i: (i, 0, 0)),
        compiler_params=params(),
        cost_estimate=cost(8),
        name="down_grads",
    )(acts, g_second)


def rest_kernel(ratio, groups, cut, meta, low_ref, ginner_ref, *refs):
    ctxs = refs[:groups]
    gbranch_ref, sums_one, sums_two = refs[groups : groups + 3]
    outs = refs[groups + 3 : groups + 7]
    grad = refs[groups + 7]
    me = meta[meta.shape[0] - 2]
    step = pl.program_id(0)
    devices, each, model = grad.shape

    @pl.when(step < ratio)
    def _():
        grad[...] = dot(low_ref[...], ginner_ref[0], TN).astype(BF16).reshape(grad.shape)

    @pl.when(step == ratio)
    def _():
        total = 0.0
        done = 0
        for ref in ctxs:
            parts, width, many = ref.shape
            context = ref[...].reshape(parts * width, many)
            total = total + dot(context, gbranch_ref[done : done + many])
            done += many
        grad[...] = total.astype(BF16).reshape(grad.shape)

    @pl.when(step == ratio + 1)
    def _():
        block = jnp.concatenate(
            [sums_one[...], sums_two[...], jnp.zeros((each - 24, model), F32)]
            if each > 24
            else [sums_one[...], sums_two[...]],
            axis=0,
        )
        grad[...] = jnp.broadcast_to(block.astype(BF16)[None], grad.shape)

    x_first = (X_BIT, Y_BIT, NEAR_Z_BIT, FAR_Z_BIT)
    y_first = (Y_BIT, X_BIT, NEAR_Z_BIT, FAR_Z_BIT)

    @pl.when(step < cut)
    def _():
        spread(grad, outs[0], outs[1], me, x_first)

    @pl.when(step >= cut)
    def _():
        spread(grad, outs[2], outs[3], me, y_first)


def rest_grads(meta, low, g_inner, ctxs, g_branch, sums_one, sums_two, devices, each):
    ratio, rows, model = g_inner.shape
    cut = (ratio + 2) // 2
    half = devices // 2
    shapes = [jax.ShapeDtypeStruct((half, n * each, model), BF16) for n in (cut, ratio + 2 - cut)]
    specs = [
        pl.BlockSpec((half, each, model), lambda i, m: (0, jnp.minimum(i, cut - 1), 0)),
        pl.BlockSpec((half, each, model), lambda i, m: (0, jnp.maximum(i - cut, 0), 0)),
    ]
    return pl.pallas_call(
        functools.partial(rest_kernel, ratio, len(ctxs), cut),
        out_shape=(shapes[0], shapes[0], shapes[1], shapes[1]),
        grid_spec=pltpu.PrefetchScalarGridSpec(
            num_scalar_prefetch=1,
            grid=(ratio + 2,),
            in_specs=[
                fixed(low.shape),
                pl.BlockSpec((1, rows, model), lambda i, m: (jnp.minimum(i, ratio - 1), 0, 0)),
            ]
            + [fixed(c.shape) for c in ctxs]
            + [fixed(g_branch.shape), fixed(sums_one.shape), fixed(sums_two.shape)],
            out_specs=[specs[0], specs[0], specs[1], specs[1]],
            scratch_shapes=[pltpu.VMEM((devices, each, model), BF16)],
        ),
        compiler_params=params(),
        cost_estimate=cost(10),
        name="rest_grads",
    )(meta, low, g_inner, *ctxs, g_branch, sums_one, sums_two)


def natural_grads(acts, g_second, low, g_inner, ctxs, g_branch, sums, devices, share):
    ratio, rows, model = acts.shape
    down = jnp.concatenate([dot(a, g_second, TN) for a in acts]).reshape(devices, -1, model)
    context = jnp.concatenate(ctxs, axis=2).reshape(model, rows)
    rest = [dot(low, g, TN) for g in g_inner] + [dot(context, g_branch)]
    rest = [r.reshape(devices, share, model) for r in rest]
    rest.append(jnp.broadcast_to(sums[None], (devices,) + sums.shape))
    return down.astype(BF16), jnp.concatenate(rest, axis=1).astype(BF16)


def pair(kept, sent):
    return (kept.astype(F32) + sent.astype(F32)).astype(BF16)


def halves(kept, got):
    half = kept.shape[0] // 2
    return pair(kept[half:], got[half:]), pair(kept[:half], got[:half])


def body(
    hidden_in,
    lengths,
    w_qkv,
    b_query,
    b_value,
    w_out,
    b_out,
    gain_one,
    bias_one,
    w_in,
    b_in,
    w_down,
    b_down,
    gain_two,
    bias_two,
    cotangent,
):
    seqs, seg, model = hidden_in.shape
    sizes = tuple(lax.axis_size(a) for a in ALL_AXES)
    far, wide, near_y, cores = sizes
    groups = near_y * cores
    devices = far * wide * groups
    place = lax.axis_index(ROW_AXES)
    me = lax.axis_index(ALL_AXES)
    share = model // devices
    ff = w_in.shape[1]
    ff_share = ff // devices
    ratio = ff // model
    width = model // groups
    aligned = share % 8 == 0 and devices == 8 * ratio and far == ratio
    meta = jnp.concatenate([lengths, me[None], place[None]]).astype(jnp.int32)

    first = me * share
    cut = w_qkv.reshape(share, 3, groups, width).transpose(2, 0, 1, 3)
    cut = cut.reshape(groups, share, 3 * width)
    spare = -3 * width % 128
    side = jnp.pad(jnp.stack([b_query, b_value], axis=1), ((0, 0), (0, spare - 2)))
    side = jnp.broadcast_to(side[None], (groups,) + side.shape)
    packed = jnp.concatenate([cut, side], axis=2)
    packed = jnp.broadcast_to(packed[None], (far * wide,) + packed.shape)
    qkv = exchange(packed.reshape(devices, share, -1), ALL_AXES)
    if not aligned:
        qkv = qkv.reshape(1, model, -1)

    hidden = gather_rows(hidden_in)

    small = jnp.zeros((16, model), BF16)
    vectors = jnp.stack([b_out, gain_one, bias_one, b_down, b_down, gain_two])
    small = lax.dynamic_update_slice(small, vectors, (0, first))
    small = lax.dynamic_update_slice(small, bias_two[None], (15, first))
    ff_first = me * ff_share
    ff_row = ff_first // model
    small = lax.dynamic_update_slice(small, b_in[None], (6 + ff_row, ff_first - ff_row * model))
    bundle = jnp.concatenate(
        [
            w_in.reshape(share, ratio, model).transpose(1, 0, 2).reshape(-1, model),
            w_down,
            w_out,
            small,
        ]
    )
    bundle = lax.all_gather(bundle, ALL_AXES, axis=0, tiled=False)
    at = ratio * share
    if aligned:
        weight_specs = [
            at_block((devices, share, model), 0, (at + ff_share) // share, 0),
            pl.BlockSpec((devices, share, model), lambda i, m: (0, i, 0)),
            pl.BlockSpec((devices // ratio, ff_share, model), lambda i, m: (i, 1, 0)),
            at_block((devices, 8, model), 0, (at + ff_share + share) // 8, 0),
            at_block((devices, 8, model), 0, (at + ff_share + share) // 8 + 1, 0),
        ]
        weight_args = [bundle] * 5
    else:
        win = bundle[:, :at].reshape(devices, ratio, share, model).transpose(1, 0, 2, 3)
        small = bundle[:, at + ff_share + share :]
        weight_args = [
            bundle[:, at + ff_share : at + ff_share + share].reshape(model, model),
            win.reshape(ratio, model, model),
            bundle[:, at : at + ff_share].reshape(ratio, model, model),
            small[:, :8],
            small[:, 8:],
        ]
        by_chunk = pl.BlockSpec((1, model, model), lambda i, m: (i, 0, 0))
        weight_specs = [fixed(a.shape) for a in weight_args]
        weight_specs[1] = weight_specs[2] = by_chunk

    spans = [(0, seqs - 1), (seqs - 1, 1)]
    saved = []
    ctxs = []
    for start, count in spans:
        q, k, v, ctx, lse = attend(start, count, meta, hidden, qkv)
        saved.append((q, k, v, ctx, lse))
        ctxs.append(exchange(ctx, ROW_AXES))

    (out, acts, slopes, g_second, low, start, unit, root, vecs, stats, sums_two) = onward(
        meta, ctxs, hidden_in, cotangent, weight_specs, weight_args, ratio
    )
    layer_out = out.reshape(seqs, seg, model)
    if aligned:
        down = down_grads(acts, g_second, ff_share)
        start = after(start, down)
        down = lax.psum_scatter(down, ALL_AXES, scatter_dimension=0, tiled=False)
    g_resid, g_ctx, g_inner, g_branch, sums_one = back(
        slopes, g_second, start, unit, root, vecs, weight_specs, weight_args, groups
    )
    g_ctx = exchange(g_ctx, ROW_AXES)
    if aligned:
        keep_a, send_a, keep_b, send_b = rest_grads(
            meta, low, g_inner, ctxs, g_branch, sums_one, sums_two, devices, share
        )
        got_a, got_b = swap(send_a, "c"), swap(send_b, "c")
    else:
        sums = jnp.concatenate([sums_one, sums_two])
        down, rest = natural_grads(
            acts, g_second, low, g_inner, ctxs, g_branch, sums, devices, share
        )
        down = lax.psum_scatter(down, ALL_AXES, scatter_dimension=0, tiled=False)
        rest = lax.psum_scatter(rest, ALL_AXES, scatter_dimension=0, tiled=False)

    squares = jnp.sum(stats[:4], axis=1)
    valid = jnp.sum(jnp.clip(lengths - place * seg, 0, seg)).astype(F32)
    exact = jnp.concatenate([squares, valid[None]])
    terms = []
    for _ in range(3):
        terms.append(lax.reduce_precision(exact, 8, 7))
        exact = exact - terms[-1]
    stat_rows = jnp.pad(jnp.concatenate(terms)[None], ((0, share - 1), (2, spare - 17)))

    homes = [(span, i) for span, (_, count) in enumerate(spans) for i in range(count)]
    w_sums = []
    partials = []
    inputs = [None] * seqs
    over = [None] * seqs

    def settle(b):
        kept, near = partials[b]
        here = kept[0].astype(F32) + near[0].astype(F32)
        inputs[b] = g_resid[b * seg : (b + 1) * seg] + here
        over[b] = pair(kept[1], near[1])

    for b, (span, index) in enumerate(homes):
        if b == 1 and aligned:
            go_a, keep_a = halves(keep_a, after(got_a, gin_send))
            go_b, keep_b = halves(keep_b, after(got_b, gin_send))
            g_ctx = after(g_ctx, go_a, go_b)
            got_a, got_b = swap(go_a, "x"), swap(go_b, "y")
        if b == seqs - 1 and aligned:
            go_a, keep_a = halves(keep_a, after(got_a, gin_send))
            go_b, keep_b = halves(keep_b, after(got_b, gin_send))
            g_ctx = after(g_ctx, go_a, go_b)
            got_a, got_b = swap(go_a, "y"), swap(go_b, "x")
        before = ()
        if b == seqs - 1 and aligned:
            before = [w for w_sum in w_sums for w in w_sum] + [stat_rows]
        gin_keep, gin_send, *w_sum = attend_back(
            b, index, meta, hidden, qkv, g_ctx, saved[span], before, share
        )
        block = w_sum[0]
        w_sums.append(w_sum)
        partials.append((gin_keep, swap(gin_send, "c")))
        if b:
            partials[b - 1] = after(partials[b - 1], gin_send)
            settle(b - 1)
    settle(seqs - 1)
    inputs = [mine + swap(far_part, "y").astype(F32) for mine, far_part in zip(inputs, over)]
    grad_input = jnp.stack(inputs)
    if aligned:
        rest = jnp.concatenate([keep_a, keep_b], axis=1)
        got_a, got_b, block = lax.optimization_barrier((got_a, got_b, block))
        got = jnp.concatenate([got_a, got_b], axis=1)
        go, rest = halves(rest, got)
        got = swap(after(go, over[-1]), "z", 1)
        go, rest = halves(rest, got)
        rest = pair(rest, after(swap(after(go, over[-1], down), "z", 2), grad_input))
    rest = rest.astype(F32)
    down = down.astype(F32)

    if aligned:
        own_wqkv, extra = finish(exchange(block, ALL_AXES), share, 3 * model, groups)
        own_bq, own_bv, stats = extra[0, :share], extra[1, :share], extra[2:17, 0]
    else:
        w_sum = sum(w for w, _ in w_sums).astype(BF16).reshape(devices, share, 3 * width)
        b_sum = jnp.pad(sum(w for _, w in w_sums)[None, :, 0], ((0, 7), (0, 0)))
        b_sum = b_sum + jnp.pad(stat_rows[:1], ((1, 6), (0, 3 * width - spare)))
        b_sum = jnp.broadcast_to(b_sum.astype(BF16)[None], (devices, 8, 3 * width))
        block = exchange(jnp.concatenate([w_sum, b_sum], axis=1), ALL_AXES).astype(F32)
        totals = jnp.sum(block.reshape(far * wide, groups, share + 8, 3, width), axis=0)
        totals = totals.transpose(1, 2, 0, 3).reshape(share + 8, 3 * model)
        own_wqkv, extra = totals[:share], totals[share:]
        own_bq = lax.dynamic_slice(extra, (0, first), (1, share))[0]
        own_bv = lax.dynamic_slice(extra, (0, 2 * model + first), (1, share))[0]
        stats = jnp.sum(block[:, share + 1, 2:17], axis=0)
    stats = stats[:5] + stats[5:10] + stats[10:15]
    stat_rms = jnp.sqrt(stats[:4] / (stats[4] * model))

    rest = rest.reshape(-1, model)
    own_win = rest[: ratio * share].reshape(ratio, share, model).transpose(1, 0, 2)
    own_win = own_win.reshape(share, ff)
    at = ratio * share
    own_wout = rest[at : at + share]
    at += share
    vectors = lax.dynamic_slice(rest, (at, first), (3, share))
    vectors_two = lax.dynamic_slice(rest, (at + 16, first), (3, share))
    own_bin = lax.dynamic_slice(rest, (at + 6 + ff_row, ff_first - ff_row * model), (1, ff_share))
    return (
        layer_out,
        grad_input,
        own_wqkv,
        own_bq,
        own_bv,
        own_wout,
        vectors[0],
        vectors[1],
        vectors[2],
        own_win,
        own_bin[0],
        down.reshape(ff_share, model),
        vectors_two[0],
        vectors_two[1],
        vectors_two[2],
        stat_rms,
    )


def solution(mesh):
    dp, seq = mesh.shape["dp"], mesh.shape["seq"]
    finer = Mesh(mesh.devices.reshape(dp // 2, 2, seq // 2, 2), ALL_AXES)
    token = P(BATCH_AXES, ROW_AXES, None)
    matrix = P(ALL_AXES, None)
    vector = P(ALL_AXES)
    placed = (
        (token, P(BATCH_AXES), matrix, vector, vector, matrix, vector, vector, vector)
        + (matrix, vector, matrix, vector, vector, vector, token)
    )
    results = (
        (token, token, matrix, vector, vector, matrix, vector, vector, vector)
        + (matrix, vector, matrix, vector, vector, vector, P())
    )
    return jax.shard_map(
        body, mesh=finer, in_specs=placed, out_specs=results, check_vma=False
    )
```

```python
import functools
import math

import jax
import jax.numpy as jnp
from jax import lax
from jax.experimental import pallas as pl
from jax.experimental.pallas import tpu as pltpu
from jax.sharding import Mesh
from jax.sharding import PartitionSpec as P

HD = 64
NORM_EPS = 1e-12
BATCH_AXES = ("z", "x")
ROW_AXES = ("y", "c")
ALL_AXES = BATCH_AXES + ROW_AXES
F32 = jnp.float32
BF16 = jnp.bfloat16
VMEM_LIMIT = 56 * 1024 * 1024


def dot(left, right, dims=((1,), (0,))):
    return lax.dot_general(left, right, (dims, ((), ())), preferred_element_type=F32)


NT = ((1,), (1,))
TN = ((0,), (0,))


def params():
    return pltpu.CompilerParams(vmem_limit_bytes=VMEM_LIMIT)


def cost(micros):
    return pl.CostEstimate(flops=int(micros * 1e9), transcendentals=0, bytes_accessed=0)


def after(value, *others):
    return lax.optimization_barrier((value,) + others)[0]


def fixed(shape):
    return pl.BlockSpec(shape, lambda i, m: (0,) * len(shape))


def at_block(shape, *index):
    return pl.BlockSpec(shape, lambda i, m: index)


def swap(array, axis, offset=1):
    size = lax.axis_size(axis)
    return lax.ppermute(array, axis, [(i, i ^ offset) for i in range(size)])


def exchange(array, axes):
    return lax.all_to_all(array, axes, split_axis=0, concat_axis=0, tiled=True)


def gather_rows(array):
    far = swap(array, "y")
    near = swap(array, "c")
    return [array, near, far, swap(far, "c")]


def head_lanes(width, head):
    lane = lax.broadcasted_iota(jnp.int32, (1, width), 1)
    return (lane >= head * HD) & (lane < (head + 1) * HD)


def attend_kernel(first, pieces, meta, *refs):
    hidden = refs[:pieces]
    w_ref, q_out, k_out, v_out, ctx_out, lse_out, w_all, b_all = refs[pieces:]
    width, seg = ctx_out.shape[1:]
    model = hidden[0].shape[-1]
    heads = width // HD
    length, place = meta[first + pl.program_id(0)], meta[meta.shape[0] - 1]
    filled = (length + seg - 1) // seg

    @pl.when(pl.program_id(0) == 0)
    def _():
        w_all[...] = w_ref[:, :, : 3 * width].reshape(model, 3 * width)
        each = w_ref.shape[1]
        if each < model:
            owners = width // each
            side = w_ref[pl.ds(place * owners, owners), :, 3 * width :]
        else:
            side = w_ref[:, pl.ds(pl.multiple_of(place * width, width), width), 3 * width :]
        side = side.reshape(width, -1).astype(F32)
        tall, spare = -width % 128, -side.shape[1] % 128
        side = jnp.concatenate([side, jnp.zeros((width, spare), F32)], axis=1)
        side = jnp.concatenate([side, jnp.zeros((tall, side.shape[1]), F32)], axis=0).T
        b_all[...] = jnp.zeros(b_all.shape, F32)
        b_all[0:1, :width] = side[0:1, :width]
        b_all[0:1, 2 * width :] = side[1:2, :width]

    for j in range(pieces):
        at = lax.bitwise_xor(place, j)

        @pl.when(at < filled)
        def _():
            qkv = dot(hidden[j][0], w_all[...]) + b_all[0:1]
            q_out[0, at] = qkv[:, :width].astype(BF16) * jnp.asarray(HD**-0.5, BF16)
            k_out[0, at] = qkv[:, width : 2 * width].astype(BF16)
            v_out[0, at] = qkv[:, 2 * width :].astype(BF16)

        @pl.when(at >= filled)
        def _():
            q_out[0, at] = jnp.zeros((seg, width), BF16)
            k_out[0, at] = jnp.zeros((seg, width), BF16)
            v_out[0, at] = jnp.zeros((seg, width), BF16)
            ctx_out[at] = jnp.zeros((width, seg), BF16)
            lse_out[0, at] = jnp.zeros((seg, lse_out.shape[-1]), F32)

    for count in range(1, pieces + 1):

        @pl.when(filled == count)
        def _(count=count):
            keys = k_out[0, 0:count].reshape(count * seg, width)
            values = v_out[0, 0:count].reshape(count * seg, width)
            column = lax.broadcasted_iota(jnp.int32, (1, seg), 1) + (count - 1) * seg
            tail_ok = column < length

            def block(at, carry):
                q = q_out[0, at]
                ctx = jnp.zeros((seg, width), F32)
                lse = jnp.zeros((seg, lse_out.shape[-1]), F32)
                for head in range(heads):
                    here = head_lanes(width, head)
                    scores = dot(jnp.where(here, q, jnp.zeros_like(q)), keys, NT)
                    tail = jnp.where(tail_ok, scores[:, (count - 1) * seg :], -jnp.inf)
                    if count > 1:
                        scores = jnp.concatenate([scores[:, : (count - 1) * seg], tail], axis=1)
                    else:
                        scores = tail
                    top = jnp.max(scores, axis=-1, keepdims=True)
                    weights = jnp.exp(scores - top)
                    total = jnp.sum(weights, axis=-1, keepdims=True)
                    probs = (weights * (1.0 / total)).astype(BF16)
                    ctx = jnp.where(here, dot(probs, values), ctx)
                    lane = lax.broadcasted_iota(jnp.int32, lse.shape, 1)
                    lse = jnp.where(lane == head, top + jnp.log(total), lse)
                ctx_out[at] = ctx.T.astype(BF16)
                lse_out[0, at] = lse
                return carry

            lax.fori_loop(0, count, block, 0)


def attend(first, seqs, meta, hidden, qkv):
    pieces = len(hidden)
    _, seg, model = hidden[0].shape
    width = model // pieces
    saved = jax.ShapeDtypeStruct((seqs, pieces, seg, width), BF16)
    saved_spec = pl.BlockSpec((1, pieces, seg, width), lambda i, m: (i, 0, 0, 0))
    return pl.pallas_call(
        functools.partial(attend_kernel, first, pieces),
        out_shape=(saved,) * 3
        + (
            jax.ShapeDtypeStruct((pieces, width, seqs * seg), BF16),
            jax.ShapeDtypeStruct((seqs, pieces, seg, 128), F32),
        ),
        grid_spec=pltpu.PrefetchScalarGridSpec(
            num_scalar_prefetch=1,
            grid=(seqs,),
            in_specs=[pl.BlockSpec((1, seg, model), lambda i, m: (first + i, 0, 0))] * pieces
            + [fixed(qkv.shape)],
            out_specs=[saved_spec] * 3
            + [
                pl.BlockSpec((pieces, width, seg), lambda i, m: (0, 0, i)),
                pl.BlockSpec((1, pieces, seg, 128), lambda i, m: (i, 0, 0, 0)),
            ],
            scratch_shapes=[pltpu.VMEM((model, 3 * width), BF16), pltpu.VMEM((8, 3 * width), F32)],
        ),
        compiler_params=params(),
        cost_estimate=cost(9 * seqs),
        name="attend",
    )(meta, *hidden, qkv)


def attend_back_kernel(seq, pieces, earlier, meta, *refs):
    hidden = refs[:pieces]
    (w_ref, grad_in, q_in, k_in, v_in, ctx_in, lse_in) = refs[pieces : pieces + 7]
    before = refs[pieces + 7 : pieces + 7 + earlier]
    if earlier:
        gin_keep, gin_send, block_out, w_all, dq_t, d_all, out_w, out_b = refs[pieces + 7 + earlier :]
    else:
        gin_keep, gin_send, out_w, out_b, w_all, dq_t, d_all = refs[pieces + 7 :]
    width, seg = grad_in.shape[1:]
    heads = width // HD
    model = hidden[0].shape[-1]
    length, place = meta[seq], meta[meta.shape[0] - 1]
    filled = (length + seg - 1) // seg
    w_all[...] = w_ref[:, :, : 3 * width].reshape(model, 3 * width)
    out_w[...] = jnp.zeros(out_w.shape, F32)
    out_b[...] = jnp.zeros(out_b.shape, F32)

    for count in range(1, pieces + 1):

        @pl.when(filled == count)
        def _(count=count):
            rows = count * seg
            queries = q_in[0, 0:count].reshape(rows, width)
            queries_t = queries.T
            upstream_t = jnp.concatenate([grad_in[at] for at in range(count)], axis=1)
            upstream = upstream_t.T
            ctx_t = jnp.concatenate([ctx_in[at] for at in range(count)], axis=1)
            lse_t = jnp.concatenate([lse_in[0, at].T[0:8] for at in range(count)], axis=1)
            product_t = ctx_t.astype(F32) * upstream_t.astype(F32)
            delta_t = [
                jnp.sum(product_t[h * HD : (h + 1) * HD], axis=0, keepdims=True)
                for h in range(heads)
            ]
            dq_t[:, 0:rows] = jnp.zeros((width, rows), F32)

            def block(at, carry):
                keys = k_in[0, at]
                values = v_in[0, at]
                keys_t = keys.T
                row = lax.broadcasted_iota(jnp.int32, (seg, 1), 0) + at * seg
                row_ok = row < length
                dk = jnp.zeros((seg, width), F32)
                dv = jnp.zeros((seg, width), F32)
                for head in range(heads):
                    here = head_lanes(width, head)
                    scores = dot(jnp.where(here, keys, jnp.zeros_like(keys)), queries_t)
                    probs = jnp.exp(scores - lse_t[head : head + 1])
                    probs = jnp.where(row_ok, probs, 0.0)
                    g_probs = dot(jnp.where(here, values, jnp.zeros_like(values)), upstream_t)
                    g_scores = (probs * (g_probs - delta_t[head])).astype(BF16)
                    dv = jnp.where(here, dot(probs.astype(BF16), upstream), dv)
                    dk = jnp.where(here, dot(g_scores, queries), dk)
                    part = slice(head * HD, (head + 1) * HD)
                    dq_t[part, 0:rows] += dot(keys_t[part], g_scores)
                d_all[at, :, width : 2 * width] = dk.astype(BF16)
                d_all[at, :, 2 * width :] = dv.astype(BF16)
                return carry

            lax.fori_loop(0, count, block, 0)
            for at in range(count):
                piece = dq_t[:, at * seg : (at + 1) * seg]
                d_all[at, :, 0:width] = (piece.T * HD**-0.5).astype(BF16)

    for j in range(pieces):
        at = lax.bitwise_xor(place, j)
        gin_out = (gin_send if j % 2 else gin_keep).at[j // 2]

        @pl.when(at < filled)
        def _():
            grads = d_all[at]
            gin_out[...] = dot(grads, w_all[...], NT).astype(BF16)
            out_w[...] += dot(hidden[j][0], grads, TN)
            out_b[...] += dot(grads, jnp.ones((seg, out_b.shape[-1]), BF16), TN)

        @pl.when(at >= filled)
        def _():
            gin_out[...] = jnp.zeros((seg, model), BF16)

    if earlier:
        devices, share, full = block_out.shape
        total = out_w[...]
        columns = out_b[...]
        for w_sum, b_sum in zip(before[:-1:2], before[1:-1:2]):
            total = total + w_sum[...]
            columns = columns + b_sum[...]
        block_out[:, :, : 3 * width] = total.astype(BF16).reshape(devices, share, 3 * width)
        spare = full - 3 * width
        side = before[-1][...]
        block_out[:, :, 3 * width :] = jnp.broadcast_to(
            side.astype(BF16)[None], (devices, share, spare)
        )
        lane = lax.broadcasted_iota(jnp.int32, (share, spare), 1)
        owners = width // share
        for k in range(owners):
            query = columns[k * share : (k + 1) * share, :spare]
            value = columns[2 * width + k * share : 2 * width + (k + 1) * share, :spare]
            mine = jnp.where(lane == 0, query, jnp.where(lane == 1, value, side))
            block_out[place * owners + k, :, 3 * width :] = mine.astype(BF16)


def finish_kernel(groups, block, own_ref, extra_ref):
    share, full = own_ref.shape
    devices = block.shape[0]
    part = full // (3 * groups)
    side = 0.0
    for g in range(groups):
        total = 0.0
        for r in range(devices // groups):
            total = total + block[r * groups + g].astype(F32)
        for p in range(3):
            at = p * groups * part + g * part
            own_ref[:, at : at + part] = total[:, p * part : (p + 1) * part]
        side = side + total[:, 3 * part :]
    spare = side.shape[1]
    side = jnp.concatenate([side, jnp.zeros((128 - share, spare), F32)], axis=0)
    side = jnp.concatenate([side, jnp.zeros((128, 128 - spare), F32)], axis=1)
    extra_ref[...] = side.T[: extra_ref.shape[0]]


def finish(block, share, full, groups):
    return pl.pallas_call(
        functools.partial(finish_kernel, groups),
        out_shape=[jax.ShapeDtypeStruct(s, F32) for s in ((share, full), (32, 128))],
        compiler_params=params(),
        name="finish",
    )(block)


def attend_back(seq, index, meta, hidden, qkv, grad_ctx, saved, before=(), share=1):
    pieces = len(hidden)
    _, seg, model = hidden[0].shape
    width = model // pieces
    saved_spec = at_block((1, pieces, seg, width), index, 0, 0, 0)
    gin = (pieces // 2, seg, model)
    sums = [((model, 3 * width), F32), ((3 * width, 128), F32)]
    blocks = [((model // share, share, -(-3 * width // 128) * 128), BF16)]
    outs = [(gin, BF16)] * 2 + (blocks if before else sums)
    return pl.pallas_call(
        functools.partial(attend_back_kernel, seq, pieces, len(before)),
        out_shape=[jax.ShapeDtypeStruct(*o) for o in outs],
        grid_spec=pltpu.PrefetchScalarGridSpec(
            num_scalar_prefetch=1,
            grid=(1,),
            in_specs=[at_block((1, seg, model), seq, 0, 0)] * pieces
            + [fixed(qkv.shape), at_block((pieces, width, seg), 0, 0, seq)]
            + [saved_spec] * 3
            + [
                at_block((pieces, width, seg), 0, 0, index),
                at_block((1, pieces, seg, 128), index, 0, 0, 0),
            ]
            + [fixed(a.shape) for a in before],
            out_specs=[fixed(o[0]) for o in outs],
            scratch_shapes=[
                pltpu.VMEM((model, 3 * width), BF16),
                pltpu.VMEM((width, pieces * seg), F32),
                pltpu.VMEM((pieces, seg, 3 * width), BF16),
            ]
            + [pltpu.VMEM(*o) for o in (sums if before else [])],
        ),
        compiler_params=params(),
        cost_estimate=cost(13),
        name="attend_back",
    )(meta, *hidden, qkv, grad_ctx, *saved, *before)


def normal_parts(v):
    t = 1.0 / (1.0 + (0.3275911 * 0.5**0.5) * jnp.abs(v))
    poly = t * (
        0.127414796
        + t * (-0.142248368 + t * (0.7107068705 + t * (-0.7265760135 + t * 0.5307027145)))
    )
    bell = jnp.exp2(v * v * (-0.5 / math.log(2.0)))
    upper = poly * bell
    cdf = jnp.where(v < 0, upper, 1.0 - upper)
    return cdf, bell * (0.5 / math.pi) ** 0.5


def normalise(values):
    center = values - jnp.mean(values, axis=-1, keepdims=True)
    root = lax.rsqrt(jnp.mean(center * center, axis=-1, keepdims=True) + NORM_EPS)
    return center * root, root


def normalise_back(grad, unit, root):
    mean_grad = jnp.mean(grad, axis=-1, keepdims=True)
    mean_prod = jnp.mean(grad * unit, axis=-1, keepdims=True)
    return root * (grad - mean_grad - unit * mean_prod)


ROWS = 64


def row_loop(start, stop, fn):
    def step(i, carry):
        fn(pl.ds(pl.multiple_of(start + i * ROWS, ROWS), ROWS), start + i * ROWS)
        return carry

    lax.fori_loop(0, (stop - start) // ROWS, step, 0, unroll=2)


def fold(values):
    return jnp.sum(values.reshape(-1, 8, values.shape[-1]), axis=0)


def mask_rows(meta, base, seg):
    seq = base // seg
    position = lax.broadcasted_iota(jnp.int32, (ROWS, 1), 0) + (base - seq * seg)
    return (position + meta[meta.shape[0] - 1] * seg < meta[seq]).astype(F32)


def tokens(ref, base):
    seg = ref.shape[1]
    seq = base // seg
    return ref[seq, pl.ds(pl.multiple_of(base - seq * seg, ROWS), ROWS)].astype(F32)


def over_rows(ref, k):
    return jnp.sum(ref[k], axis=0, keepdims=True)


def onward_kernel(groups, meta, *refs):
    ctxs = refs[:groups]
    (x_ref, cot_ref, wout_ref, win_ref, wdown_ref, small_a, small_b) = refs[groups : groups + 7]
    (
        out_ref,
        act_ref,
        slope_ref,
        gsecond_ref,
        low_ref,
        gres_ref,
        unit,
        root,
        vecs,
        stats_ref,
        sums_ref,
        normed,
        acc,
        inner,
        acc_sums,
    ) = refs[groups + 7 :]
    step = pl.program_id(0)
    seqs, seg, model = x_ref.shape
    rows = seqs * seg

    @pl.when(step == 0)
    def _():
        vecs[0:8] = jnp.sum(small_a[...].astype(F32), axis=0)
        vecs[8:16] = jnp.sum(small_b[...].astype(F32), axis=0)
        acc_sums[...] = jnp.zeros(acc_sums.shape, F32)
        wout = wout_ref[...].reshape(model, model)
        done = 0
        for ref in ctxs:
            parts, width, many = ref.shape
            context = ref[...].reshape(parts * width, many)
            acc[done : done + many] = dot(context, wout, TN) + vecs[0:1]
            done += many

        def first_norm(at, base):
            mask = mask_rows(meta, base, seg)
            x = tokens(x_ref, base)
            branch = acc[at]
            n1, r1 = normalise(x + branch)
            value = n1 * vecs[1:2] + vecs[2:3]
            unit[at] = n1
            root[at] = jnp.broadcast_to(r1, (ROWS, root.shape[-1]))
            normed[at] = value
            low_ref[at] = value.astype(BF16)
            acc_sums[0] += fold(x * x * mask)
            acc_sums[1] += fold(branch * branch * mask)

        row_loop(0, rows, first_norm)
        acc[...] = jnp.broadcast_to(vecs[3:4], acc.shape)

    win = win_ref[...].reshape(model, model)
    wdown = wdown_ref[...].reshape(model, model)
    bin_row = vecs[pl.ds(6 + step, 1)]
    for b in range(seqs):
        lo, hi = b * seg, (b + 1) * seg
        inner[lo:hi] = dot(low_ref[lo:hi], win)

        def activate(at, base):
            value = inner[at] + bin_row
            cdf, pdf = normal_parts(value)
            act_ref[0, at] = (value * cdf).astype(BF16)
            slope_ref[0, at] = cdf + value * pdf

        row_loop(lo, hi, activate)
        acc[lo:hi] += dot(act_ref[0, lo:hi], wdown)

    @pl.when(step == pl.num_programs(0) - 1)
    def _():
        def second_norm(at, base):
            mask = mask_rows(meta, base, seg)
            second = acc[at]
            n2, r2 = normalise(normed[at] + second)
            output = n2 * vecs[4:5] + vecs[5:6]
            out_ref[at] = (output * mask).astype(BF16)
            g_out = tokens(cot_ref, base) * mask
            g_resid = normalise_back(g_out * vecs[4:5], n2, r2)
            low = g_resid.astype(BF16)
            gsecond_ref[at] = low
            gres_ref[at] = g_resid
            acc_sums[2] += fold(second * second * mask)
            acc_sums[3] += fold(output * output * mask)
            acc_sums[4] += fold(low.astype(F32))
            acc_sums[5] += fold(g_out * n2)
            acc_sums[6] += fold(g_out)

        row_loop(0, rows, second_norm)
        for row in range(8):
            stats_ref[row : row + 1] = over_rows(acc_sums, row)
        sums_ref[...] = jnp.zeros(sums_ref.shape, F32)
        for row in range(3):
            sums_ref[row : row + 1] = over_rows(acc_sums, 4 + row)


def onward(meta, ctxs, x, cot, specs, args, ratio):
    seqs, seg, model = x.shape
    rows = seqs * seg
    flat = (rows, model)
    chunked = (ratio, rows, model)
    outs = [(flat, BF16), (chunked, BF16), (chunked, F32), (flat, BF16), (flat, BF16)]
    outs += [(flat, F32), (flat, F32), ((rows, 128), F32), ((16, model), F32)]
    outs += [((8, model), F32)] * 2
    by_chunk = pl.BlockSpec((1, rows, model), lambda i, m: (i, 0, 0))
    return pl.pallas_call(
        functools.partial(onward_kernel, len(ctxs)),
        out_shape=[jax.ShapeDtypeStruct(*o) for o in outs],
        grid_spec=pltpu.PrefetchScalarGridSpec(
            num_scalar_prefetch=1,
            grid=(ratio,),
            in_specs=[fixed(c.shape) for c in ctxs] + [fixed(x.shape), fixed(cot.shape)] + specs,
            out_specs=[by_chunk if o[0] == chunked else fixed(o[0]) for o in outs],
            scratch_shapes=[
                pltpu.VMEM(flat, F32),
                pltpu.VMEM(flat, F32),
                pltpu.VMEM(flat, F32),
                pltpu.VMEM((8, 8, model), F32),
            ],
        ),
        compiler_params=params(),
        cost_estimate=cost(28),
        name="onward",
    )(meta, *ctxs, x, cot, *args)


def back_kernel(
    slope_ref,
    gsecond_ref,
    start_ref,
    unit,
    root,
    vecs,
    wout_ref,
    win_ref,
    wdown_ref,
    gres_ref,
    gctx_ref,
    ginner_ref,
    gbranch_ref,
    sums_ref,
    acc,
    inner,
    acc_sums,
):
    step = pl.program_id(0)
    rows, model = acc.shape
    many = rows // 3 if rows % 3 == 0 else rows

    @pl.when(step == 0)
    def _():
        acc[...] = start_ref[...]
        sums_ref[...] = jnp.zeros(sums_ref.shape, F32)

    win = win_ref[...].reshape(model, model)
    wdown = wdown_ref[...].reshape(model, model)
    acc_sums[...] = jnp.zeros(acc_sums.shape, F32)
    for lo in range(0, rows, many):
        hi = lo + many
        inner[lo:hi] = dot(gsecond_ref[lo:hi], wdown, NT)

        def through(at, base):
            low = (inner[at] * slope_ref[0, at]).astype(BF16)
            ginner_ref[0, at] = low
            acc_sums[0] += fold(low.astype(F32))

        row_loop(lo, hi, through)
        acc[lo:hi] += dot(ginner_ref[0, lo:hi], win, NT)
    sums_ref[pl.ds(6 + step, 1)] = over_rows(acc_sums, 0)

    @pl.when(step == pl.num_programs(0) - 1)
    def _():
        acc_sums[0] = jnp.zeros(acc_sums.shape[1:], F32)

        def first_back(at, base):
            grad = acc[at]
            n1 = unit[at]
            g_resid = normalise_back(grad * vecs[1:2], n1, root[at][:, 0:1])
            low = g_resid.astype(BF16)
            gres_ref[at] = g_resid
            gbranch_ref[at] = low
            acc_sums[0] += fold(low.astype(F32))
            acc_sums[1] += fold(grad * n1)
            acc_sums[2] += fold(grad)

        row_loop(0, rows, first_back)
        wout = wout_ref[...].reshape(model, model)
        piece = dot(wout, gbranch_ref[...], NT).astype(BF16)
        gctx_ref[...] = piece.reshape(gctx_ref.shape)
        for row in range(3):
            sums_ref[row : row + 1] = over_rows(acc_sums, row)


def back(slopes, g_second, start, unit, root, vecs, specs, args, parts):
    ratio, rows, model = slopes.shape
    flat = (rows, model)
    chunked = (ratio, rows, model)
    outs = [(flat, F32), ((parts, model // parts, rows), BF16), (chunked, BF16)]
    outs += [(flat, BF16), ((16, model), F32)]
    by_chunk = pl.BlockSpec((1, rows, model), lambda i: (i, 0, 0))
    whole = lambda shape: pl.BlockSpec(shape, lambda i: (0,) * len(shape))
    specs = [pl.BlockSpec(x.block_shape, functools.partial(drop_last, x.index_map)) for x in specs]
    return pl.pallas_call(
        back_kernel,
        out_shape=[jax.ShapeDtypeStruct(*o) for o in outs],
        grid=(ratio,),
        in_specs=[by_chunk]
        + [whole(a.shape) for a in (g_second, start, unit, root, vecs)]
        + specs[:3],
        out_specs=[by_chunk if o[0] == chunked else whole(o[0]) for o in outs],
        scratch_shapes=[
            pltpu.VMEM(flat, F32),
            pltpu.VMEM(flat, F32),
            pltpu.VMEM((3, 8, model), F32),
        ],
        compiler_params=params(),
        cost_estimate=cost(22),
        name="back",
    )(slopes, g_second, start, unit, root, vecs, *args[:3])


def drop_last(index_map, i):
    return index_map(i, None)


def spread(grad, keep, send, me, order):
    many = keep.shape[0]
    for n in range(many):
        slot = 0
        for i, bit in enumerate(order):
            slot |= ((n >> (len(order) - 1 - i)) & 1) << bit
        keep[n] = grad[lax.bitwise_xor(me, slot)]
        send[n] = grad[lax.bitwise_xor(me, slot + 1)]


Y_BIT, X_BIT, NEAR_Z_BIT, FAR_Z_BIT = 1, 2, 3, 4


def down_kernel(act_ref, g_ref, out_ref):
    grad = dot(act_ref[0], g_ref[...], TN).astype(BF16)
    out_ref[...] = grad.reshape(out_ref.shape)


def down_grads(acts, g_second, each):
    ratio, rows, model = acts.shape
    return pl.pallas_call(
        down_kernel,
        out_shape=jax.ShapeDtypeStruct((ratio * model // each, each, model), BF16),
        grid=(ratio,),
        in_specs=[
            pl.BlockSpec((1, rows, model), lambda i: (i, 0, 0)),
            pl.BlockSpec((rows, model), lambda i: (0, 0)),
        ],
        out_specs=pl.BlockSpec((model // each, each, model), lambda i: (i, 0, 0)),
        compiler_params=params(),
        cost_estimate=cost(8),
        name="down_grads",
    )(acts, g_second)


def rest_kernel(ratio, groups, cut, meta, low_ref, ginner_ref, *refs):
    ctxs = refs[:groups]
    gbranch_ref, sums_one, sums_two = refs[groups : groups + 3]
    outs = refs[groups + 3 : groups + 7]
    grad = refs[groups + 7]
    me = meta[meta.shape[0] - 2]
    step = pl.program_id(0)
    devices, each, model = grad.shape

    @pl.when(step < ratio)
    def _():
        grad[...] = dot(low_ref[...], ginner_ref[0], TN).astype(BF16).reshape(grad.shape)

    @pl.when(step == ratio)
    def _():
        total = 0.0
        done = 0
        for ref in ctxs:
            parts, width, many = ref.shape
            context = ref[...].reshape(parts * width, many)
            total = total + dot(context, gbranch_ref[done : done + many])
            done += many
        grad[...] = total.astype(BF16).reshape(grad.shape)

    @pl.when(step == ratio + 1)
    def _():
        block = jnp.concatenate(
            [sums_one[...], sums_two[...], jnp.zeros((each - 24, model), F32)]
            if each > 24
            else [sums_one[...], sums_two[...]],
            axis=0,
        )
        grad[...] = jnp.broadcast_to(block.astype(BF16)[None], grad.shape)

    x_first = (X_BIT, Y_BIT, NEAR_Z_BIT, FAR_Z_BIT)
    y_first = (Y_BIT, X_BIT, NEAR_Z_BIT, FAR_Z_BIT)

    @pl.when(step < cut)
    def _():
        spread(grad, outs[0], outs[1], me, x_first)

    @pl.when(step >= cut)
    def _():
        spread(grad, outs[2], outs[3], me, y_first)


def rest_grads(meta, low, g_inner, ctxs, g_branch, sums_one, sums_two, devices, each):
    ratio, rows, model = g_inner.shape
    cut = (ratio + 2) // 2
    half = devices // 2
    shapes = [jax.ShapeDtypeStruct((half, n * each, model), BF16) for n in (cut, ratio + 2 - cut)]
    specs = [
        pl.BlockSpec((half, each, model), lambda i, m: (0, jnp.minimum(i, cut - 1), 0)),
        pl.BlockSpec((half, each, model), lambda i, m: (0, jnp.maximum(i - cut, 0), 0)),
    ]
    return pl.pallas_call(
        functools.partial(rest_kernel, ratio, len(ctxs), cut),
        out_shape=(shapes[0], shapes[0], shapes[1], shapes[1]),
        grid_spec=pltpu.PrefetchScalarGridSpec(
            num_scalar_prefetch=1,
            grid=(ratio + 2,),
            in_specs=[
                fixed(low.shape),
                pl.BlockSpec((1, rows, model), lambda i, m: (jnp.minimum(i, ratio - 1), 0, 0)),
            ]
            + [fixed(c.shape) for c in ctxs]
            + [fixed(g_branch.shape), fixed(sums_one.shape), fixed(sums_two.shape)],
            out_specs=[specs[0], specs[0], specs[1], specs[1]],
            scratch_shapes=[pltpu.VMEM((devices, each, model), BF16)],
        ),
        compiler_params=params(),
        cost_estimate=cost(10),
        name="rest_grads",
    )(meta, low, g_inner, *ctxs, g_branch, sums_one, sums_two)


def natural_grads(acts, g_second, low, g_inner, ctxs, g_branch, sums, devices, share):
    ratio, rows, model = acts.shape
    down = jnp.concatenate([dot(a, g_second, TN) for a in acts]).reshape(devices, -1, model)
    context = jnp.concatenate(ctxs, axis=2).reshape(model, rows)
    rest = [dot(low, g, TN) for g in g_inner] + [dot(context, g_branch)]
    rest = [r.reshape(devices, share, model) for r in rest]
    rest.append(jnp.broadcast_to(sums[None], (devices,) + sums.shape))
    return down.astype(BF16), jnp.concatenate(rest, axis=1).astype(BF16)


def pair(kept, sent):
    return (kept.astype(F32) + sent.astype(F32)).astype(BF16)


def halves(kept, got):
    half = kept.shape[0] // 2
    return pair(kept[half:], got[half:]), pair(kept[:half], got[:half])


def body(
    hidden_in,
    lengths,
    w_qkv,
    b_query,
    b_value,
    w_out,
    b_out,
    gain_one,
    bias_one,
    w_in,
    b_in,
    w_down,
    b_down,
    gain_two,
    bias_two,
    cotangent,
):
    seqs, seg, model = hidden_in.shape
    sizes = tuple(lax.axis_size(a) for a in ALL_AXES)
    far, wide, near_y, cores = sizes
    groups = near_y * cores
    devices = far * wide * groups
    place = lax.axis_index(ROW_AXES)
    me = lax.axis_index(ALL_AXES)
    share = model // devices
    ff = w_in.shape[1]
    ff_share = ff // devices
    ratio = ff // model
    width = model // groups
    aligned = share % 8 == 0 and devices == 8 * ratio and far == ratio
    meta = jnp.concatenate([lengths, me[None], place[None]]).astype(jnp.int32)

    first = me * share
    cut = w_qkv.reshape(share, 3, groups, width).transpose(2, 0, 1, 3)
    cut = cut.reshape(groups, share, 3 * width)
    spare = -3 * width % 128
    side = jnp.pad(jnp.stack([b_query, b_value], axis=1), ((0, 0), (0, spare - 2)))
    side = jnp.broadcast_to(side[None], (groups,) + side.shape)
    packed = jnp.concatenate([cut, side], axis=2)
    packed = jnp.broadcast_to(packed[None], (far * wide,) + packed.shape)
    qkv = exchange(packed.reshape(devices, share, -1), ALL_AXES)
    if not aligned:
        qkv = qkv.reshape(1, model, -1)

    hidden = gather_rows(hidden_in)

    small = jnp.zeros((16, model), BF16)
    vectors = jnp.stack([b_out, gain_one, bias_one, b_down, gain_two, bias_two])
    small = lax.dynamic_update_slice(small, vectors, (0, first))
    ff_first = me * ff_share
    ff_row = ff_first // model
    small = lax.dynamic_update_slice(small, b_in[None], (6 + ff_row, ff_first - ff_row * model))
    bundle = jnp.concatenate(
        [
            w_in.reshape(share, ratio, model).transpose(1, 0, 2).reshape(-1, model),
            w_down,
            w_out,
            small,
        ]
    )
    bundle = lax.all_gather(bundle, ALL_AXES, axis=0, tiled=False)
    at = ratio * share
    if aligned:
        weight_specs = [
            at_block((devices, share, model), 0, (at + ff_share) // share, 0),
            pl.BlockSpec((devices, share, model), lambda i, m: (0, i, 0)),
            pl.BlockSpec((devices // ratio, ff_share, model), lambda i, m: (i, 1, 0)),
            at_block((devices, 8, model), 0, (at + ff_share + share) // 8, 0),
            at_block((devices, 8, model), 0, (at + ff_share + share) // 8 + 1, 0),
        ]
        weight_args = [bundle] * 5
    else:
        win = bundle[:, :at].reshape(devices, ratio, share, model).transpose(1, 0, 2, 3)
        small = bundle[:, at + ff_share + share :]
        weight_args = [
            bundle[:, at + ff_share : at + ff_share + share].reshape(model, model),
            win.reshape(ratio, model, model),
            bundle[:, at : at + ff_share].reshape(ratio, model, model),
            small[:, :8],
            small[:, 8:],
        ]
        by_chunk = pl.BlockSpec((1, model, model), lambda i, m: (i, 0, 0))
        weight_specs = [fixed(a.shape) for a in weight_args]
        weight_specs[1] = weight_specs[2] = by_chunk

    spans = [(0, seqs - 1), (seqs - 1, 1)]
    saved = []
    ctxs = []
    for start, count in spans:
        q, k, v, ctx, lse = attend(start, count, meta, hidden, qkv)
        saved.append((q, k, v, ctx, lse))
        ctxs.append(exchange(ctx, ROW_AXES))

    (out, acts, slopes, g_second, low, start, unit, root, vecs, stats, sums_two) = onward(
        meta, ctxs, hidden_in, cotangent, weight_specs, weight_args, ratio
    )
    layer_out = out.reshape(seqs, seg, model)
    if aligned:
        down = down_grads(acts, g_second, ff_share)
        start = after(start, down)
        down = lax.psum_scatter(down, ALL_AXES, scatter_dimension=0, tiled=False)
    g_resid, g_ctx, g_inner, g_branch, sums_one = back(
        slopes, g_second, start, unit, root, vecs, weight_specs, weight_args, groups
    )
    g_ctx = exchange(g_ctx, ROW_AXES)
    if aligned:
        keep_a, send_a, keep_b, send_b = rest_grads(
            meta, low, g_inner, ctxs, g_branch, sums_one, sums_two, devices, share
        )
        got_a, got_b = swap(send_a, "c"), swap(send_b, "c")
    else:
        sums = jnp.concatenate([sums_one, sums_two])
        down, rest = natural_grads(
            acts, g_second, low, g_inner, ctxs, g_branch, sums, devices, share
        )
        down = lax.psum_scatter(down, ALL_AXES, scatter_dimension=0, tiled=False)
        rest = lax.psum_scatter(rest, ALL_AXES, scatter_dimension=0, tiled=False)

    squares = jnp.sum(stats[:4], axis=1)
    valid = jnp.sum(jnp.clip(lengths - place * seg, 0, seg)).astype(F32)
    exact = jnp.concatenate([squares, valid[None]])
    terms = []
    for _ in range(3):
        terms.append(lax.reduce_precision(exact, 8, 7))
        exact = exact - terms[-1]
    stat_rows = jnp.pad(jnp.concatenate(terms)[None], ((0, share - 1), (2, spare - 17)))

    homes = [(span, i) for span, (_, count) in enumerate(spans) for i in range(count)]
    w_sums = []
    partials = []
    inputs = [None] * seqs
    over = [None] * seqs

    def settle(b):
        kept, near = partials[b]
        here = kept[0].astype(F32) + near[0].astype(F32)
        inputs[b] = g_resid[b * seg : (b + 1) * seg] + here
        over[b] = pair(kept[1], near[1])

    for b, (span, index) in enumerate(homes):
        if b == 1 and aligned:
            go_a, keep_a = halves(keep_a, after(got_a, gin_send))
            go_b, keep_b = halves(keep_b, after(got_b, gin_send))
            g_ctx = after(g_ctx, go_a, go_b)
            got_a, got_b = swap(go_a, "x"), swap(go_b, "y")
        if b == seqs - 1 and aligned:
            go_a, keep_a = halves(keep_a, after(got_a, gin_send))
            go_b, keep_b = halves(keep_b, after(got_b, gin_send))
            g_ctx = after(g_ctx, go_a, go_b)
            got_a, got_b = swap(go_a, "y"), swap(go_b, "x")
        before = ()
        if b == seqs - 1 and aligned:
            before = [w for w_sum in w_sums for w in w_sum] + [stat_rows]
        gin_keep, gin_send, *w_sum = attend_back(
            b, index, meta, hidden, qkv, g_ctx, saved[span], before, share
        )
        block = w_sum[0]
        w_sums.append(w_sum)
        partials.append((gin_keep, swap(gin_send, "c")))
        if b:
            partials[b - 1] = after(partials[b - 1], gin_send)
            settle(b - 1)
    settle(seqs - 1)
    inputs = [mine + swap(far_part, "y").astype(F32) for mine, far_part in zip(inputs, over)]
    grad_input = jnp.stack(inputs)
    if aligned:
        rest = jnp.concatenate([keep_a, keep_b], axis=1)
        got_a, got_b, block = lax.optimization_barrier((got_a, got_b, block))
        got = jnp.concatenate([got_a, got_b], axis=1)
        go, rest = halves(rest, got)
        got = swap(after(go, over[-1]), "z", 1)
        go, rest = halves(rest, got)
        rest = pair(rest, after(swap(after(go, over[-1], down), "z", 2), grad_input))
    rest = rest.astype(F32)
    down = down.astype(F32)

    if aligned:
        own_wqkv, extra = finish(exchange(block, ALL_AXES), share, 3 * model, groups)
        own_bq, own_bv, stats = extra[0, :share], extra[1, :share], extra[2:17, 0]
    else:
        w_sum = sum(w for w, _ in w_sums).astype(BF16).reshape(devices, share, 3 * width)
        b_sum = jnp.pad(sum(w for _, w in w_sums)[None, :, 0], ((0, 7), (0, 0)))
        b_sum = b_sum + jnp.pad(stat_rows[:1], ((1, 6), (0, 3 * width - spare)))
        b_sum = jnp.broadcast_to(b_sum.astype(BF16)[None], (devices, 8, 3 * width))
        block = exchange(jnp.concatenate([w_sum, b_sum], axis=1), ALL_AXES).astype(F32)
        totals = jnp.sum(block.reshape(far * wide, groups, share + 8, 3, width), axis=0)
        totals = totals.transpose(1, 2, 0, 3).reshape(share + 8, 3 * model)
        own_wqkv, extra = totals[:share], totals[share:]
        own_bq = lax.dynamic_slice(extra, (0, first), (1, share))[0]
        own_bv = lax.dynamic_slice(extra, (0, 2 * model + first), (1, share))[0]
        stats = jnp.sum(block[:, share + 1, 2:17], axis=0)
    stats = stats[:5] + stats[5:10] + stats[10:15]
    stat_rms = jnp.sqrt(stats[:4] / (stats[4] * model))

    rest = rest.reshape(-1, model)
    own_win = rest[: ratio * share].reshape(ratio, share, model).transpose(1, 0, 2)
    own_win = own_win.reshape(share, ff)
    at = ratio * share
    own_wout = rest[at : at + share]
    at += share
    vectors = lax.dynamic_slice(rest, (at, first), (3, share))
    vectors_two = lax.dynamic_slice(rest, (at + 16, first), (3, share))
    own_bin = lax.dynamic_slice(rest, (at + 6 + ff_row, ff_first - ff_row * model), (1, ff_share))
    return (
        layer_out,
        grad_input,
        own_wqkv,
        own_bq,
        own_bv,
        own_wout,
        vectors[0],
        vectors[1],
        vectors[2],
        own_win,
        own_bin[0],
        down.reshape(ff_share, model),
        vectors_two[0],
        vectors_two[1],
        vectors_two[2],
        stat_rms,
    )


def solution(mesh):
    dp, seq = mesh.shape["dp"], mesh.shape["seq"]
    finer = Mesh(mesh.devices.reshape(dp // 2, 2, seq // 2, 2), ALL_AXES)
    token = P(BATCH_AXES, ROW_AXES, None)
    matrix = P(ALL_AXES, None)
    vector = P(ALL_AXES)
    placed = (
        (token, P(BATCH_AXES), matrix, vector, vector, matrix, vector, vector, vector)
        + (matrix, vector, matrix, vector, vector, vector, token)
    )
    results = (
        (token, token, matrix, vector, vector, matrix, vector, vector, vector)
        + (matrix, vector, matrix, vector, vector, vector, P())
    )
    return jax.shard_map(
        body, mesh=finer, in_specs=placed, out_specs=results, check_vma=False
    )
```
